32 devices in a mesh: gx: 4 (over y, x), gy: 4 (over z), gz: 2 (over core).
Axes of the slice: x: 2, y: 2, z: 4, core: 2. Of those that a mesh axis runs over, the one named last changes fastest.
Arguments:
- coarse: bfloat16 [2, 5, 8, 32, 128], P(None, None, 'gz', 'gx', 'gy'), may hold values from -1.5 to 1.5
- detail_x1: bfloat16 [2, 5, 8, 32, 128], P(None, None, 'gz', 'gx', 'gy'), may hold values from -1 to 1
- detail_y1: bfloat16 [2, 5, 8, 64, 128], P(None, None, 'gz', 'gx', 'gy'), may hold values from -1 to 1
- detail_x2: bfloat16 [2, 5, 8, 64, 256], P(None, None, 'gz', 'gx', 'gy'), may hold values from -1 to 1
- detail_y2: bfloat16 [2, 5, 8, 128, 256], P(None, None, 'gz', 'gx', 'gy'), may hold values from -1 to 1
- significance: int32 [2, 8, 16, 16], P(None, 'gz', 'gx', 'gy'), may hold values 0 or 1
- adjoint: float32 [5, 8, 128, 512], P(None, 'gz', 'gx', 'gy'), may hold values from -6 to 6
Outputs:
- adjoint_next: float32 [5, 8, 128, 512], P(None, 'gz', 'gx', 'gy')
The draws below stay inside these ranges and needn't reach their ends.
Inputs may be any that keep to these rules, and one draw needn't show every extreme that they name: `significance`: each entry flags one tile.
All inputs are finite; a program needn't handle non-finite values. No bound on the sum of `significance` on one device may be relied on, other than what follows from the above.
Results may differ from the reference program's by a relative error of at most 0.0012.
Values may be sent and summed in bfloat16 or wider, within the bound.
A program may use at most 64 MiB of HBM per device.

```python
import jax
import jax.numpy as jnp
from jax import lax

NX = 128
NY = 512
NZ = 8


def plant(values, key, low, high):
    extent = values.shape
    place = [jax.random.randint(jax.random.fold_in(key, axis), (), 0, extent[axis]) for axis in range(len(extent))]
    values = values.at[tuple(place)].set(low)
    longest = extent.index(max(extent))
    place[longest] = (place[longest] + 1) % extent[longest]
    return values.at[tuple(place)].set(high)


def shard_levels(own_key, dims, shards, smallest, largest):
    gain, own = 1.0, jax.random.fold_in(own_key, 6)
    for position, shards_of in shards:
        heights = jnp.exp(jax.random.uniform(jax.random.fold_in(own, position), (shards_of,), jnp.float32, smallest / len(shards), largest / len(shards)))
        gain = gain * jnp.repeat(heights, dims[position] // shards_of).reshape([-1 if axis == position else 1 for axis in range(len(dims))])
    return gain


def scatter_about(stream_key, dims, deviation, reach, pieces=(), kind=jnp.bfloat16):
    values = jax.random.normal(stream_key, dims, jnp.float32) * deviation
    if len(pieces) > 0:
        values = shard_levels(stream_key, dims, pieces, -0.22, 0.18) * values
    return jnp.clip(values, min=-reach, max=reach).astype(kind)


def setup_inputs(seed: int = 0) -> dict:
    streams_of = jax.random.split(jax.random.key(seed), 8)
    return {
        "coarse": scatter_about(streams_of[0], (2, 5, NZ, NX // 4, NY // 4), 0.5, 1.5, ((2, 2), (3, 4), (4, 4))),
        "detail_x1": scatter_about(streams_of[1], (2, 5, NZ, NX // 4, NY // 4), 0.3, 1.0, ((2, 2), (3, 4), (4, 4))),
        "detail_y1": scatter_about(streams_of[2], (2, 5, NZ, NX // 2, NY // 4), 0.3, 1.0, ((2, 2), (3, 4), (4, 4))),
        "detail_x2": scatter_about(streams_of[3], (2, 5, NZ, NX // 2, NY // 2), 0.3, 1.0, ((2, 2), (3, 4), (4, 4))),
        "detail_y2": scatter_about(streams_of[4], (2, 5, NZ, NX, NY // 2), 0.3, 1.0, ((2, 2), (3, 4), (4, 4))),
        "significance": plant((jax.random.randint(streams_of[5], (2, NZ, NX // 8, NY // 32), 0, 4) < 3).astype(jnp.int32), jax.random.fold_in(streams_of[5], 1), 0, 1),
        "adjoint": scatter_about(streams_of[6], (5, NZ, NX, NY), 1.0, 6.0, ((1, 2), (2, 4), (3, 4)), jnp.float32),
    }


time_step = 0.1
viscosity = 0.2
heat_ratio_less_one = 0.4

def displace(values, axis_dim, offset, wrap):
    if wrap:
        return jnp.roll(values, offset, axis=axis_dim)
    length = values.shape[axis_dim]
    zeros_part = jnp.zeros_like(lax.slice_in_dim(values, 0, abs(offset), axis=axis_dim))
    if offset > 0:
        return jnp.concatenate([zeros_part, lax.slice_in_dim(values, 0, length - offset, axis=axis_dim)], axis=axis_dim)
    return jnp.concatenate([lax.slice_in_dim(values, -offset, length, axis=axis_dim), zeros_part], axis=axis_dim)

def refine(coarse_part, detail, axis_dim):
    centre = coarse_part
    behind = displace(coarse_part, axis_dim, 1, True)
    ahead_one = displace(coarse_part, axis_dim, -1, True)
    ahead_two = displace(coarse_part, axis_dim, -2, True)
    odd_values = detail + (9.0 * (centre + ahead_one) - (behind + ahead_two)) / 16.0
    stacked = jnp.stack([centre, odd_values], axis=axis_dim + 1)
    target = list(coarse_part.shape)
    target[axis_dim] = 2 * coarse_part.shape[axis_dim]
    return stacked.reshape(target)

def spread_mask(tile_flags, rows_tile, cols_tile):
    ones_block = jnp.ones((1, 1, 1, rows_tile, 1, cols_tile), jnp.float32)
    widened = tile_flags.astype(jnp.float32)[:, :, :, None, :, None] * ones_block
    return widened.reshape(tile_flags.shape[0], tile_flags.shape[1], tile_flags.shape[2] * rows_tile, tile_flags.shape[3] * cols_tile)[:, None]

def face_flux(physical_variable_set, component):
    volumetric_matter = jnp.exp(0.5 * physical_variable_set[0])
    velocity = physical_variable_set[1:4]
    thermal_state_value = physical_variable_set[4]
    thermo_normal_stress = volumetric_matter * thermal_state_value
    normal_speed = velocity[component]
    velocity_norm_square = velocity[0] * velocity[0] + velocity[1] * velocity[1] + velocity[2] * velocity[2]
    whole_conserved_work = volumetric_matter * (thermal_state_value / heat_ratio_less_one + 0.5 * velocity_norm_square)
    mass_flux = volumetric_matter * normal_speed
    momenta = [mass_flux * velocity[which] for which in range(3)]
    momenta[component] = momenta[component] + thermo_normal_stress
    return jnp.stack([mass_flux] + momenta + [normal_speed * (whole_conserved_work + thermo_normal_stress)])

def face_term(upper_state, lower_state, upper_adjoint, lower_adjoint, component):
    middle_state = 0.5 * (upper_state + lower_state)
    jump = upper_adjoint - lower_adjoint
    unused, pullback = jax.vjp(lambda values: face_flux(values, component), middle_state)
    return pullback(jump)[0]

def synthesize(coarse, detail_x1, detail_y1, detail_x2, detail_y2, significance):
    refined = refine(coarse.astype(jnp.float32), detail_x1.astype(jnp.float32), 3)
    refined = refine(refined, detail_y1.astype(jnp.float32), 4)
    refined = refine(refined, detail_x2.astype(jnp.float32) * spread_mask(significance, 4, 16), 3)
    return refine(refined, detail_y2.astype(jnp.float32) * spread_mask(significance, 8, 16), 4)

def adjoint_rate(physical_variable_set, adjoint_now):
    totals = jnp.zeros_like(adjoint_now)
    for component, axis_dim, wrap in ((0, 2, True), (1, 3, True), (2, 1, False)):
        upper_adjoint = displace(adjoint_now, axis_dim, -1, wrap)
        lower_adjoint = displace(adjoint_now, axis_dim, 1, wrap)
        face_terms = face_term(displace(physical_variable_set, axis_dim, -1, wrap), physical_variable_set, upper_adjoint, adjoint_now, component)
        totals = totals + 0.5 * face_terms + 0.5 * displace(face_terms, axis_dim, 1, wrap)
        totals = totals + viscosity * (upper_adjoint + lower_adjoint - 2.0 * adjoint_now)
    return totals

def reference(coarse, detail_x1, detail_y1, detail_x2, detail_y2, significance, adjoint):
    primitives = synthesize(coarse, detail_x1, detail_y1, detail_x2, detail_y2, significance)
    first_rate = adjoint_rate(primitives[0], adjoint)
    middle = adjoint + time_step * first_rate
    second_rate = adjoint_rate(primitives[1], middle)
    return adjoint + 0.5 * time_step * (first_rate + second_rate)
```

```python
import functools

import jax
import jax.numpy as jnp
import ml_dtypes
import numpy as np
from jax import lax
from jax.experimental import pallas as pl
from jax.experimental.pallas import tpu as pltpu
from jax.sharding import PartitionSpec as P

time_step = 0.1
viscosity = 0.2
heat_ratio_less_one = 0.4
f32 = jnp.float32
bf16 = jnp.bfloat16
MESH = pl.DeviceIdType.MESH


def predict(index):
    k = index // 2
    if index % 2 == 0:
        return {("c", k): 1.0}
    return {
        ("d", k): 1.0,
        ("c", k): 9 / 16,
        ("c", k + 1): 9 / 16,
        ("c", k - 1): -1 / 16,
        ("c", k + 2): -1 / 16,
    }


def predict_twice(index):
    whole = {}
    for (kind, k), weight in predict(index).items():
        if kind == "d":
            whole[("e", k)] = weight
            continue
        whole[("m", k)] = weight
        for key, inner in predict(k).items():
            whole[key] = whole.get(key, 0.0) + weight * inner
    return whole


def halo_row(kind, k):
    if kind == "c":
        return k - 32 if k >= 32 else 11 + k
    if kind == "d":
        return 3 if k >= 32 else 11
    if kind == "m":
        return 4 + k - 64 if k >= 64 else 14 + k
    return 7 if k >= 64 else 14


def y_matrices():
    own = np.zeros((4, 64, 256), np.float32)
    halo = np.zeros((5, 16, 256), np.float32)
    corner = np.zeros((4, 8, 256), np.float32)
    columns = [(y, y) for y in range(128)] + [(128, 128), (129, 129), (-1, 255), (-2, 254)]
    for y, column in columns:
        for (kind, k), weight in predict_twice(y).items():
            role = "cdme".index(kind)
            length = 32 if role < 2 else 64
            if 0 <= k < length:
                own[role, k, column] += weight
                continue
            row = halo_row(kind, k)
            halo[role, row, column] += weight
            if kind == "e":
                halo[4, row + 1, column] += weight
            if k >= length:
                corner[role, k - length, column] += weight
            else:
                corner[role, (5 if length == 32 else 7) + k, column] += weight
    parts = [own.reshape(256, 256), halo.reshape(80, 256), corner.reshape(32, 256)]
    return np.concatenate(parts).astype(ml_dtypes.bfloat16)


def small_matrices():
    mats = np.zeros((144, 128), np.float32)
    for x in range(-2, 34):
        row = x + 8
        for (kind, k), weight in predict_twice(x).items():
            if kind == "c":
                at = 50 + k if k < 0 else (k if k < 8 else 56 + k - 8)
            elif kind == "d":
                at = 50 if k < 0 else (8 + k if k < 8 else 59)
            elif kind == "m":
                at = 53 + k if k < 0 else (16 + k if k < 16 else 60 + k - 16)
            else:
                at = 53 if k < 0 else (32 + k if k < 16 else 63)
            mats[row, at] += weight
    mats[6, 54] = 1.0
    mats[7, 55] = 1.0
    mats[0:48, 64:128] = mats[0:48, 0:64]
    picks = mats[48:128].reshape(5, 16, 128)
    for row, column in ((0, 0), (1, 1), (2, 2), (9, 30), (10, 31)):
        picks[0, row, column] = 1.0
    for row, column in ((3, 0), (11, 31)):
        picks[1, row, column] = 1.0
    for row, column in ((4, 0), (5, 1), (6, 2), (12, 62), (13, 63)):
        picks[2, row, column] = 1.0
    for row, column in ((7, 0), (14, 63)):
        picks[3, row, column] = 1.0
        picks[4, row + 1, column] = 1.0
    for row, column in ((0, 0), (1, 1), (2, 2), (3, 30), (4, 31), (5, 62), (6, 63)):
        mats[128 + row, column] = 1.0
    return mats.astype(ml_dtypes.bfloat16)


def face(mean, jump, k):
    q, u, t = mean[0], mean[1:4], mean[4]
    rho = jnp.exp(0.5 * q)
    speed = u[k]
    half_square = 0.5 * (u[0] * u[0] + u[1] * u[1] + u[2] * u[2])
    enthalpy = (1.0 / heat_ratio_less_one + 1.0) * t + half_square
    inner = jump[0] + jump[1] * u[0] + jump[2] * u[1] + jump[3] * u[2] + jump[4] * enthalpy
    flow = rho * speed
    grads = [flow * (jump[1 + j] + jump[4] * u[j]) for j in range(3)]
    grads[k] = grads[k] + rho * inner
    dq = 0.5 * (flow * inner + rho * t * jump[1 + k])
    dt = rho * jump[1 + k] + (1.0 / heat_ratio_less_one + 1.0) * flow * jump[4]
    return [dq] + grads + [dt]


def kernel(
    c_in, x1_in, y1_in, x2_in, y2_in, sig_in, adj_in, ay_in, small_in,
    out_any,
    cx_ref, y1_ref, x2_ref, y2_ref, sig_ref, adj_ref, ay_ref, small_ref,
    out_ref, load_sem,
    tiles, mask_x, mask_y, ext, hy2,
    cols_send, cols_recv, low_send, low_recv, high_send, high_recv, corner_send, corner_recv,
    ax_send, ax_recv, ay_send, ay_recv, ad_recv, rim,
    mapped, mapped_y2, state, adj, mid, gx_terms, gz_terms,
    send_sem, recv_sem,
):
    gx, gy, gz = lax.axis_index("gx"), lax.axis_index("gy"), lax.axis_index("gz")
    nx, ny = lax.axis_size("gx"), lax.axis_size("gy")
    up_x, down_x = lax.rem(gx + 1, nx), lax.rem(gx + nx - 1, nx)
    up_y, down_y = lax.rem(gy + 1, ny), lax.rem(gy + ny - 1, ny)
    x_up, x_down = {"gx": up_x}, {"gx": down_x}
    y_up, y_down = {"gy": up_y}, {"gy": down_y}
    diagonal = (
        {"gx": up_x, "gy": down_y},
        {"gx": up_x, "gy": up_y},
        {"gx": down_x, "gy": down_y},
        {"gx": down_x, "gy": up_y},
    )
    z_other = {"gz": 1 - gz}
    barrier = pltpu.get_barrier_semaphore()
    for peer in (x_up, x_down, y_up, y_down, z_other) + diagonal:
        pl.semaphore_signal(barrier, inc=1, device_id=peer, device_id_type=MESH)

    pairs = (
        (sig_in, sig_ref), (x2_in, x2_ref), (y2_in, y2_ref), (c_in, cx_ref.at[0:320]),
        (x1_in, cx_ref.at[320:640]), (y1_in, y1_ref), (small_in, small_ref), (adj_in, adj_ref),
        (ay_in, ay_ref),
    )
    loads = [
        pltpu.make_async_copy(source, target, load_sem.at[i])
        for i, (source, target) in enumerate(pairs)
    ]
    for load in loads:
        load.start()

    def remote(index, source, target, peer):
        return pltpu.make_async_remote_copy(
            src_ref=source,
            dst_ref=target,
            send_sem=send_sem.at[index],
            recv_sem=recv_sem.at[index],
            device_id=peer,
            device_id_type=MESH,
        )

    def transposed(left, right):
        return lax.dot_general(left, right, (((1,), (1,)), ((), ())), preferred_element_type=f32)

    lane = lax.broadcasted_iota(jnp.int32, (8, 128), 1)
    lane_wide = lax.broadcasted_iota(jnp.int32, (32, 128), 1)
    lane_full = lax.broadcasted_iota(jnp.int32, (48, 128), 1)

    for load in loads[:8]:
        load.wait()
    lane_tile = lax.broadcasted_iota(jnp.int32, (4, 64), 1) // 16
    row_half = lax.broadcasted_iota(jnp.int32, (8, 64), 0) < 4
    for c in range(2):
        for z in range(4):
            flags = sig_ref[c, z].astype(f32)
            wide = jnp.zeros((4, 64), f32)
            for t in range(4):
                wide = jnp.where(lane_tile == t, flags[:, t : t + 1], wide)
            tiles[c, z, 0:4] = wide
            each = [jnp.broadcast_to(tiles[c, z, t : t + 1], (8, 64)) for t in range(4)]
            for t in range(4):
                mask_y[c, z, 8 * t : 8 * t + 8] = each[t]
            for t in range(2):
                mask_x[c, z, 8 * t : 8 * t + 8] = jnp.where(row_half, each[2 * t], each[2 * t + 1])

    kept_x2 = x2_ref[...].astype(f32).reshape(2, 5, 4, 16, 64) * mask_x[...][:, None]
    kept_y2 = y2_ref[...].astype(f32).reshape(2, 5, 4, 32, 64) * mask_y[...][:, None]
    ext[...] = jnp.zeros_like(ext)
    ext[0:640, 0:32] = cx_ref[...].astype(f32)
    ext[640:1280, 0:32] = y1_ref[...].astype(f32)
    ext[1280:1920, 0:64] = kept_x2.reshape(640, 64)
    ext[1920:3200, 0:64] = kept_y2.reshape(1280, 64)

    def own(begin, end):
        return ext[begin:end, 0:64].astype(bf16)

    starts = (0, 640, 1280, 1920, 2560)
    cols = jnp.zeros((16, 640), f32)
    for which, begin in enumerate(starts):
        pick = small_ref[48 + 16 * which : 64 + 16 * which, 0:64]
        cols = cols + transposed(pick, own(begin, begin + 640))
    cols_send[...] = cols.astype(bf16)

    coarse_e = ext[0:320].reshape(40, 8, 128)
    x1_e = ext[320:640].reshape(40, 8, 128)
    y1_e = ext[640:1280].reshape(40, 16, 128)
    x2_e = ext[1280:1920].reshape(40, 16, 128)
    y2_e = ext[1920:3200].reshape(40, 32, 128)
    low = jnp.concatenate(
        [coarse_e[:, 6:8], x1_e[:, 7:8], y1_e[:, 14:16], x2_e[:, 15:16], y2_e[:, 30:32]], 1
    ).reshape(320, 128)
    high = jnp.concatenate(
        [coarse_e[:, 0:3], x1_e[:, 0:1], y1_e[:, 0:3], x2_e[:, 0:1]], 1
    ).reshape(320, 128)
    hy2[80:96] = jnp.zeros((16, 128), f32)
    for p in range(40):
        hy2[2 * p : 2 * p + 2] = ext[1920 + 32 * p : 1922 + 32 * p]
    more = hy2[0:48] + pltpu.roll(hy2[48:96], 64, 1)
    low_send[...] = (low[0:160] + pltpu.roll(low[160:320], 64, 1)).astype(bf16)
    high_send[0:160] = (high[0:160] + pltpu.roll(high[160:320], 64, 1)).astype(bf16)
    high_send[160:208] = more.astype(bf16)
    rows = jnp.concatenate([low, high, hy2[0:80]], 0)[:, 0:64].astype(bf16)
    corner_send[:, 0:720] = transposed(small_ref[128:144, 0:64], rows)[0:8].astype(bf16)
    corner_send[:, 720:768] = jnp.zeros((8, 48), bf16)

    columns = jnp.zeros((32, 128), f32)
    for i in range(20):
        plane = adj_ref[i // 4, i % 4]
        columns = jnp.where(lane_wide // 4 == i, pltpu.roll(plane, 4 * i + 2, 1), columns)
        ax_send[0, 2 * i : 2 * i + 2] = plane[0:2]
        ax_send[1, 2 * i : 2 * i + 2] = plane[30:32]
    ay_send[...] = columns

    pl.semaphore_wait(barrier, 9)
    adj_copies = [
        remote(8, ay_send, ay_recv.at[0], y_down),
        remote(9, ay_send, ay_recv.at[1], y_up),
        remote(10, ax_send.at[0], ax_recv.at[1], x_down),
        remote(11, ax_send.at[1], ax_recv.at[0], x_up),
    ] + [
        remote(12 + i, ay_send.at[24 - 24 * (i // 2) : 32 - 24 * (i // 2)], ad_recv.at[i], diagonal[i])
        for i in range(4)
    ]
    raw_copies = [
        remote(0, cols_send, cols_recv.at[0], y_down),
        remote(1, cols_send, cols_recv.at[1], y_up),
        remote(2, low_send, low_recv, x_up),
        remote(3, high_send, high_recv, x_down),
    ] + [remote(4 + i, corner_send, corner_recv.at[i], diagonal[i]) for i in range(4)]
    for copy in adj_copies + raw_copies:
        copy.start()

    loads[8].wait()
    for begin, count, role, target, at in (
        (0, 8, 0, mapped, 0),
        (320, 8, 0, mapped, 8),
        (640, 16, 1, mapped, 16),
        (1280, 16, 2, mapped, 32),
        (1920, 32, 3, mapped_y2, 0),
    ):
        product = jnp.dot(
            own(begin, begin + 40 * count),
            ay_ref[64 * role : 64 * role + 64],
            preferred_element_type=f32,
        )
        target[:, at : at + count] = product.reshape(40, count, 256)
    mapped_y2[:, 32:40] = jnp.zeros((40, 8, 256), f32)

    outer = 5 * gz
    z_side = 3 - 3 * gz
    blank = jnp.zeros((48, 128), f32)
    for t in range(2):
        for v in range(5):
            adj[t, v, outer] = blank
            mid[t, v, outer] = blank
        for cv in range(10):
            state[t, cv, outer] = blank
    for i in range(20):
        v, z = i // 4, i % 4
        adj[0, v, z + 1, 0:8] = blank[0:8]
        adj[0, v, z + 1, 40:48] = blank[0:8]
        adj[0, v, z + 1, 8:40] = adj_ref[v, z]
    rim[...] = blank

    for copy in adj_copies:
        copy.wait()
    for i in range(20):
        v, z = i // 4, i % 4
        adj[0, v, z + 1, 6:8] = ax_recv[0, 2 * i : 2 * i + 2]
        adj[0, v, z + 1, 40:42] = ax_recv[1, 2 * i : 2 * i + 2]
    first = lane_wide % 4 >= 2
    first_row = first[0:1]
    rim[8:40] = jnp.where(first, ay_recv[0], ay_recv[1])
    rim[7:8] = jnp.where(first_row, ad_recv[0, 7:8], ad_recv[1, 7:8])
    rim[40:41] = jnp.where(first_row, ad_recv[2, 0:1], ad_recv[3, 0:1])
    whole_rim = rim[...]
    near = (lane_full < 2) | (lane_full >= 126)
    for i in range(20):
        adj[1, i // 4, i % 4 + 1] = jnp.where(
            near, pltpu.roll(whole_rim, (126 - 4 * i) % 128, 1), 0.0
        )
    adj_z = remote(16, adj.at[:, :, z_side + 1], adj.at[:, :, outer], z_other)
    adj_z.start()

    for copy in raw_copies:
        copy.wait()
    sublane = lax.broadcasted_iota(jnp.int32, (16, 640), 0)
    joined = jnp.where(sublane < 9, cols_recv[0].astype(f32), cols_recv[1].astype(f32)).T.astype(bf16)
    halo = [
        jnp.dot(joined, ay_ref[256 + 16 * i : 272 + 16 * i], preferred_element_type=f32)
        for i in range(5)
    ]
    mapped[:, 0:8] += halo[0][0:320].reshape(40, 8, 256)
    mapped[:, 8:16] += halo[0][320:640].reshape(40, 8, 256)
    mapped[:, 16:32] += halo[1].reshape(40, 16, 256)
    mapped[:, 32:48] += halo[2].reshape(40, 16, 256)
    mapped_y2[0:20, 0:32] += halo[3].reshape(20, 32, 256)
    mapped_y2[20:40, 0:32] += halo[4].reshape(20, 32, 256)

    corner_row = lax.broadcasted_iota(jnp.int32, (8, 768), 0)
    corner_lane = lax.broadcasted_iota(jnp.int32, (8, 768), 1)
    parts = [corner_recv[i].astype(f32) for i in range(4)]
    corners = jnp.where(
        corner_lane < 320,
        jnp.where(corner_row < 3, parts[0], parts[1]),
        jnp.where(corner_row < 3, parts[2], parts[3]),
    )
    kind = corner_lane % 8
    low_role = jnp.where(kind < 3, 0, jnp.where(kind < 5, 1, jnp.where(kind < 6, 2, 3)))
    high_role = jnp.where(kind < 4, 0, jnp.where(kind < 7, 1, 2))
    role_of = jnp.where(corner_lane < 320, low_role, jnp.where(corner_lane < 640, high_role, 3))
    stacked = jnp.concatenate([jnp.where(role_of == r, corners, 0.0) for r in range(4)], 0)
    stacked = stacked.T.astype(bf16)
    from_corner = jnp.dot(stacked, ay_ref[336:368], preferred_element_type=f32)
    low_half, high_half = low_recv[...].astype(f32), high_recv[...].astype(f32)

    def unpacked(half, begin, end):
        part = half[begin:end]
        return jnp.concatenate([part[:, 0:64], part[:, 64:128]], 0)

    received = (
        (unpacked(low_half, 0, 160), 0, ((0, 3), (3, 5), (5, 6), (6, 8))),
        (unpacked(high_half, 0, 160), 320, ((0, 4), (4, 7), (7, 8), (8, 8))),
    )
    row_kind = lax.broadcasted_iota(jnp.int32, (320, 64), 0) % 8
    for (values, at, bounds), target in zip(received, (48, 56)):
        total = from_corner[at : at + 320]
        for role, (begin, end) in enumerate(bounds):
            if begin < end:
                part = jnp.where((row_kind >= begin) & (row_kind < end), values, 0.0)
                total = total + jnp.dot(
                    part.astype(bf16), ay_ref[64 * role : 64 * role + 64], preferred_element_type=f32
                )
        mapped[:, target : target + 8] = total.reshape(40, 8, 256)
    more = unpacked(high_half, 160, 208)[0:80].astype(bf16)
    beyond = from_corner[640:720] + jnp.dot(more, ay_ref[192:256], preferred_element_type=f32)
    for p in range(40):
        mapped_y2[p, 32:34] = beyond[2 * p : 2 * p + 2]

    def synthesize(order, cv, carry):
        for z in order:
            p = cv * 4 + z
            exact = mapped[p]
            coarse_bits = exact.astype(bf16)
            rest = (exact - coarse_bits.astype(f32)).astype(bf16)
            whole = jnp.dot(
                small_ref[0:48],
                jnp.concatenate([coarse_bits, rest], axis=0),
                preferred_element_type=f32,
            )
            extra = mapped_y2[p]
            for t in range(2):
                at = slice(128 * t, 128 * t + 128)
                state[t, cv, z + 1, 0:8] = whole[0:8, at]
                state[t, cv, z + 1, 8:48] = whole[8:48, at] + extra[:, at]
        return carry

    def synthesize_sides(pair, carry):
        for j in range(5):
            synthesize((z_side,), 5 * pair + j, carry)
        return carry

    lax.fori_loop(0, 2, synthesize_sides, 0)
    state_first = remote(17, state.at[:, 0:5, z_side + 1], state.at[:, 0:5, outer], z_other)
    state_second = remote(
        18, state.at[0, 5:10, z_side + 1, 8:40], state.at[0, 5:10, outer, 8:40], z_other
    )
    state_first.start()
    state_second.start()
    lax.fori_loop(0, 10, functools.partial(synthesize, (gz, gz + 1, gz + 2)), 0)
    adj_z.wait()
    state_first.wait()

    keep_bottom = jnp.where(gz > 0, 1.0, 0.0).astype(f32)

    def ahead(a, b):
        return pltpu.roll(jnp.where(lane == 0, b, a), 127, 1)

    def behind(a, b):
        return pltpu.roll(jnp.where(lane == 127, b, a), 1, 1)

    def x_face(t, base, source, z, r, start):
        low_at = slice(start + 8 * r, start + 8 + 8 * r)
        high_at = slice(start + 1 + 8 * r, start + 9 + 8 * r)
        mean = [
            0.5 * (state[t, base + v, z + 1, low_at] + state[t, base + v, z + 1, high_at])
            for v in range(5)
        ]
        jump = [source[t, v, z + 1, high_at] - source[t, v, z + 1, low_at] for v in range(5)]
        terms = face(mean, jump, 0)
        for v in range(5):
            gx_terms[t, v, 8 * r : 8 * r + 8] = terms[v]

    def z_face(t, base, source, k, count, start):
        for r in range(count):
            at = slice(start + 8 * r, start + 8 + 8 * r)
            mean = [
                0.5 * (state[t, base + v, k, at] + state[t, base + v, k + 1, at]) for v in range(5)
            ]
            jump = [source[t, v, k + 1, at] - source[t, v, k, at] for v in range(5)]
            terms = face(mean, jump, 2)
            factor = jnp.where(k == 0, keep_bottom, 1.0)
            for v in range(5):
                gz_terms[t, v, k, 8 * r : 8 * r + 8] = terms[v] * factor

    def first_z(k, carry):
        for t in range(2):
            z_face(t, 0, adj, k, 5, 7)
        return carry

    lax.fori_loop(0, 5, first_z, 0)
    mid_z = remote(19, mid.at[0, :, z_side + 1, 8:40], mid.at[0, :, outer, 8:40], z_other)

    def first_plane(j, carry):
        @pl.when(j == 1)
        def _():
            mid_z.start()

        z = jnp.where(gz > 0, j, 3 - j)
        for t in range(2):
            for r in range(5):
                x_face(t, 0, adj, z, r, 6)
        for r in range(5):
            at, rows = slice(7 + 8 * r, 15 + 8 * r), slice(8 * r, 8 * r + 8)
            here = [[state[t, v, z + 1, at] for v in range(5)] for t in range(2)]
            held = [[adj[t, v, z + 1, at] for v in range(5)] for t in range(2)]
            adj_up = [[ahead(held[t][v], held[1 - t][v]) for v in range(5)] for t in range(2)]
            up = [
                face(
                    [0.5 * (here[t][v] + ahead(here[t][v], here[1 - t][v])) for v in range(5)],
                    [adj_up[t][v] - held[t][v] for v in range(5)],
                    1,
                )
                for t in range(2)
            ]
            for t in range(2):
                for v in range(5):
                    halves = (
                        up[t][v]
                        + behind(up[t][v], up[1 - t][v])
                        + gx_terms[t, v, rows]
                        + gx_terms[t, v, 8 * r + 1 : 8 * r + 9]
                        + gz_terms[t, v, z, rows]
                        + gz_terms[t, v, z + 1, rows]
                    )
                    around = (
                        adj_up[t][v]
                        + behind(held[t][v], held[1 - t][v])
                        + adj[t, v, z + 1, 6 + 8 * r : 14 + 8 * r]
                        + adj[t, v, z + 1, 8 + 8 * r : 16 + 8 * r]
                        + adj[t, v, z, at]
                        + adj[t, v, z + 2, at]
                    )
                    value = 0.5 * halves + viscosity * (around - 6.0 * held[t][v])
                    mid[t, v, z + 1, at] = held[t][v] + time_step * value
                    if t == 0:
                        out_ref[v, z, at] = held[t][v] + 0.5 * time_step * value
        return carry

    lax.fori_loop(0, 4, first_plane, 0)
    state_second.wait()

    def second_z(k, carry):
        z_face(0, 5, mid, k, 4, 8)
        return carry

    lax.fori_loop(gz, gz + 4, second_z, 0)

    def store(z):
        return pltpu.make_async_copy(out_ref.at[:, z, 8:40], out_any.at[:, z], load_sem.at[9 + z])

    def second_plane(j, carry):
        z = jnp.where(gz > 0, 3 - j, j)

        @pl.when(j == 3)
        def _():
            mid_z.wait()
            z_face(0, 5, mid, 4 - 4 * gz, 4, 8)

        for r in range(5):
            x_face(0, 5, mid, z, r, 7)
        for r in range(4):
            at, rows = slice(8 + 8 * r, 16 + 8 * r), slice(8 * r, 8 * r + 8)
            here = [state[0, 5 + v, z + 1, at] for v in range(5)]
            edge = [state[1, 5 + v, z + 1, at] for v in range(5)]
            held = [mid[0, v, z + 1, at] for v in range(5)]
            held_edge = [mid[1, v, z + 1, at] for v in range(5)]
            adj_up = [ahead(held[v], held_edge[v]) for v in range(5)]
            adj_down = [behind(held[v], held_edge[v]) for v in range(5)]
            up = face(
                [0.5 * (here[v] + ahead(here[v], edge[v])) for v in range(5)],
                [adj_up[v] - held[v] for v in range(5)],
                1,
            )
            down = face(
                [0.5 * (here[v] + behind(here[v], edge[v])) for v in range(5)],
                [held[v] - adj_down[v] for v in range(5)],
                1,
            )
            for v in range(5):
                halves = (
                    up[v]
                    + down[v]
                    + gx_terms[0, v, rows]
                    + gx_terms[0, v, 8 * r + 1 : 8 * r + 9]
                    + gz_terms[0, v, z, rows]
                    + gz_terms[0, v, z + 1, rows]
                )
                around = (
                    adj_up[v]
                    + adj_down[v]
                    + mid[0, v, z + 1, 7 + 8 * r : 15 + 8 * r]
                    + mid[0, v, z + 1, 9 + 8 * r : 17 + 8 * r]
                    + mid[0, v, z, at]
                    + mid[0, v, z + 2, at]
                )
                value = 0.5 * halves + viscosity * (around - 6.0 * held[v])
                out_ref[v, z, at] += 0.5 * time_step * value
        store(z).start()
        return carry

    lax.fori_loop(0, 4, second_plane, 0)
    for z in range(4):
        store(z).wait()


def shards(coarse, detail_x1, detail_y1, detail_x2, detail_y2, significance, adjoint):
    anywhere = pl.BlockSpec(memory_space=pl.ANY)
    return pl.pallas_call(
        kernel,
        out_shape=jax.ShapeDtypeStruct(adjoint.shape, f32),
        in_specs=[anywhere] * 9,
        out_specs=anywhere,
        scratch_shapes=[
            pltpu.VMEM((640, 32), bf16),
            pltpu.VMEM((640, 32), bf16),
            pltpu.VMEM((640, 64), bf16),
            pltpu.VMEM((1280, 64), bf16),
            pltpu.VMEM((2, 4, 4, 4), jnp.int32),
            pltpu.VMEM((5, 4, 32, 128), f32),
            pltpu.VMEM((368, 256), bf16),
            pltpu.VMEM((144, 128), bf16),
            pltpu.VMEM((5, 4, 48, 128), f32),
            pltpu.SemaphoreType.DMA((13,)),
            pltpu.VMEM((2, 4, 8, 64), f32),
            pltpu.VMEM((2, 4, 16, 64), f32),
            pltpu.VMEM((2, 4, 32, 64), f32),
            pltpu.VMEM((3200, 128), f32),
            pltpu.VMEM((96, 128), f32),
            pltpu.VMEM((16, 640), bf16),
            pltpu.VMEM((2, 16, 640), bf16),
            pltpu.VMEM((160, 128), bf16),
            pltpu.VMEM((160, 128), bf16),
            pltpu.VMEM((208, 128), bf16),
            pltpu.VMEM((208, 128), bf16),
            pltpu.VMEM((8, 768), bf16),
            pltpu.VMEM((4, 8, 768), bf16),
            pltpu.VMEM((2, 40, 128), f32),
            pltpu.VMEM((2, 40, 128), f32),
            pltpu.VMEM((32, 128), f32),
            pltpu.VMEM((2, 32, 128), f32),
            pltpu.VMEM((4, 8, 128), f32),
            pltpu.VMEM((48, 128), f32),
            pltpu.VMEM((40, 64, 256), f32),
            pltpu.VMEM((40, 40, 256), f32),
            pltpu.VMEM((2, 10, 6, 48, 128), f32),
            pltpu.VMEM((2, 5, 6, 48, 128), f32),
            pltpu.VMEM((2, 5, 6, 48, 128), f32),
            pltpu.VMEM((2, 5, 48, 128), f32),
            pltpu.VMEM((2, 5, 5, 40, 128), f32),
            pltpu.SemaphoreType.DMA((20,)),
            pltpu.SemaphoreType.DMA((20,)),
        ],
        compiler_params=pltpu.CompilerParams(collective_id=0, has_side_effects=True),
    )(
        coarse.reshape(320, 32),
        detail_x1.reshape(320, 32),
        detail_y1.reshape(640, 32),
        detail_x2.reshape(640, 64),
        detail_y2.reshape(1280, 64),
        significance,
        adjoint,
        jnp.asarray(y_matrices()),
        jnp.asarray(small_matrices()),
    )


def solution(mesh):
    return jax.shard_map(
        shards,
        mesh=mesh,
        in_specs=(
            P(None, None, "gz", "gx", "gy"),
            P(None, None, "gz", "gx", "gy"),
            P(None, None, "gz", "gx", "gy"),
            P(None, None, "gz", "gx", "gy"),
            P(None, None, "gz", "gx", "gy"),
            P(None, "gz", "gx", "gy"),
            P(None, "gz", "gx", "gy"),
        ),
        out_specs=P(None, "gz", "gx", "gy"),
        check_vma=False,
    )
```

```python
import functools

import jax
import jax.numpy as jnp
import ml_dtypes
import numpy as np
from jax import lax
from jax.experimental import pallas as pl
from jax.experimental.pallas import tpu as pltpu
from jax.sharding import PartitionSpec as P

time_step = 0.1
viscosity = 0.2
heat_ratio_less_one = 0.4
f32 = jnp.float32
bf16 = jnp.bfloat16
MESH = pl.DeviceIdType.MESH


def predict(index):
    k = index // 2
    if index % 2 == 0:
        return {("c", k): 1.0}
    return {
        ("d", k): 1.0,
        ("c", k): 9 / 16,
        ("c", k + 1): 9 / 16,
        ("c", k - 1): -1 / 16,
        ("c", k + 2): -1 / 16,
    }


def predict_twice(index):
    whole = {}
    for (kind, k), weight in predict(index).items():
        if kind == "d":
            whole[("e", k)] = weight
            continue
        whole[("m", k)] = weight
        for key, inner in predict(k).items():
            whole[key] = whole.get(key, 0.0) + weight * inner
    return whole


def halo_row(kind, k):
    if kind == "c":
        return k - 32 if k >= 32 else 11 + k
    if kind == "d":
        return 3 if k >= 32 else 11
    if kind == "m":
        return 4 + k - 64 if k >= 64 else 14 + k
    return 7 if k >= 64 else 14


def y_matrices():
    own = np.zeros((4, 64, 256), np.float32)
    halo = np.zeros((5, 16, 256), np.float32)
    corner = np.zeros((4, 8, 256), np.float32)
    columns = [(y, y) for y in range(128)] + [(128, 128), (129, 129), (-1, 255), (-2, 254)]
    for y, column in columns:
        for (kind, k), weight in predict_twice(y).items():
            role = "cdme".index(kind)
            length = 32 if role < 2 else 64
            if 0 <= k < length:
                own[role, k, column] += weight
                continue
            row = halo_row(kind, k)
            halo[role, row, column] += weight
            if kind == "e":
                halo[4, row + 1, column] += weight
            if k >= length:
                corner[role, k - length, column] += weight
            else:
                corner[role, (5 if length == 32 else 7) + k, column] += weight
    parts = [own.reshape(256, 256), halo.reshape(80, 256), corner.reshape(32, 256)]
    return np.concatenate(parts).astype(ml_dtypes.bfloat16)


def small_matrices():
    mats = np.zeros((144, 128), np.float32)
    for x in range(-2, 34):
        row = x + 8
        for (kind, k), weight in predict_twice(x).items():
            if kind == "c":
                at = 50 + k if k < 0 else (k if k < 8 else 56 + k - 8)
            elif kind == "d":
                at = 50 if k < 0 else (8 + k if k < 8 else 59)
            elif kind == "m":
                at = 53 + k if k < 0 else (16 + k if k < 16 else 60 + k - 16)
            else:
                at = 53 if k < 0 else (32 + k if k < 16 else 63)
            mats[row, at] += weight
    mats[6, 54] = 1.0
    mats[7, 55] = 1.0
    mats[0:48, 64:128] = mats[0:48, 0:64]
    picks = mats[48:128].reshape(5, 16, 128)
    for row, column in ((0, 0), (1, 1), (2, 2), (9, 30), (10, 31)):
        picks[0, row, column] = 1.0
    for row, column in ((3, 0), (11, 31)):
        picks[1, row, column] = 1.0
    for row, column in ((4, 0), (5, 1), (6, 2), (12, 62), (13, 63)):
        picks[2, row, column] = 1.0
    for row, column in ((7, 0), (14, 63)):
        picks[3, row, column] = 1.0
        picks[4, row + 1, column] = 1.0
    for row, column in ((0, 0), (1, 1), (2, 2), (3, 30), (4, 31), (5, 62), (6, 63)):
        mats[128 + row, column] = 1.0
    return mats.astype(ml_dtypes.bfloat16)


def face(mean, jump, k):
    q, u, t = mean[0], mean[1:4], mean[4]
    rho = jnp.exp(0.5 * q)
    speed = u[k]
    half_square = 0.5 * (u[0] * u[0] + u[1] * u[1] + u[2] * u[2])
    enthalpy = (1.0 / heat_ratio_less_one + 1.0) * t + half_square
    inner = jump[0] + jump[1] * u[0] + jump[2] * u[1] + jump[3] * u[2] + jump[4] * enthalpy
    flow = rho * speed
    grads = [flow * (jump[1 + j] + jump[4] * u[j]) for j in range(3)]
    grads[k] = grads[k] + rho * inner
    dq = 0.5 * (flow * inner + rho * t * jump[1 + k])
    dt = rho * jump[1 + k] + (1.0 / heat_ratio_less_one + 1.0) * flow * jump[4]
    return [dq] + grads + [dt]


def kernel(
    c_in, x1_in, y1_in, x2_in, y2_in, sig_in, adj_in, ay_in, small_in,
    result,
    cx_ref, y1_ref, x2_ref, y2_ref, sig_ref, adj_ref, ay_ref, small_ref,
    partial, load_sem,
    tiles, mask_x, mask_y, ext, hy2,
    cols_send, cols_recv, low_send, low_recv, high_send, high_recv, corner_send, corner_recv,
    ax_send, ax_recv, ay_send, ay_recv, ad_recv, rim,
    mapped, mapped_y2, state, adj, mid, gx_terms, gz_terms,
    send_sem, recv_sem,
):
    gx, gy, gz = lax.axis_index("gx"), lax.axis_index("gy"), lax.axis_index("gz")
    nx, ny = lax.axis_size("gx"), lax.axis_size("gy")
    up_x, down_x = lax.rem(gx + 1, nx), lax.rem(gx + nx - 1, nx)
    up_y, down_y = lax.rem(gy + 1, ny), lax.rem(gy + ny - 1, ny)
    x_up, x_down = {"gx": up_x}, {"gx": down_x}
    y_up, y_down = {"gy": up_y}, {"gy": down_y}
    diagonal = (
        {"gx": up_x, "gy": down_y},
        {"gx": up_x, "gy": up_y},
        {"gx": down_x, "gy": down_y},
        {"gx": down_x, "gy": up_y},
    )
    z_other = {"gz": 1 - gz}
    barrier = pltpu.get_barrier_semaphore()
    for peer in (x_up, x_down, y_up, y_down, z_other) + diagonal:
        pl.semaphore_signal(barrier, inc=1, device_id=peer, device_id_type=MESH)

    pairs = (
        (sig_in, sig_ref), (x2_in, x2_ref), (y2_in, y2_ref), (c_in, cx_ref.at[0:320]),
        (x1_in, cx_ref.at[320:640]), (y1_in, y1_ref), (small_in, small_ref), (adj_in, adj_ref),
        (ay_in, ay_ref),
    )
    loads = [
        pltpu.make_async_copy(source, target, load_sem.at[i])
        for i, (source, target) in enumerate(pairs)
    ]
    for load in loads:
        load.start()

    def remote(index, source, target, peer):
        return pltpu.make_async_remote_copy(
            src_ref=source,
            dst_ref=target,
            send_sem=send_sem.at[index],
            recv_sem=recv_sem.at[index],
            device_id=peer,
            device_id_type=MESH,
        )

    def transposed(left, right):
        return lax.dot_general(left, right, (((1,), (1,)), ((), ())), preferred_element_type=f32)

    lane = lax.broadcasted_iota(jnp.int32, (8, 128), 1)
    lane_wide = lax.broadcasted_iota(jnp.int32, (32, 128), 1)
    lane_full = lax.broadcasted_iota(jnp.int32, (48, 128), 1)

    for load in loads[:8]:
        load.wait()
    lane_tile = lax.broadcasted_iota(jnp.int32, (4, 64), 1) // 16
    row_half = lax.broadcasted_iota(jnp.int32, (8, 64), 0) < 4
    for c in range(2):
        for z in range(4):
            flags = sig_ref[c, z].astype(f32)
            wide = jnp.zeros((4, 64), f32)
            for t in range(4):
                wide = jnp.where(lane_tile == t, flags[:, t : t + 1], wide)
            tiles[c, z, 0:4] = wide
            each = [jnp.broadcast_to(tiles[c, z, t : t + 1], (8, 64)) for t in range(4)]
            for t in range(4):
                mask_y[c, z, 8 * t : 8 * t + 8] = each[t]
            for t in range(2):
                mask_x[c, z, 8 * t : 8 * t + 8] = jnp.where(row_half, each[2 * t], each[2 * t + 1])

    kept_x2 = x2_ref[...].astype(f32).reshape(2, 5, 4, 16, 64) * mask_x[...][:, None]
    kept_y2 = y2_ref[...].astype(f32).reshape(2, 5, 4, 32, 64) * mask_y[...][:, None]
    ext[...] = jnp.zeros_like(ext)
    ext[0:640, 0:32] = cx_ref[...].astype(f32)
    ext[640:1280, 0:32] = y1_ref[...].astype(f32)
    ext[1280:1920, 0:64] = kept_x2.reshape(640, 64)
    ext[1920:3200, 0:64] = kept_y2.reshape(1280, 64)

    def own(begin, end):
        return ext[begin:end, 0:64].astype(bf16)

    starts = (0, 640, 1280, 1920, 2560)
    cols = jnp.zeros((16, 640), f32)
    for which, begin in enumerate(starts):
        pick = small_ref[48 + 16 * which : 64 + 16 * which, 0:64]
        cols = cols + transposed(pick, own(begin, begin + 640))
    cols_send[...] = cols.astype(bf16)

    coarse_e = ext[0:320].reshape(40, 8, 128)
    x1_e = ext[320:640].reshape(40, 8, 128)
    y1_e = ext[640:1280].reshape(40, 16, 128)
    x2_e = ext[1280:1920].reshape(40, 16, 128)
    y2_e = ext[1920:3200].reshape(40, 32, 128)
    low = jnp.concatenate(
        [coarse_e[:, 6:8], x1_e[:, 7:8], y1_e[:, 14:16], x2_e[:, 15:16], y2_e[:, 30:32]], 1
    ).reshape(320, 128)
    high = jnp.concatenate(
        [coarse_e[:, 0:3], x1_e[:, 0:1], y1_e[:, 0:3], x2_e[:, 0:1]], 1
    ).reshape(320, 128)
    hy2[80:96] = jnp.zeros((16, 128), f32)
    for p in range(40):
        hy2[2 * p : 2 * p + 2] = ext[1920 + 32 * p : 1922 + 32 * p]
    more = hy2[0:48] + pltpu.roll(hy2[48:96], 64, 1)
    low_send[...] = (low[0:160] + pltpu.roll(low[160:320], 64, 1)).astype(bf16)
    high_send[0:160] = (high[0:160] + pltpu.roll(high[160:320], 64, 1)).astype(bf16)
    high_send[160:208] = more.astype(bf16)
    rows = jnp.concatenate([low, high, hy2[0:80]], 0)[:, 0:64].astype(bf16)
    corner_send[:, 0:720] = transposed(small_ref[128:144, 0:64], rows)[0:8].astype(bf16)
    corner_send[:, 720:768] = jnp.zeros((8, 48), bf16)

    columns = jnp.zeros((32, 128), f32)
    for i in range(20):
        plane = adj_ref[i // 4, i % 4]
        columns = jnp.where(lane_wide // 4 == i, pltpu.roll(plane, 4 * i + 2, 1), columns)
        ax_send[0, 2 * i : 2 * i + 2] = plane[0:2]
        ax_send[1, 2 * i : 2 * i + 2] = plane[30:32]
    ay_send[...] = columns

    pl.semaphore_wait(barrier, 9)
    adj_copies = [
        remote(8, ay_send, ay_recv.at[0], y_down),
        remote(9, ay_send, ay_recv.at[1], y_up),
        remote(10, ax_send.at[0], ax_recv.at[1], x_down),
        remote(11, ax_send.at[1], ax_recv.at[0], x_up),
    ] + [
        remote(12 + i, ay_send.at[24 - 24 * (i // 2) : 32 - 24 * (i // 2)], ad_recv.at[i], diagonal[i])
        for i in range(4)
    ]
    raw_copies = [
        remote(0, cols_send, cols_recv.at[0], y_down),
        remote(1, cols_send, cols_recv.at[1], y_up),
        remote(2, low_send, low_recv, x_up),
        remote(3, high_send, high_recv, x_down),
    ] + [remote(4 + i, corner_send, corner_recv.at[i], diagonal[i]) for i in range(4)]
    for copy in adj_copies + raw_copies:
        copy.start()

    loads[8].wait()
    for begin, count, role, target, at in (
        (0, 8, 0, mapped, 0),
        (320, 8, 0, mapped, 8),
        (640, 16, 1, mapped, 16),
        (1280, 16, 2, mapped, 32),
        (1920, 32, 3, mapped_y2, 0),
    ):
        product = jnp.dot(
            own(begin, begin + 40 * count),
            ay_ref[64 * role : 64 * role + 64],
            preferred_element_type=f32,
        )
        target[:, at : at + count] = product.reshape(40, count, 256)
    mapped_y2[:, 32:40] = jnp.zeros((40, 8, 256), f32)

    outer = 5 * gz
    z_side = 3 - 3 * gz
    blank = jnp.zeros((48, 128), f32)
    for t in range(2):
        for v in range(5):
            adj[t, v, outer] = blank
            mid[t, v, outer] = blank
        for cv in range(10):
            state[t, cv, outer] = blank
    for i in range(20):
        v, z = i // 4, i % 4
        adj[0, v, z + 1, 0:8] = blank[0:8]
        adj[0, v, z + 1, 40:48] = blank[0:8]
        adj[0, v, z + 1, 8:40] = adj_ref[v, z]
    rim[...] = blank

    for copy in adj_copies:
        copy.wait()
    for i in range(20):
        v, z = i // 4, i % 4
        adj[0, v, z + 1, 6:8] = ax_recv[0, 2 * i : 2 * i + 2]
        adj[0, v, z + 1, 40:42] = ax_recv[1, 2 * i : 2 * i + 2]
    first = lane_wide % 4 >= 2
    first_row = first[0:1]
    rim[8:40] = jnp.where(first, ay_recv[0], ay_recv[1])
    rim[7:8] = jnp.where(first_row, ad_recv[0, 7:8], ad_recv[1, 7:8])
    rim[40:41] = jnp.where(first_row, ad_recv[2, 0:1], ad_recv[3, 0:1])
    whole_rim = rim[...]
    near = (lane_full < 2) | (lane_full >= 126)
    for i in range(20):
        adj[1, i // 4, i % 4 + 1] = jnp.where(
            near, pltpu.roll(whole_rim, (126 - 4 * i) % 128, 1), 0.0
        )
    adj_z = remote(16, adj.at[:, :, z_side + 1], adj.at[:, :, outer], z_other)
    adj_z.start()

    for copy in raw_copies:
        copy.wait()
    sublane = lax.broadcasted_iota(jnp.int32, (16, 640), 0)
    joined = jnp.where(sublane < 9, cols_recv[0].astype(f32), cols_recv[1].astype(f32)).T.astype(bf16)
    halo = [
        jnp.dot(joined, ay_ref[256 + 16 * i : 272 + 16 * i], preferred_element_type=f32)
        for i in range(5)
    ]
    mapped[:, 0:8] += halo[0][0:320].reshape(40, 8, 256)
    mapped[:, 8:16] += halo[0][320:640].reshape(40, 8, 256)
    mapped[:, 16:32] += halo[1].reshape(40, 16, 256)
    mapped[:, 32:48] += halo[2].reshape(40, 16, 256)
    mapped_y2[0:20, 0:32] += halo[3].reshape(20, 32, 256)
    mapped_y2[20:40, 0:32] += halo[4].reshape(20, 32, 256)

    corner_row = lax.broadcasted_iota(jnp.int32, (8, 768), 0)
    corner_lane = lax.broadcasted_iota(jnp.int32, (8, 768), 1)
    parts = [corner_recv[i].astype(f32) for i in range(4)]
    corners = jnp.where(
        corner_lane < 320,
        jnp.where(corner_row < 3, parts[0], parts[1]),
        jnp.where(corner_row < 3, parts[2], parts[3]),
    )
    kind = corner_lane % 8
    low_role = jnp.where(kind < 3, 0, jnp.where(kind < 5, 1, jnp.where(kind < 6, 2, 3)))
    high_role = jnp.where(kind < 4, 0, jnp.where(kind < 7, 1, 2))
    role_of = jnp.where(corner_lane < 320, low_role, jnp.where(corner_lane < 640, high_role, 3))
    stacked = jnp.concatenate([jnp.where(role_of == r, corners, 0.0) for r in range(4)], 0)
    stacked = stacked.T.astype(bf16)
    from_corner = jnp.dot(stacked, ay_ref[336:368], preferred_element_type=f32)
    low_half, high_half = low_recv[...].astype(f32), high_recv[...].astype(f32)

    def unpacked(half, begin, end):
        part = half[begin:end]
        return jnp.concatenate([part[:, 0:64], part[:, 64:128]], 0)

    received = (
        (unpacked(low_half, 0, 160), 0, ((0, 3), (3, 5), (5, 6), (6, 8))),
        (unpacked(high_half, 0, 160), 320, ((0, 4), (4, 7), (7, 8), (8, 8))),
    )
    row_kind = lax.broadcasted_iota(jnp.int32, (320, 64), 0) % 8
    for (values, at, bounds), target in zip(received, (48, 56)):
        total = from_corner[at : at + 320]
        for role, (begin, end) in enumerate(bounds):
            if begin < end:
                part = jnp.where((row_kind >= begin) & (row_kind < end), values, 0.0)
                total = total + jnp.dot(
                    part.astype(bf16), ay_ref[64 * role : 64 * role + 64], preferred_element_type=f32
                )
        mapped[:, target : target + 8] = total.reshape(40, 8, 256)
    more = unpacked(high_half, 160, 208)[0:80].astype(bf16)
    beyond = from_corner[640:720] + jnp.dot(more, ay_ref[192:256], preferred_element_type=f32)
    for p in range(40):
        mapped_y2[p, 32:34] = beyond[2 * p : 2 * p + 2]

    def synthesize(order, cv, carry):
        for z in order:
            p = cv * 4 + z
            exact = mapped[p]
            coarse_bits = exact.astype(bf16)
            rest = (exact - coarse_bits.astype(f32)).astype(bf16)
            whole = jnp.dot(
                small_ref[0:48],
                jnp.concatenate([coarse_bits, rest], axis=0),
                preferred_element_type=f32,
            )
            extra = mapped_y2[p]
            for t in range(2):
                at = slice(128 * t, 128 * t + 128)
                state[t, cv, z + 1, 0:8] = whole[0:8, at]
                state[t, cv, z + 1, 8:48] = whole[8:48, at] + extra[:, at]
        return carry

    def synthesize_sides(pair, carry):
        for j in range(5):
            synthesize((z_side,), 5 * pair + j, carry)
        return carry

    for cv in range(10):
        synthesize((z_side,), cv, 0)
    state_first = remote(17, state.at[:, 0:5, z_side + 1], state.at[:, 0:5, outer], z_other)
    state_second = remote(
        18, state.at[0, 5:10, z_side + 1, 8:40], state.at[0, 5:10, outer, 8:40], z_other
    )
    state_first.start()
    state_second.start()
    def synthesize_rest(pair, carry):
        for j in range(5):
            synthesize((gz, gz + 1, gz + 2), 5 * pair + j, carry)
        return carry

    lax.fori_loop(0, 2, synthesize_rest, 0)
    adj_z.wait()
    state_first.wait()

    keep_bottom = jnp.where(gz > 0, 1.0, 0.0).astype(f32)

    def ahead(a, b):
        return pltpu.roll(jnp.where(lane == 0, b, a), 127, 1)

    def behind(a, b):
        return pltpu.roll(jnp.where(lane == 127, b, a), 1, 1)

    def x_face(t, base, source, z, r, start):
        low_at = slice(start + 8 * r, start + 8 + 8 * r)
        high_at = slice(start + 1 + 8 * r, start + 9 + 8 * r)
        mean = [
            0.5 * (state[t, base + v, z + 1, low_at] + state[t, base + v, z + 1, high_at])
            for v in range(5)
        ]
        jump = [source[t, v, z + 1, high_at] - source[t, v, z + 1, low_at] for v in range(5)]
        terms = face(mean, jump, 0)
        for v in range(5):
            gx_terms[t, v, 8 * r : 8 * r + 8] = terms[v]

    def z_face(t, base, source, k, count, start):
        for r in range(count):
            at = slice(start + 8 * r, start + 8 + 8 * r)
            mean = [
                0.5 * (state[t, base + v, k, at] + state[t, base + v, k + 1, at]) for v in range(5)
            ]
            jump = [source[t, v, k + 1, at] - source[t, v, k, at] for v in range(5)]
            terms = face(mean, jump, 2)
            factor = jnp.where(k == 0, keep_bottom, 1.0)
            for v in range(5):
                gz_terms[t, v, k, 8 * r : 8 * r + 8] = terms[v] * factor

    def first_z(k, carry):
        for t in range(2):
            z_face(t, 0, adj, k, 5, 7)
        return carry

    lax.fori_loop(0, 5, first_z, 0)
    mid_z = remote(19, mid.at[0, :, z_side + 1, 8:40], mid.at[0, :, outer, 8:40], z_other)

    def first_plane(j, carry):
        @pl.when(j == 1)
        def _():
            mid_z.start()

        z = jnp.where(gz > 0, j, 3 - j)
        for t in range(2):
            for r in range(5):
                x_face(t, 0, adj, z, r, 6)
        for r in range(5):
            at, rows = slice(7 + 8 * r, 15 + 8 * r), slice(8 * r, 8 * r + 8)
            here = [[state[t, v, z + 1, at] for v in range(5)] for t in range(2)]
            held = [[adj[t, v, z + 1, at] for v in range(5)] for t in range(2)]
            adj_up = [[ahead(held[t][v], held[1 - t][v]) for v in range(5)] for t in range(2)]
            up = [
                face(
                    [0.5 * (here[t][v] + ahead(here[t][v], here[1 - t][v])) for v in range(5)],
                    [adj_up[t][v] - held[t][v] for v in range(5)],
                    1,
                )
                for t in range(2)
            ]
            for t in range(2):
                for v in range(5):
                    halves = (
                        up[t][v]
                        + behind(up[t][v], up[1 - t][v])
                        + gx_terms[t, v, rows]
                        + gx_terms[t, v, 8 * r + 1 : 8 * r + 9]
                        + gz_terms[t, v, z, rows]
                        + gz_terms[t, v, z + 1, rows]
                    )
                    around = (
                        adj_up[t][v]
                        + behind(held[t][v], held[1 - t][v])
                        + adj[t, v, z + 1, 6 + 8 * r : 14 + 8 * r]
                        + adj[t, v, z + 1, 8 + 8 * r : 16 + 8 * r]
                        + adj[t, v, z, at]
                        + adj[t, v, z + 2, at]
                    )
                    value = 0.5 * halves + viscosity * (around - 6.0 * held[t][v])
                    mid[t, v, z + 1, at] = held[t][v] + time_step * value
                    if t == 0:
                        partial[v, z, at] = held[t][v] + 0.5 * time_step * value
        return carry

    lax.fori_loop(0, 4, first_plane, 0)
    state_second.wait()

    def second_z(k, carry):
        z_face(0, 5, mid, k, 4, 8)
        return carry

    lax.fori_loop(gz, gz + 4, second_z, 0)

    def second_plane(j, carry):
        z = jnp.where(gz > 0, 3 - j, j)

        @pl.when(j == 3)
        def _():
            mid_z.wait()
            z_face(0, 5, mid, 4 - 4 * gz, 4, 8)

        for r in range(5):
            x_face(0, 5, mid, z, r, 7)
        for r in range(4):
            at, rows = slice(8 + 8 * r, 16 + 8 * r), slice(8 * r, 8 * r + 8)
            here = [state[0, 5 + v, z + 1, at] for v in range(5)]
            edge = [state[1, 5 + v, z + 1, at] for v in range(5)]
            held = [mid[0, v, z + 1, at] for v in range(5)]
            held_edge = [mid[1, v, z + 1, at] for v in range(5)]
            adj_up = [ahead(held[v], held_edge[v]) for v in range(5)]
            adj_down = [behind(held[v], held_edge[v]) for v in range(5)]
            up = face(
                [0.5 * (here[v] + ahead(here[v], edge[v])) for v in range(5)],
                [adj_up[v] - held[v] for v in range(5)],
                1,
            )
            down = face(
                [0.5 * (here[v] + behind(here[v], edge[v])) for v in range(5)],
                [held[v] - adj_down[v] for v in range(5)],
                1,
            )
            for v in range(5):
                halves = (
                    up[v]
                    + down[v]
                    + gx_terms[0, v, rows]
                    + gx_terms[0, v, 8 * r + 1 : 8 * r + 9]
                    + gz_terms[0, v, z, rows]
                    + gz_terms[0, v, z + 1, rows]
                )
                around = (
                    adj_up[v]
                    + adj_down[v]
                    + mid[0, v, z + 1, 7 + 8 * r : 15 + 8 * r]
                    + mid[0, v, z + 1, 9 + 8 * r : 17 + 8 * r]
                    + mid[0, v, z, at]
                    + mid[0, v, z + 2, at]
                )
                value = 0.5 * halves + viscosity * (around - 6.0 * held[v])
                result[v, z, rows] = partial[v, z, at] + 0.5 * time_step * value
        return carry

    lax.fori_loop(0, 4, second_plane, 0)


def shards(coarse, detail_x1, detail_y1, detail_x2, detail_y2, significance, adjoint):
    operands = [
        pltpu.with_memory_space_constraint(value, pltpu.HBM)
        for value in (
            coarse.reshape(320, 32),
            detail_x1.reshape(320, 32),
            detail_y1.reshape(640, 32),
            detail_x2.reshape(640, 64),
            detail_y2.reshape(1280, 64),
            significance,
            adjoint,
            jnp.asarray(y_matrices()),
            jnp.asarray(small_matrices()),
        )
    ]
    anywhere = pl.BlockSpec(memory_space=pl.ANY)
    return pl.pallas_call(
        kernel,
        out_shape=jax.ShapeDtypeStruct(adjoint.shape, f32),
        in_specs=[anywhere] * 9,
        out_specs=pl.BlockSpec(memory_space=pltpu.VMEM),
        scratch_shapes=[
            pltpu.VMEM((640, 32), bf16),
            pltpu.VMEM((640, 32), bf16),
            pltpu.VMEM((640, 64), bf16),
            pltpu.VMEM((1280, 64), bf16),
            pltpu.VMEM((2, 4, 4, 4), jnp.int32),
            pltpu.VMEM((5, 4, 32, 128), f32),
            pltpu.VMEM((368, 256), bf16),
            pltpu.VMEM((144, 128), bf16),
            pltpu.VMEM((5, 4, 48, 128), f32),
            pltpu.SemaphoreType.DMA((9,)),
            pltpu.VMEM((2, 4, 8, 64), f32),
            pltpu.VMEM((2, 4, 16, 64), f32),
            pltpu.VMEM((2, 4, 32, 64), f32),
            pltpu.VMEM((3200, 128), f32),
            pltpu.VMEM((96, 128), f32),
            pltpu.VMEM((16, 640), bf16),
            pltpu.VMEM((2, 16, 640), bf16),
            pltpu.VMEM((160, 128), bf16),
            pltpu.VMEM((160, 128), bf16),
            pltpu.VMEM((208, 128), bf16),
            pltpu.VMEM((208, 128), bf16),
            pltpu.VMEM((8, 768), bf16),
            pltpu.VMEM((4, 8, 768), bf16),
            pltpu.VMEM((2, 40, 128), f32),
            pltpu.VMEM((2, 40, 128), f32),
            pltpu.VMEM((32, 128), f32),
            pltpu.VMEM((2, 32, 128), f32),
            pltpu.VMEM((4, 8, 128), f32),
            pltpu.VMEM((48, 128), f32),
            pltpu.VMEM((40, 64, 256), f32),
            pltpu.VMEM((40, 40, 256), f32),
            pltpu.VMEM((2, 10, 6, 48, 128), f32),
            pltpu.VMEM((2, 5, 6, 48, 128), f32),
            pltpu.VMEM((2, 5, 6, 48, 128), f32),
            pltpu.VMEM((2, 5, 48, 128), f32),
            pltpu.VMEM((2, 5, 5, 40, 128), f32),
            pltpu.SemaphoreType.DMA((20,)),
            pltpu.SemaphoreType.DMA((20,)),
        ],
        compiler_params=pltpu.CompilerParams(collective_id=0, has_side_effects=True, vmem_limit_bytes=40*2**20),
    )(
        *operands,
    )


def solution(mesh):
    return jax.shard_map(
        shards,
        mesh=mesh,
        in_specs=(
            P(None, None, "gz", "gx", "gy"),
            P(None, None, "gz", "gx", "gy"),
            P(None, None, "gz", "gx", "gy"),
            P(None, None, "gz", "gx", "gy"),
            P(None, None, "gz", "gx", "gy"),
            P(None, "gz", "gx", "gy"),
            P(None, "gz", "gx", "gy"),
        ),
        out_specs=P(None, "gz", "gx", "gy"),
        check_vma=False,
    )
```

```python
import functools

import jax
import jax.numpy as jnp
import ml_dtypes
import numpy as np
from jax import lax
from jax.experimental import pallas as pl
from jax.experimental.pallas import tpu as pltpu
from jax.sharding import PartitionSpec as P

time_step = 0.1
viscosity = 0.2
heat_ratio_less_one = 0.4
f32 = jnp.float32
bf16 = jnp.bfloat16
MESH = pl.DeviceIdType.MESH


def predict(index):
    k = index // 2
    if index % 2 == 0:
        return {("c", k): 1.0}
    return {
        ("d", k): 1.0,
        ("c", k): 9 / 16,
        ("c", k + 1): 9 / 16,
        ("c", k - 1): -1 / 16,
        ("c", k + 2): -1 / 16,
    }


def predict_twice(index):
    whole = {}
    for (kind, k), weight in predict(index).items():
        if kind == "d":
            whole[("e", k)] = weight
            continue
        whole[("m", k)] = weight
        for key, inner in predict(k).items():
            whole[key] = whole.get(key, 0.0) + weight * inner
    return whole


def halo_row(kind, k):
    if kind == "c":
        return k - 32 if k >= 32 else 11 + k
    if kind == "d":
        return 3 if k >= 32 else 11
    if kind == "m":
        return 4 + k - 64 if k >= 64 else 14 + k
    return 7 if k >= 64 else 14


def y_matrices():
    own = np.zeros((4, 64, 256), np.float32)
    halo = np.zeros((5, 16, 256), np.float32)
    corner = np.zeros((4, 8, 256), np.float32)
    columns = [(y, y) for y in range(128)] + [(128, 128), (129, 129), (-1, 255), (-2, 254)]
    for y, column in columns:
        for (kind, k), weight in predict_twice(y).items():
            role = "cdme".index(kind)
            length = 32 if role < 2 else 64
            if 0 <= k < length:
                own[role, k, column] += weight
                continue
            row = halo_row(kind, k)
            halo[role, row, column] += weight
            if kind == "e":
                halo[4, row + 1, column] += weight
            if k >= length:
                corner[role, k - length, column] += weight
            else:
                corner[role, (5 if length == 32 else 7) + k, column] += weight
    parts = [own.reshape(256, 256), halo.reshape(80, 256), corner.reshape(32, 256)]
    return (0.5 * np.concatenate(parts)).astype(ml_dtypes.bfloat16)


def small_matrices():
    mats = np.zeros((144, 128), np.float32)
    for x in range(-2, 34):
        row = x + 8
        for (kind, k), weight in predict_twice(x).items():
            if kind == "c":
                at = 50 + k if k < 0 else (k if k < 8 else 56 + k - 8)
            elif kind == "d":
                at = 50 if k < 0 else (8 + k if k < 8 else 59)
            elif kind == "m":
                at = 53 + k if k < 0 else (16 + k if k < 16 else 60 + k - 16)
            else:
                at = 53 if k < 0 else (32 + k if k < 16 else 63)
            mats[row, at] += weight
    mats[6, 54] = 1.0
    mats[7, 55] = 1.0
    mats[0:48, 64:128] = mats[0:48, 0:64]
    picks = mats[48:128].reshape(5, 16, 128)
    for row, column in ((0, 0), (1, 1), (2, 2), (9, 30), (10, 31)):
        picks[0, row, column] = 1.0
    for row, column in ((3, 0), (11, 31)):
        picks[1, row, column] = 1.0
    for row, column in ((4, 0), (5, 1), (6, 2), (12, 62), (13, 63)):
        picks[2, row, column] = 1.0
    for row, column in ((7, 0), (14, 63)):
        picks[3, row, column] = 1.0
        picks[4, row + 1, column] = 1.0
    for row, column in ((0, 0), (1, 1), (2, 2), (3, 30), (4, 31), (5, 62), (6, 63)):
        mats[128 + row, column] = 1.0
    return mats.astype(ml_dtypes.bfloat16)


def face(mean, jump, k):
    q, u, t = mean[0], mean[1:4], mean[4]
    rho = jnp.exp(0.5 * q)
    speed = u[k]
    half_square = 0.5 * (u[0] * u[0] + u[1] * u[1] + u[2] * u[2])
    enthalpy = (1.0 / heat_ratio_less_one + 1.0) * t + half_square
    inner = jump[0] + jump[1] * u[0] + jump[2] * u[1] + jump[3] * u[2] + jump[4] * enthalpy
    flow = rho * speed
    grads = [flow * (jump[1 + j] + jump[4] * u[j]) for j in range(3)]
    grads[k] = grads[k] + rho * inner
    dq = 0.5 * (flow * inner + rho * t * jump[1 + k])
    dt = rho * jump[1 + k] + (1.0 / heat_ratio_less_one + 1.0) * flow * jump[4]
    return [dq] + grads + [dt]


def kernel(
    c_in, x1_in, y1_in, x2_in, y2_in, sig_in, adj_in, ay_in, small_in,
    result,
    cx_ref, y1_ref, x2_ref, y2_ref, sig_ref, adj_ref, ay_ref, small_ref,
    partial, load_sem,
    tiles, mask_x, mask_y, ext, hy2,
    first_send, first_recv, last_send, last_recv, low_send, low_recv, high_send, high_recv,
    corner_low, corner_low_recv, corner_high, corner_high_recv,
    ax_rows, ax_send, ax_recv, ay_send, ay_recv, rim,
    mapped, mapped_y2, state, adj, mid, gx_terms, gz_terms,
    send_sem, recv_sem,
):
    gx, gy, gz = lax.axis_index("gx"), lax.axis_index("gy"), lax.axis_index("gz")
    nx, ny = lax.axis_size("gx"), lax.axis_size("gy")
    up_x, down_x = lax.rem(gx + 1, nx), lax.rem(gx + nx - 1, nx)
    up_y, down_y = lax.rem(gy + 1, ny), lax.rem(gy + ny - 1, ny)
    x_up, x_down = {"gx": up_x}, {"gx": down_x}
    y_up, y_down = {"gy": up_y}, {"gy": down_y}
    diagonal = (
        {"gx": up_x, "gy": down_y},
        {"gx": up_x, "gy": up_y},
        {"gx": down_x, "gy": down_y},
        {"gx": down_x, "gy": up_y},
    )
    z_other = {"gz": 1 - gz}
    barrier = pltpu.get_barrier_semaphore()
    for peer in (x_up, x_down, y_up, y_down, z_other) + diagonal:
        pl.semaphore_signal(barrier, inc=1, device_id=peer, device_id_type=MESH)

    pairs = (
        (sig_in, sig_ref), (x2_in, x2_ref), (y2_in, y2_ref), (c_in, cx_ref.at[0:320]),
        (x1_in, cx_ref.at[320:640]), (y1_in, y1_ref), (small_in, small_ref), (adj_in, adj_ref),
        (ay_in, ay_ref),
    )
    loads = [
        pltpu.make_async_copy(source, target, load_sem.at[i])
        for i, (source, target) in enumerate(pairs)
    ]
    for load in loads:
        load.start()

    def remote(index, source, target, peer):
        return pltpu.make_async_remote_copy(
            src_ref=source,
            dst_ref=target,
            send_sem=send_sem.at[index],
            recv_sem=recv_sem.at[index],
            device_id=peer,
            device_id_type=MESH,
        )

    def transposed(left, right):
        return lax.dot_general(left, right, (((1,), (1,)), ((), ())), preferred_element_type=f32)

    lane = lax.broadcasted_iota(jnp.int32, (8, 128), 1)
    lane_wide = lax.broadcasted_iota(jnp.int32, (32, 128), 1)
    lane_full = lax.broadcasted_iota(jnp.int32, (48, 128), 1)

    for load in loads[:8]:
        load.wait()
    lane_tile = lax.broadcasted_iota(jnp.int32, (4, 64), 1) // 16
    row_half = lax.broadcasted_iota(jnp.int32, (8, 64), 0) < 4
    for c in range(2):
        for z in range(4):
            flags = sig_ref[c, z].astype(f32)
            wide = jnp.zeros((4, 64), f32)
            for t in range(4):
                wide = jnp.where(lane_tile == t, flags[:, t : t + 1], wide)
            tiles[c, z, 0:4] = wide
            each = [jnp.broadcast_to(tiles[c, z, t : t + 1], (8, 64)) for t in range(4)]
            for t in range(4):
                mask_y[c, z, 8 * t : 8 * t + 8] = each[t]
            for t in range(2):
                mask_x[c, z, 8 * t : 8 * t + 8] = jnp.where(row_half, each[2 * t], each[2 * t + 1])

    kept_x2 = x2_ref[...].astype(f32).reshape(2, 5, 4, 16, 64) * mask_x[...][:, None]
    kept_y2 = y2_ref[...].astype(f32).reshape(2, 5, 4, 32, 64) * mask_y[...][:, None]
    ext[...] = jnp.zeros_like(ext)
    ext[0:640, 0:32] = cx_ref[...].astype(f32)
    ext[640:1280, 0:32] = y1_ref[...].astype(f32)
    ext[1280:1920, 0:64] = kept_x2.reshape(640, 64)
    ext[1920:3200, 0:64] = kept_y2.reshape(1280, 64)

    def own(begin, end):
        return ext[begin:end, 0:64].astype(bf16)

    starts = (0, 640, 1280, 1920, 2560)
    cols = jnp.zeros((16, 640), f32)
    for which, begin in enumerate(starts):
        pick = small_ref[48 + 16 * which : 64 + 16 * which, 0:64]
        cols = cols + transposed(pick, own(begin, begin + 640))
    first_send[...] = cols.astype(bf16)
    last_send[...] = cols[8:16].astype(bf16)

    coarse_e = ext[0:320].reshape(40, 8, 128)
    x1_e = ext[320:640].reshape(40, 8, 128)
    y1_e = ext[640:1280].reshape(40, 16, 128)
    x2_e = ext[1280:1920].reshape(40, 16, 128)
    y2_e = ext[1920:3200].reshape(40, 32, 128)
    low = jnp.concatenate(
        [coarse_e[:, 6:8], x1_e[:, 7:8], y1_e[:, 14:16], x2_e[:, 15:16], y2_e[:, 30:32]], 1
    ).reshape(320, 128)
    high = jnp.concatenate(
        [coarse_e[:, 0:3], x1_e[:, 0:1], y1_e[:, 0:3], x2_e[:, 0:1]], 1
    ).reshape(320, 128)
    hy2[80:96] = jnp.zeros((16, 128), f32)
    for p in range(40):
        hy2[2 * p : 2 * p + 2] = ext[1920 + 32 * p : 1922 + 32 * p]
    more = hy2[0:48] + pltpu.roll(hy2[48:96], 64, 1)
    low_send[...] = (low[0:160] + pltpu.roll(low[160:320], 64, 1)).astype(bf16)
    high_send[0:160] = (high[0:160] + pltpu.roll(high[160:320], 64, 1)).astype(bf16)
    high_send[160:208] = more.astype(bf16)
    columns = jnp.zeros((32, 128), f32)
    for i in range(20):
        plane = adj_ref[i // 4, i % 4]
        columns = jnp.where(lane_wide // 4 == i, pltpu.roll(plane, 4 * i + 2, 1), columns)
        ax_rows[0, 2 * i : 2 * i + 2] = plane[0:2]
        ax_rows[1, 2 * i : 2 * i + 2] = plane[30:32]
    ax_rows[:, 40:48] = jnp.zeros((2, 8, 128), f32)
    ax_send[...] = ax_rows[...].astype(bf16)
    ay_send[...] = columns.astype(bf16)

    last_row = lax.broadcasted_iota(jnp.int32, (8, 128), 0) == 7
    for target, pieces, row in (
        (corner_low, (low, jnp.zeros((64, 128), f32)), columns[31:32]),
        (corner_high, (high, hy2[0:80], jnp.zeros((112, 128), f32)), columns[0:1]),
    ):
        rows = jnp.concatenate(pieces, 0)[:, 0:64].astype(bf16)
        picked = transposed(small_ref[128:144, 0:64], rows)[0:8]
        target[:, 0:128] = jnp.where(last_row, row, picked[:, 0:128]).astype(bf16)
        target[:, 128:] = picked[:, 128:].astype(bf16)

    pl.semaphore_wait(barrier, 9)
    corner_copies = [remote(4 + i, corner_low, corner_low_recv.at[i], diagonal[i]) for i in range(2)]
    corner_copies += [
        remote(6 + i, corner_high, corner_high_recv.at[i], diagonal[2 + i]) for i in range(2)
    ]
    column_copies = [remote(0, first_send, first_recv, y_down), remote(1, last_send, last_recv, y_up)]
    row_copies = [remote(2, low_send, low_recv, x_up), remote(3, high_send, high_recv, x_down)]
    adj_copies = [
        remote(8, ay_send, ay_recv.at[0], y_down),
        remote(9, ay_send, ay_recv.at[1], y_up),
        remote(10, ax_send.at[0], ax_recv.at[1], x_down),
        remote(11, ax_send.at[1], ax_recv.at[0], x_up),
    ]
    for copy in corner_copies + column_copies + adj_copies + row_copies:
        copy.start()

    loads[8].wait()
    for begin, count, role, target, at in (
        (0, 8, 0, mapped, 0),
        (320, 8, 0, mapped, 8),
        (640, 16, 1, mapped, 16),
        (1280, 16, 2, mapped, 32),
        (1920, 32, 3, mapped_y2, 0),
    ):
        product = jnp.dot(
            own(begin, begin + 40 * count),
            ay_ref[64 * role : 64 * role + 64],
            preferred_element_type=f32,
        )
        target[:, at : at + count] = product.reshape(40, count, 256)
    mapped_y2[:, 32:40] = jnp.zeros((40, 8, 256), f32)

    outer = 5 * gz
    z_side = 3 - 3 * gz
    blank = jnp.zeros((48, 128), f32)
    for t in range(2):
        for v in range(5):
            adj[t, v, outer] = blank
            mid[t, v, outer] = blank
        for cv in range(10):
            state[t, cv, outer] = blank
    for i in range(20):
        v, z = i // 4, i % 4
        adj[0, v, z + 1, 0:8] = blank[0:8]
        adj[0, v, z + 1, 40:48] = blank[0:8]
        adj[0, v, z + 1, 8:40] = adj_ref[v, z]
    rim[...] = blank

    for copy in adj_copies:
        copy.wait()
    ax_rows[...] = ax_recv[...].astype(f32)
    for i in range(20):
        v, z = i // 4, i % 4
        adj[0, v, z + 1, 6:8] = ax_rows[0, 2 * i : 2 * i + 2]
        adj[0, v, z + 1, 40:42] = ax_rows[1, 2 * i : 2 * i + 2]
    first = lane_wide % 4 >= 2
    rim[8:40] = jnp.where(first, ay_recv[0].astype(f32), ay_recv[1].astype(f32))
    near = (lane_full < 2) | (lane_full >= 126)

    def fill_rim(begin, end):
        part = rim[begin:end]
        for i in range(20):
            adj[1, i // 4, i % 4 + 1, begin:end] = jnp.where(
                near[begin:end], pltpu.roll(part, (126 - 4 * i) % 128, 1), 0.0
            )

    fill_rim(8, 40)

    for copy in column_copies:
        copy.wait()
    firsts, lasts = first_recv[...].astype(f32), last_recv[...].astype(f32)
    top = lax.broadcasted_iota(jnp.int32, (8, 640), 0) == 0
    joined = jnp.concatenate([firsts[0:8], jnp.where(top, firsts[8:16], lasts)], 0).T.astype(bf16)
    halo = [
        jnp.dot(joined, ay_ref[256 + 16 * i : 272 + 16 * i], preferred_element_type=f32)
        for i in range(5)
    ]
    mapped[:, 0:8] += halo[0][0:320].reshape(40, 8, 256)
    mapped[:, 8:16] += halo[0][320:640].reshape(40, 8, 256)
    mapped[:, 16:32] += halo[1].reshape(40, 16, 256)
    mapped[:, 32:48] += halo[2].reshape(40, 16, 256)
    mapped_y2[0:20, 0:32] += halo[3].reshape(20, 32, 256)
    mapped_y2[20:40, 0:32] += halo[4].reshape(20, 32, 256)

    for copy in row_copies:
        copy.wait()
    low_half, high_half = low_recv[...].astype(f32), high_recv[...].astype(f32)

    def unpacked(half, begin, end):
        part = half[begin:end]
        return jnp.concatenate([part[:, 0:64], part[:, 64:128]], 0)

    received = (
        (unpacked(low_half, 0, 160), ((0, 3), (3, 5), (5, 6), (6, 8))),
        (unpacked(high_half, 0, 160), ((0, 4), (4, 7), (7, 8), (8, 8))),
    )
    row_kind = lax.broadcasted_iota(jnp.int32, (320, 64), 0) % 8
    for (values, bounds), target in zip(received, (48, 56)):
        total = jnp.zeros((320, 256), f32)
        for role, (begin, end) in enumerate(bounds):
            if begin < end:
                part = jnp.where((row_kind >= begin) & (row_kind < end), values, 0.0)
                total = total + jnp.dot(
                    part.astype(bf16), ay_ref[64 * role : 64 * role + 64], preferred_element_type=f32
                )
        mapped[:, target : target + 8] = total.reshape(40, 8, 256)
    more = unpacked(high_half, 160, 208)[0:80].astype(bf16)
    beyond = jnp.dot(more, ay_ref[192:256], preferred_element_type=f32)

    def from_corners(parts, role_of):
        width = parts.shape[2]
        row = lax.broadcasted_iota(jnp.int32, (8, width), 0)
        corners = jnp.where(row < 3, parts[0].astype(f32), parts[1].astype(f32))
        role = role_of(lax.broadcasted_iota(jnp.int32, (8, width), 1))
        stacked = jnp.concatenate([jnp.where(role == r, corners, 0.0) for r in range(4)], 0)
        return jnp.dot(stacked.T.astype(bf16), ay_ref[336:368], preferred_element_type=f32)

    def low_role(place):
        kind = place % 8
        return jnp.where(kind < 3, 0, jnp.where(kind < 5, 1, jnp.where(kind < 6, 2, 3)))

    def high_role(place):
        kind = place % 8
        inner = jnp.where(kind < 4, 0, jnp.where(kind < 7, 1, 2))
        return jnp.where(place < 320, inner, 3)

    for copy in corner_copies:
        copy.wait()
    from_low = from_corners(corner_low_recv, low_role)
    from_high = from_corners(corner_high_recv, high_role)
    mapped[:, 48:56] += from_low[0:320].reshape(40, 8, 256)
    mapped[:, 56:64] += from_high[0:320].reshape(40, 8, 256)
    beyond = beyond + from_high[320:400]
    for p in range(40):
        mapped_y2[p, 32:34] = beyond[2 * p : 2 * p + 2]
    for parts, at in ((corner_low_recv, 7), (corner_high_recv, 40)):
        rows = [parts[i, :, 0:128].astype(f32)[7:8] for i in range(2)]
        rim[at : at + 1] = jnp.where(first[0:1], rows[0], rows[1])
    fill_rim(0, 8)
    fill_rim(40, 48)
    adj_z = remote(12, adj.at[:, :, z_side + 1], adj.at[:, :, outer], z_other)
    adj_z.start()

    def synthesize(order, cv, carry):
        for z in order:
            p = cv * 4 + z
            exact = mapped[p]
            coarse_bits = exact.astype(bf16)
            rest = (exact - coarse_bits.astype(f32)).astype(bf16)
            whole = jnp.dot(
                small_ref[0:48],
                jnp.concatenate([coarse_bits, rest], axis=0),
                preferred_element_type=f32,
            )
            extra = mapped_y2[p]
            for t in range(2):
                at = slice(128 * t, 128 * t + 128)
                state[t, cv, z + 1, 0:8] = whole[0:8, at]
                state[t, cv, z + 1, 8:48] = whole[8:48, at] + extra[:, at]
        return carry

    def synthesize_sides(pair, carry):
        for j in range(5):
            synthesize((z_side,), 5 * pair + j, carry)
        return carry

    for cv in range(10):
        synthesize((z_side,), cv, 0)
    state_first = remote(13, state.at[:, 0:5, z_side + 1], state.at[:, 0:5, outer], z_other)
    state_second = remote(
        14, state.at[0, 5:10, z_side + 1, 8:40], state.at[0, 5:10, outer, 8:40], z_other
    )
    state_first.start()
    state_second.start()
    def synthesize_rest(pair, carry):
        for j in range(5):
            synthesize((gz, gz + 1, gz + 2), 5 * pair + j, carry)
        return carry

    lax.fori_loop(0, 2, synthesize_rest, 0)
    adj_z.wait()
    state_first.wait()

    keep_bottom = jnp.where(gz > 0, 1.0, 0.0).astype(f32)

    def ahead(a, b):
        return pltpu.roll(jnp.where(lane == 0, b, a), 127, 1)

    def behind(a, b):
        return pltpu.roll(jnp.where(lane == 127, b, a), 1, 1)

    def x_face(t, base, source, z, r, start):
        low_at = slice(start + 8 * r, start + 8 + 8 * r)
        high_at = slice(start + 1 + 8 * r, start + 9 + 8 * r)
        mean = [
            (state[t, base + v, z + 1, low_at] + state[t, base + v, z + 1, high_at])
            for v in range(5)
        ]
        jump = [source[t, v, z + 1, high_at] - source[t, v, z + 1, low_at] for v in range(5)]
        terms = face(mean, jump, 0)
        for v in range(5):
            gx_terms[t, v, 8 * r : 8 * r + 8] = terms[v]

    def z_face(t, base, source, k, count, start):
        for r in range(count):
            at = slice(start + 8 * r, start + 8 + 8 * r)
            mean = [
                state[t, base + v, k, at] + state[t, base + v, k + 1, at] for v in range(5)
            ]
            jump = [source[t, v, k + 1, at] - source[t, v, k, at] for v in range(5)]
            terms = face(mean, jump, 2)
            factor = jnp.where(k == 0, keep_bottom, 1.0)
            for v in range(5):
                gz_terms[t, v, k, 8 * r : 8 * r + 8] = terms[v] * factor

    def first_z(k, carry):
        for t in range(2):
            z_face(t, 0, adj, k, 5, 7)
        return carry

    lax.fori_loop(0, 5, first_z, 0)
    mid_z = remote(15, mid.at[0, :, z_side + 1, 8:40], mid.at[0, :, outer, 8:40], z_other)

    def first_plane(j, carry):
        @pl.when(j == 1)
        def _():
            mid_z.start()

        z = jnp.where(gz > 0, j, 3 - j)
        for t in range(2):
            for r in range(5):
                x_face(t, 0, adj, z, r, 6)
        for r in range(5):
            at, rows = slice(7 + 8 * r, 15 + 8 * r), slice(8 * r, 8 * r + 8)
            here = [[state[t, v, z + 1, at] for v in range(5)] for t in range(2)]
            held = [[adj[t, v, z + 1, at] for v in range(5)] for t in range(2)]
            adj_up = [[ahead(held[t][v], held[1 - t][v]) for v in range(5)] for t in range(2)]
            up = [
                face(
                    [(here[t][v] + ahead(here[t][v], here[1 - t][v])) for v in range(5)],
                    [adj_up[t][v] - held[t][v] for v in range(5)],
                    1,
                )
                for t in range(2)
            ]
            for t in range(2):
                for v in range(5):
                    halves = (
                        up[t][v]
                        + behind(up[t][v], up[1 - t][v])
                        + gx_terms[t, v, rows]
                        + gx_terms[t, v, 8 * r + 1 : 8 * r + 9]
                        + gz_terms[t, v, z, rows]
                        + gz_terms[t, v, z + 1, rows]
                    )
                    around = (
                        adj_up[t][v]
                        + behind(held[t][v], held[1 - t][v])
                        + adj[t, v, z + 1, 6 + 8 * r : 14 + 8 * r]
                        + adj[t, v, z + 1, 8 + 8 * r : 16 + 8 * r]
                        + adj[t, v, z, at]
                        + adj[t, v, z + 2, at]
                    )
                    value = 0.5 * halves + viscosity * (around - 6.0 * held[t][v])
                    mid[t, v, z + 1, at] = held[t][v] + time_step * value
                    if t == 0:
                        partial[v, z, at] = held[t][v] + 0.5 * time_step * value
        return carry

    lax.fori_loop(0, 4, first_plane, 0)
    state_second.wait()

    def second_z(k, carry):
        z_face(0, 5, mid, k, 4, 8)
        return carry

    lax.fori_loop(gz, gz + 4, second_z, 0)

    def second_plane(j, carry):
        z = jnp.where(gz > 0, 3 - j, j)

        @pl.when(j == 3)
        def _():
            mid_z.wait()
            z_face(0, 5, mid, 4 - 4 * gz, 4, 8)

        for r in range(5):
            x_face(0, 5, mid, z, r, 7)
        for r in range(4):
            at, rows = slice(8 + 8 * r, 16 + 8 * r), slice(8 * r, 8 * r + 8)
            here = [state[0, 5 + v, z + 1, at] for v in range(5)]
            edge = [state[1, 5 + v, z + 1, at] for v in range(5)]
            held = [mid[0, v, z + 1, at] for v in range(5)]
            held_edge = [mid[1, v, z + 1, at] for v in range(5)]
            adj_up = [ahead(held[v], held_edge[v]) for v in range(5)]
            adj_down = [behind(held[v], held_edge[v]) for v in range(5)]
            up = face(
                [(here[v] + ahead(here[v], edge[v])) for v in range(5)],
                [adj_up[v] - held[v] for v in range(5)],
                1,
            )
            down = face(
                [(here[v] + behind(here[v], edge[v])) for v in range(5)],
                [held[v] - adj_down[v] for v in range(5)],
                1,
            )
            for v in range(5):
                halves = (
                    up[v]
                    + down[v]
                    + gx_terms[0, v, rows]
                    + gx_terms[0, v, 8 * r + 1 : 8 * r + 9]
                    + gz_terms[0, v, z, rows]
                    + gz_terms[0, v, z + 1, rows]
                )
                around = (
                    adj_up[v]
                    + adj_down[v]
                    + mid[0, v, z + 1, 7 + 8 * r : 15 + 8 * r]
                    + mid[0, v, z + 1, 9 + 8 * r : 17 + 8 * r]
                    + mid[0, v, z, at]
                    + mid[0, v, z + 2, at]
                )
                value = 0.5 * halves + viscosity * (around - 6.0 * held[v])
                result[v, z, rows] = partial[v, z, at] + 0.5 * time_step * value
        return carry

    lax.fori_loop(0, 4, second_plane, 0)


def shards(coarse, detail_x1, detail_y1, detail_x2, detail_y2, significance, adjoint):
    operands = [
        pltpu.with_memory_space_constraint(value, pltpu.HBM)
        for value in (
            coarse.reshape(320, 32),
            detail_x1.reshape(320, 32),
            detail_y1.reshape(640, 32),
            detail_x2.reshape(640, 64),
            detail_y2.reshape(1280, 64),
            significance,
            adjoint,
            jnp.asarray(y_matrices()),
            jnp.asarray(small_matrices()),
        )
    ]
    anywhere = pl.BlockSpec(memory_space=pl.ANY)
    return pl.pallas_call(
        kernel,
        out_shape=jax.ShapeDtypeStruct(adjoint.shape, f32),
        in_specs=[anywhere] * 9,
        out_specs=pl.BlockSpec(memory_space=pltpu.VMEM),
        scratch_shapes=[
            pltpu.VMEM((640, 32), bf16),
            pltpu.VMEM((640, 32), bf16),
            pltpu.VMEM((640, 64), bf16),
            pltpu.VMEM((1280, 64), bf16),
            pltpu.VMEM((2, 4, 4, 4), jnp.int32),
            pltpu.VMEM((5, 4, 32, 128), f32),
            pltpu.VMEM((368, 256), bf16),
            pltpu.VMEM((144, 128), bf16),
            pltpu.VMEM((5, 4, 48, 128), f32),
            pltpu.SemaphoreType.DMA((9,)),
            pltpu.VMEM((2, 4, 8, 64), f32),
            pltpu.VMEM((2, 4, 16, 64), f32),
            pltpu.VMEM((2, 4, 32, 64), f32),
            pltpu.VMEM((3200, 128), f32),
            pltpu.VMEM((96, 128), f32),
            pltpu.VMEM((16, 640), bf16),
            pltpu.VMEM((16, 640), bf16),
            pltpu.VMEM((8, 640), bf16),
            pltpu.VMEM((8, 640), bf16),
            pltpu.VMEM((160, 128), bf16),
            pltpu.VMEM((160, 128), bf16),
            pltpu.VMEM((208, 128), bf16),
            pltpu.VMEM((208, 128), bf16),
            pltpu.VMEM((8, 384), bf16),
            pltpu.VMEM((2, 8, 384), bf16),
            pltpu.VMEM((8, 512), bf16),
            pltpu.VMEM((2, 8, 512), bf16),
            pltpu.VMEM((2, 48, 128), f32),
            pltpu.VMEM((2, 48, 128), bf16),
            pltpu.VMEM((2, 48, 128), bf16),
            pltpu.VMEM((32, 128), bf16),
            pltpu.VMEM((2, 32, 128), bf16),
            pltpu.VMEM((48, 128), f32),
            pltpu.VMEM((40, 64, 256), f32),
            pltpu.VMEM((40, 40, 256), f32),
            pltpu.VMEM((2, 10, 6, 48, 128), f32),
            pltpu.VMEM((2, 5, 6, 48, 128), f32),
            pltpu.VMEM((2, 5, 6, 48, 128), f32),
            pltpu.VMEM((2, 5, 48, 128), f32),
            pltpu.VMEM((2, 5, 5, 40, 128), f32),
            pltpu.SemaphoreType.DMA((16,)),
            pltpu.SemaphoreType.DMA((16,)),
        ],
        compiler_params=pltpu.CompilerParams(collective_id=0, has_side_effects=True, vmem_limit_bytes=40*2**20),
    )(
        *operands,
    )


def solution(mesh):
    return jax.shard_map(
        shards,
        mesh=mesh,
        in_specs=(
            P(None, None, "gz", "gx", "gy"),
            P(None, None, "gz", "gx", "gy"),
            P(None, None, "gz", "gx", "gy"),
            P(None, None, "gz", "gx", "gy"),
            P(None, None, "gz", "gx", "gy"),
            P(None, "gz", "gx", "gy"),
            P(None, "gz", "gx", "gy"),
        ),
        out_specs=P(None, "gz", "gx", "gy"),
        check_vma=False,
    )
```

```python
import functools

import jax
import jax.numpy as jnp
import ml_dtypes
import numpy as np
from jax import lax
from jax.experimental import pallas as pl
from jax.experimental.pallas import tpu as pltpu
from jax.sharding import PartitionSpec as P

time_step = 0.1
viscosity = 0.2
heat_ratio_less_one = 0.4
f32 = jnp.float32
bf16 = jnp.bfloat16
MESH = pl.DeviceIdType.MESH


def predict(index):
    k = index // 2
    if index % 2 == 0:
        return {("c", k): 1.0}
    return {
        ("d", k): 1.0,
        ("c", k): 9 / 16,
        ("c", k + 1): 9 / 16,
        ("c", k - 1): -1 / 16,
        ("c", k + 2): -1 / 16,
    }


def predict_twice(index):
    whole = {}
    for (kind, k), weight in predict(index).items():
        if kind == "d":
            whole[("e", k)] = weight
            continue
        whole[("m", k)] = weight
        for key, inner in predict(k).items():
            whole[key] = whole.get(key, 0.0) + weight * inner
    return whole


def halo_row(kind, k):
    if kind == "c":
        return k - 32 if k >= 32 else 11 + k
    if kind == "d":
        return 3 if k >= 32 else 11
    if kind == "m":
        return 4 + k - 64 if k >= 64 else 14 + k
    return 7 if k >= 64 else 14


def y_matrices():
    own = np.zeros((4, 64, 256), np.float32)
    halo = np.zeros((5, 16, 256), np.float32)
    corner = np.zeros((4, 8, 256), np.float32)
    columns = [(y, y) for y in range(128)] + [(128, 128), (129, 129), (-1, 255), (-2, 254)]
    for y, column in columns:
        for (kind, k), weight in predict_twice(y).items():
            role = "cdme".index(kind)
            length = 32 if role < 2 else 64
            if 0 <= k < length:
                own[role, k, column] += weight
                continue
            row = halo_row(kind, k)
            halo[role, row, column] += weight
            if kind == "e":
                halo[4, row + 1, column] += weight
            if k >= length:
                corner[role, k - length, column] += weight
            else:
                corner[role, (5 if length == 32 else 7) + k, column] += weight
    parts = [own.reshape(256, 256), halo.reshape(80, 256), corner.reshape(32, 256)]
    return (0.5 * np.concatenate(parts)).astype(ml_dtypes.bfloat16)


def small_matrices():
    mats = np.zeros((144, 128), np.float32)
    for x in range(-2, 34):
        row = x + 8
        for (kind, k), weight in predict_twice(x).items():
            if kind == "c":
                at = 50 + k if k < 0 else (k if k < 8 else 56 + k - 8)
            elif kind == "d":
                at = 50 if k < 0 else (8 + k if k < 8 else 59)
            elif kind == "m":
                at = 53 + k if k < 0 else (16 + k if k < 16 else 60 + k - 16)
            else:
                at = 53 if k < 0 else (32 + k if k < 16 else 63)
            mats[row, at] += weight
    mats[6, 54] = 1.0
    mats[7, 55] = 1.0
    mats[0:48, 64:128] = mats[0:48, 0:64]
    picks = mats[48:128].reshape(5, 16, 128)
    for row, column in ((0, 0), (1, 1), (2, 2), (9, 30), (10, 31)):
        picks[0, row, column] = 1.0
    for row, column in ((3, 0), (11, 31)):
        picks[1, row, column] = 1.0
    for row, column in ((4, 0), (5, 1), (6, 2), (12, 62), (13, 63)):
        picks[2, row, column] = 1.0
    for row, column in ((7, 0), (14, 63)):
        picks[3, row, column] = 1.0
        picks[4, row + 1, column] = 1.0
    for row, column in ((0, 0), (1, 1), (2, 2), (3, 30), (4, 31), (5, 62), (6, 63)):
        mats[128 + row, column] = 1.0
    return mats.astype(ml_dtypes.bfloat16)


def face(mean, jump, k, factor=None):
    q, u, t = mean[0], mean[1:4], mean[4]
    rho = (0.5 * time_step) * jnp.exp(0.5 * q)
    if factor is not None:
        rho = rho * factor
    speed = u[k]
    half_square = 0.5 * (u[0] * u[0] + u[1] * u[1] + u[2] * u[2])
    enthalpy = (1.0 / heat_ratio_less_one + 1.0) * t + half_square
    inner = jump[0] + jump[1] * u[0] + jump[2] * u[1] + jump[3] * u[2] + jump[4] * enthalpy
    flow = rho * speed
    push = rho * jump[1 + k]
    grads = [flow * (jump[1 + j] + jump[4] * u[j]) for j in range(3)]
    grads[k] = grads[k] + rho * inner
    dq = 0.5 * (flow * inner + t * push)
    dt = push + (1.0 / heat_ratio_less_one + 1.0) * (flow * jump[4])
    terms = [dq] + grads + [dt]
    spread = [(viscosity * time_step) * jump[v] for v in range(5)]
    return [terms[v] + spread[v] for v in range(5)], [terms[v] - spread[v] for v in range(5)]


def kernel(
    c_in, x1_in, y1_in, x2_in, y2_in, sig_in, adj_in, ay_in, small_in,
    result,
    cx_ref, y1_ref, x2_ref, y2_ref, sig_ref, adj_ref, ay_ref, small_ref,
    load_sem,
    tiles, mask_x, mask_y, ext, hy2,
    first_send, first_recv, last_send, last_recv, low_send, low_recv, high_send, high_recv,
    corner_low, corner_low_recv, corner_high, corner_high_recv,
    ax_rows, ax_send, ax_recv, ay_send, ay_recv, rim,
    mapped, mapped_y2, state, adj, mid, gx_terms, gz_terms,
    send_sem, recv_sem,
):
    gx, gy, gz = lax.axis_index("gx"), lax.axis_index("gy"), lax.axis_index("gz")
    nx, ny = lax.axis_size("gx"), lax.axis_size("gy")
    up_x, down_x = lax.rem(gx + 1, nx), lax.rem(gx + nx - 1, nx)
    up_y, down_y = lax.rem(gy + 1, ny), lax.rem(gy + ny - 1, ny)
    x_up, x_down = {"gx": up_x}, {"gx": down_x}
    y_up, y_down = {"gy": up_y}, {"gy": down_y}
    diagonal = (
        {"gx": up_x, "gy": down_y},
        {"gx": up_x, "gy": up_y},
        {"gx": down_x, "gy": down_y},
        {"gx": down_x, "gy": up_y},
    )
    z_other = {"gz": 1 - gz}
    barrier = pltpu.get_barrier_semaphore()
    for peer in (x_up, x_down, y_up, y_down, z_other) + diagonal:
        pl.semaphore_signal(barrier, inc=1, device_id=peer, device_id_type=MESH)

    pairs = (
        (sig_in, sig_ref), (x2_in, x2_ref), (y2_in, y2_ref), (c_in, cx_ref.at[0:320]),
        (x1_in, cx_ref.at[320:640]), (y1_in, y1_ref), (small_in, small_ref), (adj_in, adj_ref),
        (ay_in, ay_ref),
    )
    loads = [
        pltpu.make_async_copy(source, target, load_sem.at[i])
        for i, (source, target) in enumerate(pairs)
    ]
    for load in loads:
        load.start()

    def remote(index, source, target, peer):
        return pltpu.make_async_remote_copy(
            src_ref=source,
            dst_ref=target,
            send_sem=send_sem.at[index],
            recv_sem=recv_sem.at[index],
            device_id=peer,
            device_id_type=MESH,
        )

    def transposed(left, right):
        return lax.dot_general(left, right, (((1,), (1,)), ((), ())), preferred_element_type=f32)

    lane = lax.broadcasted_iota(jnp.int32, (8, 128), 1)
    lane_wide = lax.broadcasted_iota(jnp.int32, (32, 128), 1)
    lane_full = lax.broadcasted_iota(jnp.int32, (48, 128), 1)

    for load in loads[:8]:
        load.wait()
    lane_tile = lax.broadcasted_iota(jnp.int32, (4, 64), 1) // 16
    row_half = lax.broadcasted_iota(jnp.int32, (8, 64), 0) < 4
    for c in range(2):
        for z in range(4):
            flags = sig_ref[c, z].astype(f32)
            wide = jnp.zeros((4, 64), f32)
            for t in range(4):
                wide = jnp.where(lane_tile == t, flags[:, t : t + 1], wide)
            tiles[c, z, 0:4] = wide
            each = [jnp.broadcast_to(tiles[c, z, t : t + 1], (8, 64)) for t in range(4)]
            for t in range(4):
                mask_y[c, z, 8 * t : 8 * t + 8] = each[t]
            for t in range(2):
                mask_x[c, z, 8 * t : 8 * t + 8] = jnp.where(row_half, each[2 * t], each[2 * t + 1])

    kept_x2 = x2_ref[...].astype(f32).reshape(2, 5, 4, 16, 64) * mask_x[...][:, None]
    kept_y2 = y2_ref[...].astype(f32).reshape(2, 5, 4, 32, 64) * mask_y[...][:, None]
    ext[...] = jnp.zeros_like(ext)
    ext[0:640, 0:32] = cx_ref[...].astype(f32)
    ext[640:1280, 0:32] = y1_ref[...].astype(f32)
    ext[1280:1920, 0:64] = kept_x2.reshape(640, 64)
    ext[1920:3200, 0:64] = kept_y2.reshape(1280, 64)

    def own(begin, end):
        return ext[begin:end, 0:64].astype(bf16)

    starts = (0, 640, 1280, 1920, 2560)
    cols = jnp.zeros((16, 640), f32)
    for which, begin in enumerate(starts):
        pick = small_ref[48 + 16 * which : 64 + 16 * which, 0:64]
        cols = cols + transposed(pick, own(begin, begin + 640))
    first_send[...] = cols.astype(bf16)
    last_send[...] = cols[8:16].astype(bf16)

    coarse_e = ext[0:320].reshape(40, 8, 128)
    x1_e = ext[320:640].reshape(40, 8, 128)
    y1_e = ext[640:1280].reshape(40, 16, 128)
    x2_e = ext[1280:1920].reshape(40, 16, 128)
    y2_e = ext[1920:3200].reshape(40, 32, 128)
    low = jnp.concatenate(
        [coarse_e[:, 6:8], x1_e[:, 7:8], y1_e[:, 14:16], x2_e[:, 15:16], y2_e[:, 30:32]], 1
    ).reshape(320, 128)
    high = jnp.concatenate(
        [coarse_e[:, 0:3], x1_e[:, 0:1], y1_e[:, 0:3], x2_e[:, 0:1]], 1
    ).reshape(320, 128)
    hy2[80:96] = jnp.zeros((16, 128), f32)
    for p in range(40):
        hy2[2 * p : 2 * p + 2] = ext[1920 + 32 * p : 1922 + 32 * p]
    more = hy2[0:48] + pltpu.roll(hy2[48:96], 64, 1)
    low_send[...] = (low[0:160] + pltpu.roll(low[160:320], 64, 1)).astype(bf16)
    high_send[0:160] = (high[0:160] + pltpu.roll(high[160:320], 64, 1)).astype(bf16)
    high_send[160:208] = more.astype(bf16)
    columns = jnp.zeros((32, 128), f32)
    for i in range(20):
        plane = adj_ref[i // 4, i % 4]
        columns = jnp.where(lane_wide // 4 == i, pltpu.roll(plane, 4 * i + 2, 1), columns)
        ax_rows[0, 2 * i : 2 * i + 2] = plane[0:2]
        ax_rows[1, 2 * i : 2 * i + 2] = plane[30:32]
    ax_rows[:, 40:48] = jnp.zeros((2, 8, 128), f32)
    ax_send[...] = ax_rows[...].astype(bf16)
    ay_send[...] = columns.astype(bf16)

    last_row = lax.broadcasted_iota(jnp.int32, (8, 128), 0) == 7
    for target, pieces, row in (
        (corner_low, (low, jnp.zeros((64, 128), f32)), columns[31:32]),
        (corner_high, (high, hy2[0:80], jnp.zeros((112, 128), f32)), columns[0:1]),
    ):
        rows = jnp.concatenate(pieces, 0)[:, 0:64].astype(bf16)
        picked = transposed(small_ref[128:144, 0:64], rows)[0:8]
        target[:, 0:128] = jnp.where(last_row, row, picked[:, 0:128]).astype(bf16)
        target[:, 128:] = picked[:, 128:].astype(bf16)

    pl.semaphore_wait(barrier, 9)
    corner_copies = [remote(4 + i, corner_low, corner_low_recv.at[i], diagonal[i]) for i in range(2)]
    corner_copies += [
        remote(6 + i, corner_high, corner_high_recv.at[i], diagonal[2 + i]) for i in range(2)
    ]
    column_copies = [remote(0, first_send, first_recv, y_down), remote(1, last_send, last_recv, y_up)]
    row_copies = [remote(2, low_send, low_recv, x_up), remote(3, high_send, high_recv, x_down)]
    adj_copies = [
        remote(8, ay_send, ay_recv.at[0], y_down),
        remote(9, ay_send, ay_recv.at[1], y_up),
        remote(10, ax_send.at[0], ax_recv.at[1], x_down),
        remote(11, ax_send.at[1], ax_recv.at[0], x_up),
    ]
    for copy in corner_copies + column_copies + adj_copies + row_copies:
        copy.start()

    loads[8].wait()
    for begin, count, role, target, at in (
        (0, 8, 0, mapped, 0),
        (320, 8, 0, mapped, 8),
        (640, 16, 1, mapped, 16),
        (1280, 16, 2, mapped, 32),
        (1920, 32, 3, mapped_y2, 0),
    ):
        product = jnp.dot(
            own(begin, begin + 40 * count),
            ay_ref[64 * role : 64 * role + 64],
            preferred_element_type=f32,
        )
        target[:, at : at + count] = product.reshape(40, count, 256)
    mapped_y2[:, 32:40] = jnp.zeros((40, 8, 256), f32)

    outer = 5 * gz
    z_side = 3 - 3 * gz
    blank = jnp.zeros((48, 128), f32)
    for t in range(2):
        for v in range(5):
            adj[t, v, outer] = blank
            mid[t, v, outer] = blank
        for cv in range(10):
            state[t, cv, outer] = blank
    for i in range(20):
        v, z = i // 4, i % 4
        adj[0, v, z + 1, 0:8] = blank[0:8]
        adj[0, v, z + 1, 40:48] = blank[0:8]
        adj[0, v, z + 1, 8:40] = adj_ref[v, z]
    rim[...] = blank

    for copy in adj_copies:
        copy.wait()
    ax_rows[...] = ax_recv[...].astype(f32)
    for i in range(20):
        v, z = i // 4, i % 4
        adj[0, v, z + 1, 6:8] = ax_rows[0, 2 * i : 2 * i + 2]
        adj[0, v, z + 1, 40:42] = ax_rows[1, 2 * i : 2 * i + 2]
    first = lane_wide % 4 >= 2
    rim[8:40] = jnp.where(first, ay_recv[0].astype(f32), ay_recv[1].astype(f32))
    near = (lane_full < 2) | (lane_full >= 126)

    def fill_rim(begin, end):
        part = rim[begin:end]
        for i in range(20):
            adj[1, i // 4, i % 4 + 1, begin:end] = jnp.where(
                near[begin:end], pltpu.roll(part, (126 - 4 * i) % 128, 1), 0.0
            )

    fill_rim(8, 40)

    for copy in column_copies:
        copy.wait()
    firsts, lasts = first_recv[...].astype(f32), last_recv[...].astype(f32)
    top = lax.broadcasted_iota(jnp.int32, (8, 640), 0) == 0
    joined = jnp.concatenate([firsts[0:8], jnp.where(top, firsts[8:16], lasts)], 0).T.astype(bf16)
    halo = [
        jnp.dot(joined, ay_ref[256 + 16 * i : 272 + 16 * i], preferred_element_type=f32)
        for i in range(5)
    ]
    mapped[:, 0:8] += halo[0][0:320].reshape(40, 8, 256)
    mapped[:, 8:16] += halo[0][320:640].reshape(40, 8, 256)
    mapped[:, 16:32] += halo[1].reshape(40, 16, 256)
    mapped[:, 32:48] += halo[2].reshape(40, 16, 256)
    mapped_y2[0:20, 0:32] += halo[3].reshape(20, 32, 256)
    mapped_y2[20:40, 0:32] += halo[4].reshape(20, 32, 256)

    for copy in row_copies:
        copy.wait()
    low_half, high_half = low_recv[...].astype(f32), high_recv[...].astype(f32)

    upper = lax.broadcasted_iota(jnp.int32, (320, 128), 1) >= 64
    row_kind = lax.broadcasted_iota(jnp.int32, (320, 128), 0) % 8

    def doubled(half):
        turned = pltpu.roll(half, 64, 1)
        left = upper[0 : half.shape[0]]
        return jnp.concatenate([jnp.where(left, turned, half), jnp.where(left, half, turned)], 0)

    for half, bounds, target in (
        (low_half, (3, 5, 6), 48),
        (high_half[0:160], (4, 7, 8), 56),
    ):
        values = doubled(half)
        role = jnp.where(
            row_kind < bounds[0], 0, jnp.where(row_kind < bounds[1], 1, jnp.where(row_kind < bounds[2], 2, 3))
        )
        spot = jnp.where(upper, 1, 0)
        parts = [jnp.where(role == spot + 2 * i, values, 0.0) for i in range(2)]
        total = jnp.dot(
            jnp.concatenate(parts, 1).astype(bf16), ay_ref[0:256], preferred_element_type=f32
        )
        mapped[:, target : target + 8] = total.reshape(40, 8, 256)
    more = doubled(high_half[160:208])[0:80, 0:64].astype(bf16)
    beyond = jnp.dot(more, ay_ref[192:256], preferred_element_type=f32)

    def from_corners(parts, role_of):
        width = parts.shape[2]
        row = lax.broadcasted_iota(jnp.int32, (8, width), 0)
        corners = jnp.where(row < 3, parts[0].astype(f32), parts[1].astype(f32))
        role = role_of(lax.broadcasted_iota(jnp.int32, (8, width), 1))
        stacked = jnp.concatenate([jnp.where(role == r, corners, 0.0) for r in range(4)], 0)
        return jnp.dot(stacked.T.astype(bf16), ay_ref[336:368], preferred_element_type=f32)

    def low_role(place):
        kind = place % 8
        return jnp.where(kind < 3, 0, jnp.where(kind < 5, 1, jnp.where(kind < 6, 2, 3)))

    def high_role(place):
        kind = place % 8
        inner = jnp.where(kind < 4, 0, jnp.where(kind < 7, 1, 2))
        return jnp.where(place < 320, inner, 3)

    for copy in corner_copies:
        copy.wait()
    from_low = from_corners(corner_low_recv, low_role)
    from_high = from_corners(corner_high_recv, high_role)
    mapped[:, 48:56] += from_low[0:320].reshape(40, 8, 256)
    mapped[:, 56:64] += from_high[0:320].reshape(40, 8, 256)
    beyond = beyond + from_high[320:400]
    for p in range(40):
        mapped_y2[p, 32:34] = beyond[2 * p : 2 * p + 2]
    for parts, at in ((corner_low_recv, 7), (corner_high_recv, 40)):
        rows = [parts[i, :, 0:128].astype(f32)[7:8] for i in range(2)]
        rim[at : at + 1] = jnp.where(first[0:1], rows[0], rows[1])
    fill_rim(0, 8)
    fill_rim(40, 48)
    adj_z = remote(12, adj.at[:, :, z_side + 1], adj.at[:, :, outer], z_other)
    adj_z.start()

    def synthesize(order, cv, carry):
        for z in order:
            p = cv * 4 + z
            exact = mapped[p]
            coarse_bits = exact.astype(bf16)
            rest = (exact - coarse_bits.astype(f32)).astype(bf16)
            whole = jnp.dot(
                small_ref[0:48],
                jnp.concatenate([coarse_bits, rest], axis=0),
                preferred_element_type=f32,
            )
            extra = mapped_y2[p]
            for t in range(2):
                at = slice(128 * t, 128 * t + 128)
                state[t, cv, z + 1, 0:8] = whole[0:8, at]
                state[t, cv, z + 1, 8:48] = whole[8:48, at] + extra[:, at]
        return carry

    def synthesize_sides(pair, carry):
        for j in range(5):
            synthesize((z_side,), 5 * pair + j, carry)
        return carry

    for cv in range(10):
        synthesize((z_side,), cv, 0)
    state_first = remote(13, state.at[:, 0:5, z_side + 1], state.at[:, 0:5, outer], z_other)
    state_second = remote(
        14, state.at[0, 5:10, z_side + 1, 8:40], state.at[0, 5:10, outer, 8:40], z_other
    )
    state_first.start()
    state_second.start()
    def synthesize_rest(pair, carry):
        for j in range(5):
            synthesize((gz, gz + 1, gz + 2), 5 * pair + j, carry)
        return carry

    lax.fori_loop(0, 2, synthesize_rest, 0)
    adj_z.wait()
    state_first.wait()

    keep_bottom = jnp.where(gz > 0, 1.0, 0.0).astype(f32)

    def ahead(a, b):
        return pltpu.roll(jnp.where(lane == 0, b, a), 127, 1)

    def behind(a, b):
        return pltpu.roll(jnp.where(lane == 127, b, a), 1, 1)

    def x_face(t, base, source, z, r, start):
        low_at = slice(start + 8 * r, start + 8 + 8 * r)
        high_at = slice(start + 1 + 8 * r, start + 9 + 8 * r)
        mean = [
            (state[t, base + v, z + 1, low_at] + state[t, base + v, z + 1, high_at])
            for v in range(5)
        ]
        jump = [source[t, v, z + 1, high_at] - source[t, v, z + 1, low_at] for v in range(5)]
        below, above = face(mean, jump, 0)
        for v in range(5):
            gx_terms[0, t, v, 8 * r : 8 * r + 8] = below[v]
            gx_terms[1, t, v, 8 * r : 8 * r + 8] = above[v]

    def z_face(t, base, source, k, count, start):
        for r in range(count):
            at = slice(start + 8 * r, start + 8 + 8 * r)
            mean = [
                state[t, base + v, k, at] + state[t, base + v, k + 1, at] for v in range(5)
            ]
            jump = [source[t, v, k + 1, at] - source[t, v, k, at] for v in range(5)]
            below, above = face(mean, jump, 2, jnp.where(k == 0, keep_bottom, 1.0))
            for v in range(5):
                gz_terms[0, t, v, k, 8 * r : 8 * r + 8] = below[v]
                gz_terms[1, t, v, k, 8 * r : 8 * r + 8] = above[v]

    def first_z(k, carry):
        for t in range(2):
            z_face(t, 0, adj, k, 5, 7)
        return carry

    lax.fori_loop(0, 5, first_z, 0)
    mid_z = remote(15, mid.at[0, :, z_side + 1, 8:40], mid.at[0, :, outer, 8:40], z_other)

    def first_plane(j, carry):
        @pl.when(j == 1)
        def _():
            mid_z.start()

        z = jnp.where(gz > 0, j, 3 - j)
        for r in range(5):
            for t in range(2):
                x_face(t, 0, adj, z, r, 6)
        for r in range(5):
            at, rows = slice(7 + 8 * r, 15 + 8 * r), slice(8 * r, 8 * r + 8)
            here = [[state[t, v, z + 1, at] for v in range(5)] for t in range(2)]
            held = [[adj[t, v, z + 1, at] for v in range(5)] for t in range(2)]
            below, above = [None] * 2, [None] * 2
            for t in range(2):
                jump = [ahead(held[t][v], held[1 - t][v]) - held[t][v] for v in range(5)]
                mean = [here[t][v] + ahead(here[t][v], here[1 - t][v]) for v in range(5)]
                below[t], above[t] = face(mean, jump, 1)
            for t in range(2):
                for v in range(5):
                    mid[t, v, z + 1, at] = (
                        held[t][v]
                        + below[t][v]
                        + behind(above[t][v], above[1 - t][v])
                        + gx_terms[0, t, v, 8 * r + 1 : 8 * r + 9]
                        + gx_terms[1, t, v, rows]
                        + gz_terms[0, t, v, z + 1, rows]
                        + gz_terms[1, t, v, z, rows]
                    )
        return carry

    lax.fori_loop(0, 4, first_plane, 0)
    state_second.wait()

    def second_z(k, carry):
        z_face(0, 5, mid, k, 4, 8)
        return carry

    lax.fori_loop(gz, gz + 4, second_z, 0)

    def second_plane(j, carry):
        z = jnp.where(gz > 0, 3 - j, j)

        @pl.when(j == 3)
        def _():
            mid_z.wait()
            z_face(0, 5, mid, 4 - 4 * gz, 4, 8)

        for r in range(5):
            x_face(0, 5, mid, z, r, 7)
        for r in range(4):
            at, rows = slice(8 + 8 * r, 16 + 8 * r), slice(8 * r, 8 * r + 8)
            here = [state[0, 5 + v, z + 1, at] for v in range(5)]
            edge = [state[1, 5 + v, z + 1, at] for v in range(5)]
            held = [mid[0, v, z + 1, at] for v in range(5)]
            held_edge = [mid[1, v, z + 1, at] for v in range(5)]
            adj_up = [ahead(held[v], held_edge[v]) for v in range(5)]
            adj_down = [behind(held[v], held_edge[v]) for v in range(5)]
            below, _ = face(
                [here[v] + ahead(here[v], edge[v]) for v in range(5)],
                [adj_up[v] - held[v] for v in range(5)],
                1,
            )
            _, above = face(
                [here[v] + behind(here[v], edge[v]) for v in range(5)],
                [held[v] - adj_down[v] for v in range(5)],
                1,
            )
            for v in range(5):
                result[v, z, rows] = 0.5 * (
                    adj[0, v, z + 1, at]
                    + held[v]
                    + below[v]
                    + above[v]
                    + gx_terms[0, 0, v, 8 * r + 1 : 8 * r + 9]
                    + gx_terms[1, 0, v, rows]
                    + gz_terms[0, 0, v, z + 1, rows]
                    + gz_terms[1, 0, v, z, rows]
                )
        return carry

    lax.fori_loop(0, 4, second_plane, 0)


def shards(coarse, detail_x1, detail_y1, detail_x2, detail_y2, significance, adjoint):
    operands = [
        pltpu.with_memory_space_constraint(value, pltpu.HBM)
        for value in (
            coarse.reshape(320, 32),
            detail_x1.reshape(320, 32),
            detail_y1.reshape(640, 32),
            detail_x2.reshape(640, 64),
            detail_y2.reshape(1280, 64),
            significance,
            adjoint,
            jnp.asarray(y_matrices()),
            jnp.asarray(small_matrices()),
        )
    ]
    anywhere = pl.BlockSpec(memory_space=pl.ANY)
    return pl.pallas_call(
        kernel,
        out_shape=jax.ShapeDtypeStruct(adjoint.shape, f32),
        in_specs=[anywhere] * 9,
        out_specs=pl.BlockSpec(memory_space=pltpu.VMEM),
        scratch_shapes=[
            pltpu.VMEM((640, 32), bf16),
            pltpu.VMEM((640, 32), bf16),
            pltpu.VMEM((640, 64), bf16),
            pltpu.VMEM((1280, 64), bf16),
            pltpu.VMEM((2, 4, 4, 4), jnp.int32),
            pltpu.VMEM((5, 4, 32, 128), f32),
            pltpu.VMEM((368, 256), bf16),
            pltpu.VMEM((144, 128), bf16),
            pltpu.SemaphoreType.DMA((9,)),
            pltpu.VMEM((2, 4, 8, 64), f32),
            pltpu.VMEM((2, 4, 16, 64), f32),
            pltpu.VMEM((2, 4, 32, 64), f32),
            pltpu.VMEM((3200, 128), f32),
            pltpu.VMEM((96, 128), f32),
            pltpu.VMEM((16, 640), bf16),
            pltpu.VMEM((16, 640), bf16),
            pltpu.VMEM((8, 640), bf16),
            pltpu.VMEM((8, 640), bf16),
            pltpu.VMEM((160, 128), bf16),
            pltpu.VMEM((160, 128), bf16),
            pltpu.VMEM((208, 128), bf16),
            pltpu.VMEM((208, 128), bf16),
            pltpu.VMEM((8, 384), bf16),
            pltpu.VMEM((2, 8, 384), bf16),
            pltpu.VMEM((8, 512), bf16),
            pltpu.VMEM((2, 8, 512), bf16),
            pltpu.VMEM((2, 48, 128), f32),
            pltpu.VMEM((2, 48, 128), bf16),
            pltpu.VMEM((2, 48, 128), bf16),
            pltpu.VMEM((32, 128), bf16),
            pltpu.VMEM((2, 32, 128), bf16),
            pltpu.VMEM((48, 128), f32),
            pltpu.VMEM((40, 64, 256), f32),
            pltpu.VMEM((40, 40, 256), f32),
            pltpu.VMEM((2, 10, 6, 48, 128), f32),
            pltpu.VMEM((2, 5, 6, 48, 128), f32),
            pltpu.VMEM((2, 5, 6, 48, 128), f32),
            pltpu.VMEM((2, 2, 5, 48, 128), f32),
            pltpu.VMEM((2, 2, 5, 5, 40, 128), f32),
            pltpu.SemaphoreType.DMA((16,)),
            pltpu.SemaphoreType.DMA((16,)),
        ],
        compiler_params=pltpu.CompilerParams(collective_id=0, has_side_effects=True, vmem_limit_bytes=40*2**20),
    )(
        *operands,
    )


def solution(mesh):
    return jax.shard_map(
        shards,
        mesh=mesh,
        in_specs=(
            P(None, None, "gz", "gx", "gy"),
            P(None, None, "gz", "gx", "gy"),
            P(None, None, "gz", "gx", "gy"),
            P(None, None, "gz", "gx", "gy"),
            P(None, None, "gz", "gx", "gy"),
            P(None, "gz", "gx", "gy"),
            P(None, "gz", "gx", "gy"),
        ),
        out_specs=P(None, "gz", "gx", "gy"),
        check_vma=False,
    )
```

```python
import functools

import jax
import jax.numpy as jnp
import ml_dtypes
import numpy as np
from jax import lax
from jax.experimental import pallas as pl
from jax.experimental.pallas import tpu as pltpu
from jax.sharding import PartitionSpec as P

time_step = 0.1
viscosity = 0.2
heat_ratio_less_one = 0.4
f32 = jnp.float32
bf16 = jnp.bfloat16
MESH = pl.DeviceIdType.MESH


def predict(index):
    k = index // 2
    if index % 2 == 0:
        return {("c", k): 1.0}
    return {
        ("d", k): 1.0,
        ("c", k): 9 / 16,
        ("c", k + 1): 9 / 16,
        ("c", k - 1): -1 / 16,
        ("c", k + 2): -1 / 16,
    }


def predict_twice(index):
    whole = {}
    for (kind, k), weight in predict(index).items():
        if kind == "d":
            whole[("e", k)] = weight
            continue
        whole[("m", k)] = weight
        for key, inner in predict(k).items():
            whole[key] = whole.get(key, 0.0) + weight * inner
    return whole


def halo_row(kind, k):
    if kind == "c":
        return k - 32 if k >= 32 else 11 + k
    if kind == "d":
        return 3 if k >= 32 else 11
    if kind == "m":
        return 4 + k - 64 if k >= 64 else 14 + k
    return 7 if k >= 64 else 14


def y_matrices():
    own = np.zeros((4, 64, 256), np.float32)
    halo = np.zeros((5, 16, 256), np.float32)
    corner = np.zeros((4, 8, 256), np.float32)
    columns = [(y, y) for y in range(128)] + [(128, 128), (-1, 255)]
    for z in range(4):
        columns += [(y, 136 + 32 * z + j) for j, y in enumerate((-2, -1, 0, 127, 128, 129))]
    for y, column in columns:
        for (kind, k), weight in predict_twice(y).items():
            role = "cdme".index(kind)
            length = 32 if role < 2 else 64
            if 0 <= k < length:
                own[role, k, column] += weight
                continue
            row = halo_row(kind, k)
            halo[role, row, column] += weight
            if kind == "e":
                halo[4, row + 1, column] += weight
            if k >= length:
                corner[role, k - length, column] += weight
            else:
                corner[role, (5 if length == 32 else 7) + k, column] += weight
    parts = [own.reshape(256, 256), halo.reshape(80, 256), corner.reshape(32, 256)]
    return (0.5 * np.concatenate(parts)).astype(ml_dtypes.bfloat16)


def small_matrices():
    mats = np.zeros((144, 128), np.float32)
    for x in range(-2, 34):
        row = x + 8
        for (kind, k), weight in predict_twice(x).items():
            if kind == "c":
                at = 50 + k if k < 0 else (k if k < 8 else 56 + k - 8)
            elif kind == "d":
                at = 50 if k < 0 else (8 + k if k < 8 else 59)
            elif kind == "m":
                at = 53 + k if k < 0 else (16 + k if k < 16 else 60 + k - 16)
            else:
                at = 53 if k < 0 else (32 + k if k < 16 else 63)
            mats[row, at] += weight
    mats[6, 54] = 1.0
    mats[7, 55] = 1.0
    mats[0:48, 64:128] = mats[0:48, 0:64]
    picks = mats[48:128].reshape(5, 16, 128)
    for row, column in ((0, 0), (1, 1), (2, 2), (9, 30), (10, 31)):
        picks[0, row, column] = 1.0
    for row, column in ((3, 0), (11, 31)):
        picks[1, row, column] = 1.0
    for row, column in ((4, 0), (5, 1), (6, 2), (12, 62), (13, 63)):
        picks[2, row, column] = 1.0
    for row, column in ((7, 0), (14, 63)):
        picks[3, row, column] = 1.0
        picks[4, row + 1, column] = 1.0
    for row, column in ((0, 0), (1, 1), (2, 2), (3, 30), (4, 31), (5, 62), (6, 63)):
        mats[128 + row, column] = 1.0
    return mats.astype(ml_dtypes.bfloat16)


def face(mean, jump, k, factor=None):
    q, u, t = mean[0], mean[1:4], mean[4]
    rho = (0.5 * time_step) * jnp.exp(0.5 * q)
    if factor is not None:
        rho = rho * factor
    speed = u[k]
    half_square = 0.5 * (u[0] * u[0] + u[1] * u[1] + u[2] * u[2])
    enthalpy = (1.0 / heat_ratio_less_one + 1.0) * t + half_square
    inner = jump[0] + jump[1] * u[0] + jump[2] * u[1] + jump[3] * u[2] + jump[4] * enthalpy
    flow = rho * speed
    push = rho * jump[1 + k]
    grads = [flow * (jump[1 + j] + jump[4] * u[j]) for j in range(3)]
    grads[k] = grads[k] + rho * inner
    dq = 0.5 * (flow * inner + t * push)
    dt = push + (1.0 / heat_ratio_less_one + 1.0) * (flow * jump[4])
    terms = [dq] + grads + [dt]
    spread = [(viscosity * time_step) * jump[v] for v in range(5)]
    return [terms[v] + spread[v] for v in range(5)], [terms[v] - spread[v] for v in range(5)]


def kernel(
    c_in, x1_in, y1_in, x2_in, y2_in, sig_in, adj_in, ay_in, small_in,
    result,
    cx_ref, y1_ref, x2_ref, y2_ref, sig_ref, adj_ref, ay_ref, small_ref,
    load_sem,
    tiles, mask_x, mask_y, ext, hy2,
    first_send, first_recv, last_send, last_recv, low_send, low_recv, high_send, high_recv,
    corner_low, corner_low_recv, corner_high, corner_high_recv,
    ax_rows, ax_send, ax_recv, ay_send, ay_recv, rim,
    mapped, mapped_y2, state, adj, mid, gx_terms, gz_terms,
    own_cols, turned, rim_turned, own_turned, levels, levels_z, packed, beside,
    send_sem, recv_sem,
):
    gx, gy, gz = lax.axis_index("gx"), lax.axis_index("gy"), lax.axis_index("gz")
    nx, ny = lax.axis_size("gx"), lax.axis_size("gy")
    up_x, down_x = lax.rem(gx + 1, nx), lax.rem(gx + nx - 1, nx)
    up_y, down_y = lax.rem(gy + 1, ny), lax.rem(gy + ny - 1, ny)
    x_up, x_down = {"gx": up_x}, {"gx": down_x}
    y_up, y_down = {"gy": up_y}, {"gy": down_y}
    diagonal = (
        {"gx": up_x, "gy": down_y},
        {"gx": up_x, "gy": up_y},
        {"gx": down_x, "gy": down_y},
        {"gx": down_x, "gy": up_y},
    )
    z_other = {"gz": 1 - gz}
    barrier = pltpu.get_barrier_semaphore()
    for peer in (x_up, x_down, y_up, y_down, z_other) + diagonal:
        pl.semaphore_signal(barrier, inc=1, device_id=peer, device_id_type=MESH)

    pairs = (
        (sig_in, sig_ref), (x2_in, x2_ref), (y2_in, y2_ref), (c_in, cx_ref.at[0:320]),
        (x1_in, cx_ref.at[320:640]), (y1_in, y1_ref), (small_in, small_ref), (adj_in, adj_ref),
        (ay_in, ay_ref),
    )
    loads = [
        pltpu.make_async_copy(source, target, load_sem.at[i])
        for i, (source, target) in enumerate(pairs)
    ]
    for load in loads:
        load.start()

    def remote(index, source, target, peer):
        return pltpu.make_async_remote_copy(
            src_ref=source,
            dst_ref=target,
            send_sem=send_sem.at[index],
            recv_sem=recv_sem.at[index],
            device_id=peer,
            device_id_type=MESH,
        )

    def transposed(left, right):
        return lax.dot_general(left, right, (((1,), (1,)), ((), ())), preferred_element_type=f32)

    lane = lax.broadcasted_iota(jnp.int32, (8, 128), 1)
    lane_wide = lax.broadcasted_iota(jnp.int32, (32, 128), 1)
    lane_full = lax.broadcasted_iota(jnp.int32, (48, 128), 1)

    for load in loads[:8]:
        load.wait()
    lane_tile = lax.broadcasted_iota(jnp.int32, (4, 64), 1) // 16
    row_half = lax.broadcasted_iota(jnp.int32, (8, 64), 0) < 4
    for c in range(2):
        for z in range(4):
            flags = sig_ref[c, z].astype(f32)
            wide = jnp.zeros((4, 64), f32)
            for t in range(4):
                wide = jnp.where(lane_tile == t, flags[:, t : t + 1], wide)
            tiles[c, z, 0:4] = wide
            each = [jnp.broadcast_to(tiles[c, z, t : t + 1], (8, 64)) for t in range(4)]
            for t in range(4):
                mask_y[c, z, 8 * t : 8 * t + 8] = each[t]
            for t in range(2):
                mask_x[c, z, 8 * t : 8 * t + 8] = jnp.where(row_half, each[2 * t], each[2 * t + 1])

    kept_x2 = x2_ref[...].astype(f32).reshape(2, 5, 4, 16, 64) * mask_x[...][:, None]
    kept_y2 = y2_ref[...].astype(f32).reshape(2, 5, 4, 32, 64) * mask_y[...][:, None]
    ext[...] = jnp.zeros_like(ext)
    ext[0:640, 0:32] = cx_ref[...].astype(f32)
    ext[640:1280, 0:32] = y1_ref[...].astype(f32)
    ext[1280:1920, 0:64] = kept_x2.reshape(640, 64)
    ext[1920:3200, 0:64] = kept_y2.reshape(1280, 64)

    def own(begin, end):
        return ext[begin:end, 0:64].astype(bf16)

    starts = (0, 640, 1280, 1920, 2560)
    cols = jnp.zeros((16, 640), f32)
    for which, begin in enumerate(starts):
        pick = small_ref[48 + 16 * which : 64 + 16 * which, 0:64]
        cols = cols + transposed(pick, own(begin, begin + 640))
    first_send[...] = cols.astype(bf16)
    last_send[...] = cols[8:16].astype(bf16)

    coarse_e = ext[0:320].reshape(40, 8, 128)
    x1_e = ext[320:640].reshape(40, 8, 128)
    y1_e = ext[640:1280].reshape(40, 16, 128)
    x2_e = ext[1280:1920].reshape(40, 16, 128)
    y2_e = ext[1920:3200].reshape(40, 32, 128)
    low = jnp.concatenate(
        [coarse_e[:, 6:8], x1_e[:, 7:8], y1_e[:, 14:16], x2_e[:, 15:16], y2_e[:, 30:32]], 1
    ).reshape(320, 128)
    high = jnp.concatenate(
        [coarse_e[:, 0:3], x1_e[:, 0:1], y1_e[:, 0:3], x2_e[:, 0:1]], 1
    ).reshape(320, 128)
    hy2[80:96] = jnp.zeros((16, 128), f32)
    for p in range(40):
        hy2[2 * p : 2 * p + 2] = ext[1920 + 32 * p : 1922 + 32 * p]
    more = hy2[0:48] + pltpu.roll(hy2[48:96], 64, 1)
    low_send[...] = (low[0:160] + pltpu.roll(low[160:320], 64, 1)).astype(bf16)
    high_send[0:160] = (high[0:160] + pltpu.roll(high[160:320], 64, 1)).astype(bf16)
    high_send[160:208] = more.astype(bf16)
    columns = jnp.zeros((32, 128), f32)
    for i in range(20):
        plane = adj_ref[i // 4, i % 4]
        columns = jnp.where(lane_wide // 4 == i, pltpu.roll(plane, 4 * i + 2, 1), columns)
        ax_rows[0, 2 * i : 2 * i + 2] = plane[0:2]
        ax_rows[1, 2 * i : 2 * i + 2] = plane[30:32]
    ax_rows[:, 40:48] = jnp.zeros((2, 8, 128), f32)
    ax_send[...] = ax_rows[...].astype(bf16)
    ay_send[...] = columns.astype(bf16)
    own_cols[8:40] = columns

    last_row = lax.broadcasted_iota(jnp.int32, (8, 128), 0) == 7
    for target, pieces, row in (
        (corner_low, (low, jnp.zeros((64, 128), f32)), columns[31:32]),
        (corner_high, (high, hy2[0:80], jnp.zeros((112, 128), f32)), columns[0:1]),
    ):
        rows = jnp.concatenate(pieces, 0)[:, 0:64].astype(bf16)
        picked = transposed(small_ref[128:144, 0:64], rows)[0:8]
        target[:, 0:128] = jnp.where(last_row, row, picked[:, 0:128]).astype(bf16)
        target[:, 128:] = picked[:, 128:].astype(bf16)

    pl.semaphore_wait(barrier, 9)
    corner_copies = [remote(4 + i, corner_low, corner_low_recv.at[i], diagonal[i]) for i in range(2)]
    corner_copies += [
        remote(6 + i, corner_high, corner_high_recv.at[i], diagonal[2 + i]) for i in range(2)
    ]
    column_copies = [remote(0, first_send, first_recv, y_down), remote(1, last_send, last_recv, y_up)]
    row_copies = [remote(2, low_send, low_recv, x_up), remote(3, high_send, high_recv, x_down)]
    adj_copies = [
        remote(8, ay_send, ay_recv.at[0], y_down),
        remote(9, ay_send, ay_recv.at[1], y_up),
        remote(10, ax_send.at[0], ax_recv.at[1], x_down),
        remote(11, ax_send.at[1], ax_recv.at[0], x_up),
    ]
    for copy in corner_copies + column_copies + adj_copies + row_copies:
        copy.start()

    loads[8].wait()
    for begin, count, role, target, at in (
        (0, 8, 0, mapped, 0),
        (320, 8, 0, mapped, 8),
        (640, 16, 1, mapped, 16),
        (1280, 16, 2, mapped, 32),
        (1920, 32, 3, mapped_y2, 0),
    ):
        product = jnp.dot(
            own(begin, begin + 40 * count),
            ay_ref[64 * role : 64 * role + 64],
            preferred_element_type=f32,
        )
        target[:, at : at + count] = product.reshape(40, count, 256)
    mapped_y2[:, 32:40] = jnp.zeros((40, 8, 256), f32)

    outer = 5 * gz
    z_side = 3 - 3 * gz
    blank = jnp.zeros((48, 128), f32)
    for t in range(2):
        for v in range(5):
            adj[t, v, outer] = blank
            mid[t, v, outer] = blank
        for cv in range(10):
            state[t, cv, outer] = blank
    for i in range(20):
        v, z = i // 4, i % 4
        adj[0, v, z + 1, 0:8] = blank[0:8]
        adj[0, v, z + 1, 40:48] = blank[0:8]
        adj[0, v, z + 1, 8:40] = adj_ref[v, z]
    rim[...] = blank

    for copy in adj_copies:
        copy.wait()
    ax_rows[...] = ax_recv[...].astype(f32)
    for i in range(20):
        v, z = i // 4, i % 4
        adj[0, v, z + 1, 6:8] = ax_rows[0, 2 * i : 2 * i + 2]
        adj[0, v, z + 1, 40:42] = ax_rows[1, 2 * i : 2 * i + 2]
    for begin in (0, 40):
        ends = jnp.zeros((8, 128), f32)
        for i in range(20):
            tile = adj[0, i // 4, i % 4 + 1, begin : begin + 8]
            ends = jnp.where(lane // 4 == i, pltpu.roll(tile, 4 * i + 2, 1), ends)
        own_cols[begin : begin + 8] = ends
    first = lane_wide % 4 >= 2
    rim[8:40] = jnp.where(first, ay_recv[0].astype(f32), ay_recv[1].astype(f32))
    near = (lane_full < 2) | (lane_full >= 126)

    def fill_rim(begin, end):
        part = rim[begin:end]
        for i in range(20):
            adj[1, i // 4, i % 4 + 1, begin:end] = jnp.where(
                near[begin:end], pltpu.roll(part, (126 - 4 * i) % 128, 1), 0.0
            )

    fill_rim(8, 40)

    for copy in column_copies:
        copy.wait()
    firsts, lasts = first_recv[...].astype(f32), last_recv[...].astype(f32)
    top = lax.broadcasted_iota(jnp.int32, (8, 640), 0) == 0
    joined = jnp.concatenate([firsts[0:8], jnp.where(top, firsts[8:16], lasts)], 0).T.astype(bf16)
    halo = [
        jnp.dot(joined, ay_ref[256 + 16 * i : 272 + 16 * i], preferred_element_type=f32)
        for i in range(5)
    ]
    mapped[:, 0:8] += halo[0][0:320].reshape(40, 8, 256)
    mapped[:, 8:16] += halo[0][320:640].reshape(40, 8, 256)
    mapped[:, 16:32] += halo[1].reshape(40, 16, 256)
    mapped[:, 32:48] += halo[2].reshape(40, 16, 256)
    mapped_y2[0:20, 0:32] += halo[3].reshape(20, 32, 256)
    mapped_y2[20:40, 0:32] += halo[4].reshape(20, 32, 256)

    for copy in row_copies:
        copy.wait()
    low_half, high_half = low_recv[...].astype(f32), high_recv[...].astype(f32)

    upper = lax.broadcasted_iota(jnp.int32, (320, 128), 1) >= 64
    row_kind = lax.broadcasted_iota(jnp.int32, (320, 128), 0) % 8

    def doubled(half):
        turned = pltpu.roll(half, 64, 1)
        left = upper[0 : half.shape[0]]
        return jnp.concatenate([jnp.where(left, turned, half), jnp.where(left, half, turned)], 0)

    for half, bounds, target in (
        (low_half, (3, 5, 6), 48),
        (high_half[0:160], (4, 7, 8), 56),
    ):
        values = doubled(half)
        role = jnp.where(
            row_kind < bounds[0], 0, jnp.where(row_kind < bounds[1], 1, jnp.where(row_kind < bounds[2], 2, 3))
        )
        spot = jnp.where(upper, 1, 0)
        parts = [jnp.where(role == spot + 2 * i, values, 0.0) for i in range(2)]
        total = jnp.dot(
            jnp.concatenate(parts, 1).astype(bf16), ay_ref[0:256], preferred_element_type=f32
        )
        mapped[:, target : target + 8] = total.reshape(40, 8, 256)
    more = doubled(high_half[160:208])[0:80, 0:64].astype(bf16)
    beyond = jnp.dot(more, ay_ref[192:256], preferred_element_type=f32)

    def from_corners(parts, role_of):
        width = parts.shape[2]
        row = lax.broadcasted_iota(jnp.int32, (8, width), 0)
        corners = jnp.where(row < 3, parts[0].astype(f32), parts[1].astype(f32))
        role = role_of(lax.broadcasted_iota(jnp.int32, (8, width), 1))
        stacked = jnp.concatenate([jnp.where(role == r, corners, 0.0) for r in range(4)], 0)
        return jnp.dot(stacked.T.astype(bf16), ay_ref[336:368], preferred_element_type=f32)

    def low_role(place):
        kind = place % 8
        return jnp.where(kind < 3, 0, jnp.where(kind < 5, 1, jnp.where(kind < 6, 2, 3)))

    def high_role(place):
        kind = place % 8
        inner = jnp.where(kind < 4, 0, jnp.where(kind < 7, 1, 2))
        return jnp.where(place < 320, inner, 3)

    for copy in corner_copies:
        copy.wait()
    from_low = from_corners(corner_low_recv, low_role)
    from_high = from_corners(corner_high_recv, high_role)
    mapped[:, 48:56] += from_low[0:320].reshape(40, 8, 256)
    mapped[:, 56:64] += from_high[0:320].reshape(40, 8, 256)
    beyond = beyond + from_high[320:400]
    for p in range(40):
        mapped_y2[p, 32:34] = beyond[2 * p : 2 * p + 2]
    for parts, at in ((corner_low_recv, 7), (corner_high_recv, 40)):
        rows = [parts[i, :, 0:128].astype(f32)[7:8] for i in range(2)]
        rim[at : at + 1] = jnp.where(first[0:1], rows[0], rows[1])
    fill_rim(0, 8)
    fill_rim(40, 48)
    adj_z = remote(12, adj.at[0, :, z_side + 1], adj.at[0, :, outer], z_other)
    adj_z.start()
    rim_turned[:, 0:48] = rim[...].T
    own_turned[:, 0:48] = own_cols[...].T

    def level_rows(kind, level, v, low, high):
        for z in range(4):
            levels[kind, level, v, 2 * z : 2 * z + 1] = low(z)
            levels[kind, level, v, 2 * z + 1 : 2 * z + 2] = high(z)

    for v in range(5):
        for level, source, low_at, high_at in ((0, rim_turned, 1, 2), (1, rim_turned, 0, 3), (2, own_turned, 2, 1)):
            level_rows(
                0,
                level,
                v,
                lambda z: source[16 * v + 4 * z + low_at : 16 * v + 4 * z + low_at + 1],
                lambda z: source[16 * v + 4 * z + high_at : 16 * v + 4 * z + high_at + 1],
            )

    def synthesize(order, cv, carry):
        for z in order:
            p = cv * 4 + z
            exact = mapped[p]
            coarse_bits = exact.astype(bf16)
            rest = (exact - coarse_bits.astype(f32)).astype(bf16)
            whole = jnp.dot(
                small_ref[0:48],
                jnp.concatenate([coarse_bits, rest], axis=0),
                preferred_element_type=f32,
            )
            extra = mapped_y2[p]
            for t in range(2):
                at = slice(128 * t, 128 * t + 128)
                state[t, cv, z + 1, 0:8] = whole[0:8, at]
                state[t, cv, z + 1, 8:48] = whole[8:48, at] + extra[:, at]
        return carry

    def synthesize_sides(pair, carry):
        for j in range(5):
            synthesize((z_side,), 5 * pair + j, carry)
        return carry

    for cv in range(10):
        synthesize((z_side,), cv, 0)
    state_first = remote(13, state.at[0, 0:5, z_side + 1], state.at[0, 0:5, outer], z_other)
    state_second = remote(
        14, state.at[0, 5:10, z_side + 1, 8:40], state.at[0, 5:10, outer, 8:40], z_other
    )
    state_first.start()
    state_second.start()
    def synthesize_rest(pair, carry):
        for j in range(5):
            synthesize((gz, gz + 1, gz + 2), 5 * pair + j, carry)
        return carry

    lax.fori_loop(0, 2, synthesize_rest, 0)
    group = lane_full // 32
    for v in range(5):
        joint = state[1, v, 1]
        for z in range(1, 4):
            joint = jnp.where(group == z, state[1, v, z + 1], joint)
        turned[v, :, 0:48] = joint.T
    for v in range(5):
        for level, low_at, high_at in ((0, 9, 12), (1, 8, 13), (2, 10, 11)):
            level_rows(
                1,
                level,
                v,
                lambda z: turned[v, 32 * z + low_at : 32 * z + low_at + 1],
                lambda z: turned[v, 32 * z + high_at : 32 * z + high_at + 1],
            )
    levels_copy = remote(16, levels.at[:, 0], levels_z, z_other)
    levels_copy.start()
    sublane8 = lax.broadcasted_iota(jnp.int32, (8, 128), 0)
    is_low = sublane8 % 2 == 0
    sign = jnp.where(is_low, 1.0, -1.0).astype(f32)

    def level(kind, which):
        return [levels[kind, which, v] for v in range(5)]

    rim_adj, rim_state = level(0, 0), level(1, 0)
    inner_adj, inner_state = level(0, 2), level(1, 2)
    lower, upper_share = face(
        [rim_state[v] + inner_state[v] for v in range(5)],
        [sign * (inner_adj[v] - rim_adj[v]) for v in range(5)],
        1,
    )
    for v in range(5):
        packed[8 * v : 8 * v + 8] = upper_share[v]
    inner_share = [jnp.where(is_low, lower[v], upper_share[v]) for v in range(5)]
    back = packed[...].T
    for i in range(20):
        v, z = i // 4, i % 4
        beside[v, z] = pltpu.roll(back[0:48], (128 - 8 * v - 2 * z) % 128, 1)
    outer_adj, outer_state = level(0, 1), level(1, 1)
    lower, upper_share = face(
        [rim_state[v] + outer_state[v] for v in range(5)],
        [sign * (rim_adj[v] - outer_adj[v]) for v in range(5)],
        1,
    )
    rim_middle = [
        rim_adj[v] + inner_share[v] + jnp.where(is_low, upper_share[v], lower[v]) for v in range(5)
    ]
    lower, upper_share = face(
        [rim_state[v] + pltpu.roll(rim_state[v], 127, 1) for v in range(5)],
        [pltpu.roll(rim_adj[v], 127, 1) - rim_adj[v] for v in range(5)],
        0,
    )
    for v in range(5):
        levels[0, 1, v] = rim_middle[v] + lower[v] + pltpu.roll(upper_share[v], 1, 1)
    adj_z.wait()
    state_first.wait()

    keep_bottom = jnp.where(gz > 0, 1.0, 0.0).astype(f32)

    def ahead(a, b):
        return pltpu.roll(jnp.where(lane == 0, b, a), 127, 1)

    def behind(a, b):
        return pltpu.roll(jnp.where(lane == 127, b, a), 1, 1)

    def x_face(t, base, source, z, r, start):
        low_at = slice(start + 8 * r, start + 8 + 8 * r)
        high_at = slice(start + 1 + 8 * r, start + 9 + 8 * r)
        mean = [
            (state[t, base + v, z + 1, low_at] + state[t, base + v, z + 1, high_at])
            for v in range(5)
        ]
        jump = [source[t, v, z + 1, high_at] - source[t, v, z + 1, low_at] for v in range(5)]
        below, above = face(mean, jump, 0)
        for v in range(5):
            gx_terms[0, t, v, 8 * r : 8 * r + 8] = below[v]
            gx_terms[1, t, v, 8 * r : 8 * r + 8] = above[v]

    def z_face(t, base, source, k, count, start):
        for r in range(count):
            at = slice(start + 8 * r, start + 8 + 8 * r)
            mean = [
                state[t, base + v, k, at] + state[t, base + v, k + 1, at] for v in range(5)
            ]
            jump = [source[t, v, k + 1, at] - source[t, v, k, at] for v in range(5)]
            below, above = face(mean, jump, 2, jnp.where(k == 0, keep_bottom, 1.0))
            for v in range(5):
                gz_terms[0, t, v, k, 8 * r : 8 * r + 8] = below[v]
                gz_terms[1, t, v, k, 8 * r : 8 * r + 8] = above[v]

    def first_z(k, carry):
        z_face(0, 0, adj, k, 5, 7)
        return carry

    lax.fori_loop(0, 5, first_z, 0)
    mid_z = remote(15, mid.at[0, :, z_side + 1, 8:40], mid.at[0, :, outer, 8:40], z_other)

    def first_plane(j, carry):
        @pl.when(j == 1)
        def _():
            mid_z.start()

        z = jnp.where(gz > 0, j, 3 - j)
        for r in range(5):
            x_face(0, 0, adj, z, r, 6)
        for r in range(5):
            at, rows = slice(7 + 8 * r, 15 + 8 * r), slice(8 * r, 8 * r + 8)
            here = [state[0, v, z + 1, at] for v in range(5)]
            held = [adj[0, v, z + 1, at] for v in range(5)]
            below, above = face(
                [here[v] + ahead(here[v], state[1, v, z + 1, at]) for v in range(5)],
                [ahead(held[v], adj[1, v, z + 1, at]) - held[v] for v in range(5)],
                1,
            )
            for v in range(5):
                mid[0, v, z + 1, at] = (
                    held[v]
                    + below[v]
                    + jnp.where(lane == 0, beside[v, z, at], pltpu.roll(above[v], 1, 1))
                    + gx_terms[0, 0, v, 8 * r + 1 : 8 * r + 9]
                    + gx_terms[1, 0, v, rows]
                    + gz_terms[0, 0, v, z + 1, rows]
                    + gz_terms[1, 0, v, z, rows]
                )
        return carry

    lax.fori_loop(0, 4, first_plane, 0)
    levels_copy.wait()
    up_part = jnp.where(gz > 0, 0.0, 1.0).astype(f32)
    down_part = 1.0 - up_part

    def next_plane(kind, v):
        tile = levels[kind, 0, v]
        from_other = levels_z[kind, v]
        return (
            jnp.where(sublane8 >= 6, up_part * pltpu.roll(from_other, 6, 0), pltpu.roll(tile, 6, 0)),
            jnp.where(sublane8 < 2, down_part * pltpu.roll(from_other, 2, 0), pltpu.roll(tile, 2, 0)),
        )

    rim_adj, rim_state = level(0, 0), level(1, 0)
    next_adj = [next_plane(0, v) for v in range(5)]
    next_state = [next_plane(1, v) for v in range(5)]
    lower, _ = face(
        [rim_state[v] + next_state[v][0] for v in range(5)],
        [next_adj[v][0] - rim_adj[v] for v in range(5)],
        2,
    )
    _, upper_share = face(
        [rim_state[v] + next_state[v][1] for v in range(5)],
        [rim_adj[v] - next_adj[v][1] for v in range(5)],
        2,
        jnp.where(sublane8 < 2, keep_bottom, 1.0),
    )
    for v in range(5):
        packed[8 * v : 8 * v + 8] = levels[0, 1, v] + lower[v] + upper_share[v]
    back = packed[...].T
    for i in range(20):
        v, z = i // 4, i % 4
        mid[1, v, z + 1, 8:40] = pltpu.roll(back[8:40], (127 - 8 * v - 2 * z) % 128, 1)
    state_second.wait()

    def second_z(k, carry):
        z_face(0, 5, mid, k, 4, 8)
        return carry

    lax.fori_loop(gz, gz + 4, second_z, 0)

    def second_plane(j, carry):
        z = jnp.where(gz > 0, 3 - j, j)

        @pl.when(j == 3)
        def _():
            mid_z.wait()
            z_face(0, 5, mid, 4 - 4 * gz, 4, 8)

        for r in range(5):
            x_face(0, 5, mid, z, r, 7)
        for r in range(4):
            at, rows = slice(8 + 8 * r, 16 + 8 * r), slice(8 * r, 8 * r + 8)
            here = [state[0, 5 + v, z + 1, at] for v in range(5)]
            edge = [state[1, 5 + v, z + 1, at] for v in range(5)]
            held = [mid[0, v, z + 1, at] for v in range(5)]
            held_edge = [mid[1, v, z + 1, at] for v in range(5)]
            adj_up = [ahead(held[v], held_edge[v]) for v in range(5)]
            adj_down = [behind(held[v], held_edge[v]) for v in range(5)]
            below, _ = face(
                [here[v] + ahead(here[v], edge[v]) for v in range(5)],
                [adj_up[v] - held[v] for v in range(5)],
                1,
            )
            _, above = face(
                [here[v] + behind(here[v], edge[v]) for v in range(5)],
                [held[v] - adj_down[v] for v in range(5)],
                1,
            )
            for v in range(5):
                result[v, z, rows] = 0.5 * (
                    adj[0, v, z + 1, at]
                    + held[v]
                    + below[v]
                    + above[v]
                    + gx_terms[0, 0, v, 8 * r + 1 : 8 * r + 9]
                    + gx_terms[1, 0, v, rows]
                    + gz_terms[0, 0, v, z + 1, rows]
                    + gz_terms[1, 0, v, z, rows]
                )
        return carry

    lax.fori_loop(0, 4, second_plane, 0)


def shards(coarse, detail_x1, detail_y1, detail_x2, detail_y2, significance, adjoint):
    operands = [
        pltpu.with_memory_space_constraint(value, pltpu.HBM)
        for value in (
            coarse.reshape(320, 32),
            detail_x1.reshape(320, 32),
            detail_y1.reshape(640, 32),
            detail_x2.reshape(640, 64),
            detail_y2.reshape(1280, 64),
            significance,
            adjoint,
            jnp.asarray(y_matrices()),
            jnp.asarray(small_matrices()),
        )
    ]
    anywhere = pl.BlockSpec(memory_space=pl.ANY)
    return pl.pallas_call(
        kernel,
        out_shape=jax.ShapeDtypeStruct(adjoint.shape, f32),
        in_specs=[anywhere] * 9,
        out_specs=pl.BlockSpec(memory_space=pltpu.VMEM),
        scratch_shapes=[
            pltpu.VMEM((640, 32), bf16),
            pltpu.VMEM((640, 32), bf16),
            pltpu.VMEM((640, 64), bf16),
            pltpu.VMEM((1280, 64), bf16),
            pltpu.VMEM((2, 4, 4, 4), jnp.int32),
            pltpu.VMEM((5, 4, 32, 128), f32),
            pltpu.VMEM((368, 256), bf16),
            pltpu.VMEM((144, 128), bf16),
            pltpu.SemaphoreType.DMA((9,)),
            pltpu.VMEM((2, 4, 8, 64), f32),
            pltpu.VMEM((2, 4, 16, 64), f32),
            pltpu.VMEM((2, 4, 32, 64), f32),
            pltpu.VMEM((3200, 128), f32),
            pltpu.VMEM((96, 128), f32),
            pltpu.VMEM((16, 640), bf16),
            pltpu.VMEM((16, 640), bf16),
            pltpu.VMEM((8, 640), bf16),
            pltpu.VMEM((8, 640), bf16),
            pltpu.VMEM((160, 128), bf16),
            pltpu.VMEM((160, 128), bf16),
            pltpu.VMEM((208, 128), bf16),
            pltpu.VMEM((208, 128), bf16),
            pltpu.VMEM((8, 384), bf16),
            pltpu.VMEM((2, 8, 384), bf16),
            pltpu.VMEM((8, 512), bf16),
            pltpu.VMEM((2, 8, 512), bf16),
            pltpu.VMEM((2, 48, 128), f32),
            pltpu.VMEM((2, 48, 128), bf16),
            pltpu.VMEM((2, 48, 128), bf16),
            pltpu.VMEM((32, 128), bf16),
            pltpu.VMEM((2, 32, 128), bf16),
            pltpu.VMEM((48, 128), f32),
            pltpu.VMEM((40, 64, 256), f32),
            pltpu.VMEM((40, 40, 256), f32),
            pltpu.VMEM((2, 10, 6, 48, 128), f32),
            pltpu.VMEM((2, 5, 6, 48, 128), f32),
            pltpu.VMEM((2, 5, 6, 48, 128), f32),
            pltpu.VMEM((2, 1, 5, 48, 128), f32),
            pltpu.VMEM((2, 1, 5, 5, 40, 128), f32),
            pltpu.VMEM((48, 128), f32),
            pltpu.VMEM((5, 128, 128), f32),
            pltpu.VMEM((128, 128), f32),
            pltpu.VMEM((128, 128), f32),
            pltpu.VMEM((2, 3, 5, 8, 128), f32),
            pltpu.VMEM((2, 5, 8, 128), f32),
            pltpu.VMEM((128, 128), f32),
            pltpu.VMEM((5, 4, 48, 128), f32),
            pltpu.SemaphoreType.DMA((17,)),
            pltpu.SemaphoreType.DMA((17,)),
        ],
        compiler_params=pltpu.CompilerParams(collective_id=0, has_side_effects=True, vmem_limit_bytes=40*2**20),
    )(
        *operands,
    )


def solution(mesh):
    return jax.shard_map(
        shards,
        mesh=mesh,
        in_specs=(
            P(None, None, "gz", "gx", "gy"),
            P(None, None, "gz", "gx", "gy"),
            P(None, None, "gz", "gx", "gy"),
            P(None, None, "gz", "gx", "gy"),
            P(None, None, "gz", "gx", "gy"),
            P(None, "gz", "gx", "gy"),
            P(None, "gz", "gx", "gy"),
        ),
        out_specs=P(None, "gz", "gx", "gy"),
        check_vma=False,
    )
```

```python
import functools

import jax
import jax.numpy as jnp
import ml_dtypes
import numpy as np
from jax import lax
from jax.experimental import pallas as pl
from jax.experimental.pallas import tpu as pltpu
from jax.sharding import PartitionSpec as P

time_step = 0.1
viscosity = 0.2
heat_ratio_less_one = 0.4
f32 = jnp.float32
bf16 = jnp.bfloat16
MESH = pl.DeviceIdType.MESH


def predict(index):
    k = index // 2
    if index % 2 == 0:
        return {("c", k): 1.0}
    return {
        ("d", k): 1.0,
        ("c", k): 9 / 16,
        ("c", k + 1): 9 / 16,
        ("c", k - 1): -1 / 16,
        ("c", k + 2): -1 / 16,
    }


def predict_twice(index):
    whole = {}
    for (kind, k), weight in predict(index).items():
        if kind == "d":
            whole[("e", k)] = weight
            continue
        whole[("m", k)] = weight
        for key, inner in predict(k).items():
            whole[key] = whole.get(key, 0.0) + weight * inner
    return whole


def halo_row(kind, k):
    if kind == "c":
        return k - 32 if k >= 32 else 11 + k
    if kind == "d":
        return 3 if k >= 32 else 11
    if kind == "m":
        return 4 + k - 64 if k >= 64 else 14 + k
    return 7 if k >= 64 else 14


def y_matrices():
    own = np.zeros((4, 64, 256), np.float32)
    halo = np.zeros((5, 16, 256), np.float32)
    corner = np.zeros((4, 8, 256), np.float32)
    columns = [(y, y) for y in range(128)] + [(128, 128), (-1, 255)]
    for z in range(4):
        columns += [(y, 136 + 32 * z + j) for j, y in enumerate((-2, -1, 0, 127, 128, 129))]
    for y, column in columns:
        for (kind, k), weight in predict_twice(y).items():
            role = "cdme".index(kind)
            length = 32 if role < 2 else 64
            if 0 <= k < length:
                own[role, k, column] += weight
                continue
            row = halo_row(kind, k)
            halo[role, row, column] += weight
            if kind == "e":
                halo[4, row + 1, column] += weight
            if k >= length:
                corner[role, k - length, column] += weight
            else:
                corner[role, (5 if length == 32 else 7) + k, column] += weight
    parts = [own.reshape(256, 256), halo.reshape(80, 256), corner.reshape(32, 256)]
    return (0.5 * np.concatenate(parts)).astype(ml_dtypes.bfloat16)


def small_matrices():
    mats = np.zeros((144, 128), np.float32)
    for x in range(-2, 34):
        row = x + 8
        for (kind, k), weight in predict_twice(x).items():
            if kind == "c":
                at = 50 + k if k < 0 else (k if k < 8 else 56 + k - 8)
            elif kind == "d":
                at = 50 if k < 0 else (8 + k if k < 8 else 59)
            elif kind == "m":
                at = 53 + k if k < 0 else (16 + k if k < 16 else 60 + k - 16)
            else:
                at = 53 if k < 0 else (32 + k if k < 16 else 63)
            mats[row, at] += weight
    mats[6, 54] = 1.0
    mats[7, 55] = 1.0
    mats[0:48, 64:128] = mats[0:48, 0:64]
    picks = mats[48:128].reshape(5, 16, 128)
    for row, column in ((0, 0), (1, 1), (2, 2), (9, 30), (10, 31)):
        picks[0, row, column] = 1.0
    for row, column in ((3, 0), (11, 31)):
        picks[1, row, column] = 1.0
    for row, column in ((4, 0), (5, 1), (6, 2), (12, 62), (13, 63)):
        picks[2, row, column] = 1.0
    for row, column in ((7, 0), (14, 63)):
        picks[3, row, column] = 1.0
        picks[4, row + 1, column] = 1.0
    for row, column in ((0, 0), (1, 1), (2, 2), (3, 30), (4, 31), (5, 62), (6, 63)):
        mats[128 + row, column] = 1.0
    return mats.astype(ml_dtypes.bfloat16)


def face(mean, jump, k, factor=None):
    q, u, t = mean[0], mean[1:4], mean[4]
    rho = (0.5 * time_step) * jnp.exp(0.5 * q)
    if factor is not None:
        rho = rho * factor
    speed = u[k]
    half_square = 0.5 * (u[0] * u[0] + u[1] * u[1] + u[2] * u[2])
    enthalpy = (1.0 / heat_ratio_less_one + 1.0) * t + half_square
    inner = jump[0] + jump[1] * u[0] + jump[2] * u[1] + jump[3] * u[2] + jump[4] * enthalpy
    flow = rho * speed
    push = rho * jump[1 + k]
    grads = [flow * (jump[1 + j] + jump[4] * u[j]) for j in range(3)]
    grads[k] = grads[k] + rho * inner
    dq = 0.5 * (flow * inner + t * push)
    dt = push + (1.0 / heat_ratio_less_one + 1.0) * (flow * jump[4])
    terms = [dq] + grads + [dt]
    spread = [(viscosity * time_step) * jump[v] for v in range(5)]
    return [terms[v] + spread[v] for v in range(5)], [terms[v] - spread[v] for v in range(5)]


def kernel(
    c_in, x1_in, y1_in, x2_in, y2_in, sig_in, adj_in, ay_in, small_in,
    result,
    cx_ref, y1_ref, x2_ref, y2_ref, sig_ref, adj_ref, ay_ref, small_ref,
    load_sem,
    tiles, mask_x, mask_y, ext, hy2,
    first_send, first_recv, last_send, last_recv, low_send, low_recv, high_send, high_recv,
    corner_low, corner_low_recv, corner_high, corner_high_recv,
    ax_rows, ax_send, ax_recv, ay_send, ay_recv, rim,
    mapped, mapped_y2, state, adj, mid, gx_terms, gz_terms,
    own_cols, turned, rim_turned, own_turned, levels, levels_z, packed, beside,
    send_sem, recv_sem,
):
    gx, gy, gz = lax.axis_index("gx"), lax.axis_index("gy"), lax.axis_index("gz")
    nx, ny = lax.axis_size("gx"), lax.axis_size("gy")
    up_x, down_x = lax.rem(gx + 1, nx), lax.rem(gx + nx - 1, nx)
    up_y, down_y = lax.rem(gy + 1, ny), lax.rem(gy + ny - 1, ny)
    x_up, x_down = {"gx": up_x}, {"gx": down_x}
    y_up, y_down = {"gy": up_y}, {"gy": down_y}
    diagonal = (
        {"gx": up_x, "gy": down_y},
        {"gx": up_x, "gy": up_y},
        {"gx": down_x, "gy": down_y},
        {"gx": down_x, "gy": up_y},
    )
    z_other = {"gz": 1 - gz}
    barrier = pltpu.get_barrier_semaphore()
    for peer in (x_up, x_down, y_up, y_down, z_other) + diagonal:
        pl.semaphore_signal(barrier, inc=1, device_id=peer, device_id_type=MESH)

    pairs = (
        (sig_in, sig_ref), (x2_in, x2_ref), (y2_in, y2_ref), (c_in, cx_ref.at[0:320]),
        (x1_in, cx_ref.at[320:640]), (y1_in, y1_ref), (small_in, small_ref), (adj_in, adj_ref),
        (ay_in, ay_ref),
    )
    loads = [
        pltpu.make_async_copy(source, target, load_sem.at[i])
        for i, (source, target) in enumerate(pairs)
    ]
    for load in loads:
        load.start()

    def remote(index, source, target, peer):
        return pltpu.make_async_remote_copy(
            src_ref=source,
            dst_ref=target,
            send_sem=send_sem.at[index],
            recv_sem=recv_sem.at[index],
            device_id=peer,
            device_id_type=MESH,
        )

    def transposed(left, right):
        return lax.dot_general(left, right, (((1,), (1,)), ((), ())), preferred_element_type=f32)

    lane = lax.broadcasted_iota(jnp.int32, (8, 128), 1)
    lane_wide = lax.broadcasted_iota(jnp.int32, (32, 128), 1)
    lane_full = lax.broadcasted_iota(jnp.int32, (48, 128), 1)

    for load in loads[:8]:
        load.wait()
    lane_tile = lax.broadcasted_iota(jnp.int32, (4, 64), 1) // 16
    row_half = lax.broadcasted_iota(jnp.int32, (8, 64), 0) < 4
    for c in range(2):
        for z in range(4):
            flags = sig_ref[c, z].astype(f32)
            wide = jnp.zeros((4, 64), f32)
            for t in range(4):
                wide = jnp.where(lane_tile == t, flags[:, t : t + 1], wide)
            tiles[c, z, 0:4] = wide
            each = [jnp.broadcast_to(tiles[c, z, t : t + 1], (8, 64)) for t in range(4)]
            for t in range(4):
                mask_y[c, z, 8 * t : 8 * t + 8] = each[t]
            for t in range(2):
                mask_x[c, z, 8 * t : 8 * t + 8] = jnp.where(row_half, each[2 * t], each[2 * t + 1])

    kept_x2 = x2_ref[...].astype(f32).reshape(2, 5, 4, 16, 64) * mask_x[...][:, None]
    kept_y2 = y2_ref[...].astype(f32).reshape(2, 5, 4, 32, 64) * mask_y[...][:, None]
    ext[...] = jnp.zeros_like(ext)
    ext[0:640, 0:32] = cx_ref[...].astype(f32)
    ext[640:1280, 0:32] = y1_ref[...].astype(f32)
    ext[1280:1920, 0:64] = kept_x2.reshape(640, 64)
    ext[1920:3200, 0:64] = kept_y2.reshape(1280, 64)

    def own(begin, end):
        return ext[begin:end, 0:64].astype(bf16)

    starts = (0, 640, 1280, 1920, 2560)
    cols = jnp.zeros((16, 640), f32)
    for which, begin in enumerate(starts):
        pick = small_ref[48 + 16 * which : 64 + 16 * which, 0:64]
        cols = cols + transposed(pick, own(begin, begin + 640))
    first_send[...] = cols.astype(bf16)
    last_send[...] = cols[8:16].astype(bf16)

    coarse_e = ext[0:320].reshape(40, 8, 128)
    x1_e = ext[320:640].reshape(40, 8, 128)
    y1_e = ext[640:1280].reshape(40, 16, 128)
    x2_e = ext[1280:1920].reshape(40, 16, 128)
    y2_e = ext[1920:3200].reshape(40, 32, 128)
    low = jnp.concatenate(
        [coarse_e[:, 6:8], x1_e[:, 7:8], y1_e[:, 14:16], x2_e[:, 15:16], y2_e[:, 30:32]], 1
    ).reshape(320, 128)
    high = jnp.concatenate(
        [coarse_e[:, 0:3], x1_e[:, 0:1], y1_e[:, 0:3], x2_e[:, 0:1]], 1
    ).reshape(320, 128)
    hy2[80:96] = jnp.zeros((16, 128), f32)
    for p in range(40):
        hy2[2 * p : 2 * p + 2] = ext[1920 + 32 * p : 1922 + 32 * p]
    more = hy2[0:48] + pltpu.roll(hy2[48:96], 64, 1)
    low_send[...] = (low[0:160] + pltpu.roll(low[160:320], 64, 1)).astype(bf16)
    high_send[0:160] = (high[0:160] + pltpu.roll(high[160:320], 64, 1)).astype(bf16)
    high_send[160:208] = more.astype(bf16)
    columns = jnp.zeros((32, 128), f32)
    for i in range(20):
        plane = adj_ref[i // 4, i % 4]
        columns = jnp.where(lane_wide // 4 == i, pltpu.roll(plane, 4 * i + 2, 1), columns)
        ax_rows[0, 2 * i : 2 * i + 2] = plane[0:2]
        ax_rows[1, 2 * i : 2 * i + 2] = plane[30:32]
    ax_rows[:, 40:48] = jnp.zeros((2, 8, 128), f32)
    ax_send[...] = ax_rows[...].astype(bf16)
    ay_send[...] = columns.astype(bf16)
    own_cols[8:40] = columns

    last_row = lax.broadcasted_iota(jnp.int32, (8, 128), 0) == 7
    for target, pieces, row in (
        (corner_low, (low, jnp.zeros((64, 128), f32)), columns[31:32]),
        (corner_high, (high, hy2[0:80], jnp.zeros((112, 128), f32)), columns[0:1]),
    ):
        rows = jnp.concatenate(pieces, 0)[:, 0:64].astype(bf16)
        picked = transposed(small_ref[128:144, 0:64], rows)[0:8]
        target[:, 0:128] = jnp.where(last_row, row, picked[:, 0:128]).astype(bf16)
        target[:, 128:] = picked[:, 128:].astype(bf16)

    pl.semaphore_wait(barrier, 9)
    corner_copies = [remote(4 + i, corner_low, corner_low_recv.at[i], diagonal[i]) for i in range(2)]
    corner_copies += [
        remote(6 + i, corner_high, corner_high_recv.at[i], diagonal[2 + i]) for i in range(2)
    ]
    column_copies = [remote(0, first_send, first_recv, y_down), remote(1, last_send, last_recv, y_up)]
    row_copies = [remote(2, low_send, low_recv, x_up), remote(3, high_send, high_recv, x_down)]
    adj_copies = [
        remote(8, ay_send, ay_recv.at[0], y_down),
        remote(9, ay_send, ay_recv.at[1], y_up),
        remote(10, ax_send.at[0], ax_recv.at[1], x_down),
        remote(11, ax_send.at[1], ax_recv.at[0], x_up),
    ]
    for copy in corner_copies + column_copies + adj_copies + row_copies:
        copy.start()

    loads[8].wait()
    for begin, count, role, target, at in (
        (0, 8, 0, mapped, 0),
        (320, 8, 0, mapped, 8),
        (640, 16, 1, mapped, 16),
        (1280, 16, 2, mapped, 32),
        (1920, 32, 3, mapped_y2, 0),
    ):
        product = jnp.dot(
            own(begin, begin + 40 * count),
            ay_ref[64 * role : 64 * role + 64],
            preferred_element_type=f32,
        )
        target[:, at : at + count] = product.reshape(40, count, 256)
    mapped_y2[:, 32:40] = jnp.zeros((40, 8, 256), f32)

    outer = 5 * gz
    z_side = 3 - 3 * gz
    blank = jnp.zeros((48, 128), f32)
    for t in range(2):
        for v in range(5):
            adj[t, v, outer] = blank
            mid[t, v, outer] = blank
        for cv in range(10):
            state[t, cv, outer] = blank
    for i in range(20):
        v, z = i // 4, i % 4
        adj[0, v, z + 1, 0:8] = blank[0:8]
        adj[0, v, z + 1, 40:48] = blank[0:8]
        adj[0, v, z + 1, 8:40] = adj_ref[v, z]
    rim[...] = blank

    for copy in adj_copies:
        copy.wait()
    ax_rows[...] = ax_recv[...].astype(f32)
    for i in range(20):
        v, z = i // 4, i % 4
        adj[0, v, z + 1, 6:8] = ax_rows[0, 2 * i : 2 * i + 2]
        adj[0, v, z + 1, 40:42] = ax_rows[1, 2 * i : 2 * i + 2]
    for begin in (0, 40):
        ends = jnp.zeros((8, 128), f32)
        for i in range(20):
            tile = adj[0, i // 4, i % 4 + 1, begin : begin + 8]
            ends = jnp.where(lane // 4 == i, pltpu.roll(tile, 4 * i + 2, 1), ends)
        own_cols[begin : begin + 8] = ends
    first = lane_wide % 4 >= 2
    rim[8:40] = jnp.where(first, ay_recv[0].astype(f32), ay_recv[1].astype(f32))
    near = (lane_full < 2) | (lane_full >= 126)

    def fill_rim(begin, end):
        part = rim[begin:end]
        for i in range(20):
            adj[1, i // 4, i % 4 + 1, begin:end] = jnp.where(
                near[begin:end], pltpu.roll(part, (126 - 4 * i) % 128, 1), 0.0
            )

    fill_rim(8, 40)

    for copy in column_copies:
        copy.wait()
    firsts, lasts = first_recv[...].astype(f32), last_recv[...].astype(f32)
    top = lax.broadcasted_iota(jnp.int32, (8, 640), 0) == 0
    joined = jnp.concatenate([firsts[0:8], jnp.where(top, firsts[8:16], lasts)], 0).T.astype(bf16)
    halo = [
        jnp.dot(
            joined,
            ay_ref[256 + 16 * i : 272 + 16 * i, (0 if i < 3 else 128) : 256],
            preferred_element_type=f32,
        )
        for i in range(5)
    ]
    mapped[:, 0:8] += halo[0][0:320].reshape(40, 8, 256)
    mapped[:, 8:16] += halo[0][320:640].reshape(40, 8, 256)
    mapped[:, 16:32] += halo[1].reshape(40, 16, 256)
    mapped[:, 32:48] += halo[2].reshape(40, 16, 256)
    mapped_y2[0:20, 0:32, 128:256] += halo[3].reshape(20, 32, 128)
    mapped_y2[20:40, 0:32, 128:256] += halo[4].reshape(20, 32, 128)

    for copy in row_copies:
        copy.wait()
    low_half, high_half = low_recv[...].astype(f32), high_recv[...].astype(f32)

    upper = lane >= 64
    row_kind = lax.broadcasted_iota(jnp.int32, (8, 128), 0)

    def doubled(half):
        turned = pltpu.roll(half, 64, 1).reshape(half.shape[0] // 8, 8, 128)
        half = half.reshape(turned.shape)
        return jnp.concatenate(
            [jnp.where(upper[None], turned, half), jnp.where(upper[None], half, turned)], 0
        )

    for half, bounds, target in (
        (low_half, (3, 5, 6), 48),
        (high_half[0:160], (4, 7, 8), 56),
    ):
        values = doubled(half)
        role = jnp.where(
            row_kind < bounds[0], 0, jnp.where(row_kind < bounds[1], 1, jnp.where(row_kind < bounds[2], 2, 3))
        )
        spot = jnp.where(upper, 1, 0)
        parts = [
            jnp.where((role == spot + 2 * i)[None], values, 0.0).reshape(320, 128) for i in range(2)
        ]
        total = jnp.dot(
            jnp.concatenate(parts, 1).astype(bf16), ay_ref[0:256], preferred_element_type=f32
        )
        mapped[:, target : target + 8] = total.reshape(40, 8, 256)
    more = doubled(high_half[160:208]).reshape(96, 128)[0:80, 0:64].astype(bf16)
    beyond = jnp.dot(more, ay_ref[192:256], preferred_element_type=f32)

    def from_corners(parts, role_of):
        width = parts.shape[2]
        row = lax.broadcasted_iota(jnp.int32, (8, width), 0)
        corners = jnp.where(row < 3, parts[0].astype(f32), parts[1].astype(f32))
        role = role_of(lax.broadcasted_iota(jnp.int32, (8, width), 1))
        stacked = jnp.concatenate([jnp.where(role == r, corners, 0.0) for r in range(4)], 0)
        return jnp.dot(stacked.T.astype(bf16), ay_ref[336:368], preferred_element_type=f32)

    def low_role(place):
        kind = place % 8
        return jnp.where(kind < 3, 0, jnp.where(kind < 5, 1, jnp.where(kind < 6, 2, 3)))

    def high_role(place):
        kind = place % 8
        inner = jnp.where(kind < 4, 0, jnp.where(kind < 7, 1, 2))
        return jnp.where(place < 320, inner, 3)

    for copy in corner_copies:
        copy.wait()
    from_low = from_corners(corner_low_recv, low_role)
    from_high = from_corners(corner_high_recv, high_role)
    mapped[:, 48:56] += from_low[0:320].reshape(40, 8, 256)
    mapped[:, 56:64] += from_high[0:320].reshape(40, 8, 256)
    beyond = beyond + from_high[320:400]
    for p in range(40):
        mapped_y2[p, 32:34] = beyond[2 * p : 2 * p + 2]
    for parts, at in ((corner_low_recv, 7), (corner_high_recv, 40)):
        rows = [parts[i, :, 0:128].astype(f32)[7:8] for i in range(2)]
        rim[at : at + 1] = jnp.where(first[0:1], rows[0], rows[1])
    fill_rim(0, 8)
    fill_rim(40, 48)
    adj_z = remote(12, adj.at[0, :, z_side + 1], adj.at[0, :, outer], z_other)
    adj_z.start()
    rim_turned[:, 0:48] = rim[...].T
    own_turned[:, 0:48] = own_cols[...].T

    def level_rows(kind, level, v, source, step, low_at, high_at):
        levels[kind, level, v, pl.ds(0, 4, stride=2)] = source[pl.ds(low_at, 4, stride=step)]
        levels[kind, level, v, pl.ds(1, 4, stride=2)] = source[pl.ds(high_at, 4, stride=step)]

    for v in range(5):
        for level, source, low_at, high_at in ((0, rim_turned, 1, 2), (1, rim_turned, 0, 3), (2, own_turned, 2, 1)):
            level_rows(0, level, v, source, 4, 16 * v + low_at, 16 * v + high_at)

    def synthesize(order, cv, carry):
        for z in order:
            p = cv * 4 + z
            exact = mapped[p]
            coarse_bits = exact.astype(bf16)
            rest = (exact - coarse_bits.astype(f32)).astype(bf16)
            whole = jnp.dot(
                small_ref[0:48],
                jnp.concatenate([coarse_bits, rest], axis=0),
                preferred_element_type=f32,
            )
            extra = mapped_y2[p]
            for t in range(2):
                at = slice(128 * t, 128 * t + 128)
                state[t, cv, z + 1, 0:8] = whole[0:8, at]
                state[t, cv, z + 1, 8:48] = whole[8:48, at] + extra[:, at]
        return carry

    def synthesize_sides(pair, carry):
        for j in range(5):
            synthesize((z_side,), 5 * pair + j, carry)
        return carry

    for cv in range(10):
        synthesize((z_side,), cv, 0)
    state_first = remote(13, state.at[0, 0:5, z_side + 1], state.at[0, 0:5, outer], z_other)
    state_second = remote(
        14, state.at[0, 5:10, z_side + 1, 8:40], state.at[0, 5:10, outer, 8:40], z_other
    )
    state_first.start()
    state_second.start()
    def synthesize_rest(pair, carry):
        for j in range(5):
            synthesize((gz, gz + 1, gz + 2), 5 * pair + j, carry)
        return carry

    lax.fori_loop(0, 2, synthesize_rest, 0)
    keep_bottom = jnp.where(gz > 0, 1.0, 0.0).astype(f32)

    def ahead(a, b):
        return pltpu.roll(jnp.where(lane == 0, b, a), 127, 1)

    def behind(a, b):
        return pltpu.roll(jnp.where(lane == 127, b, a), 1, 1)

    def x_face(t, base, source, z, r, start):
        low_at = slice(start + 8 * r, start + 8 + 8 * r)
        high_at = slice(start + 1 + 8 * r, start + 9 + 8 * r)
        mean = [
            (state[t, base + v, z + 1, low_at] + state[t, base + v, z + 1, high_at])
            for v in range(5)
        ]
        jump = [source[t, v, z + 1, high_at] - source[t, v, z + 1, low_at] for v in range(5)]
        below, above = face(mean, jump, 0)
        for v in range(5):
            gx_terms[0, t, v, 8 * r : 8 * r + 8] = below[v]
            gx_terms[1, t, v, 8 * r : 8 * r + 8] = above[v]

    def z_face(t, base, source, k, count, start):
        for r in range(count):
            at = slice(start + 8 * r, start + 8 + 8 * r)
            mean = [
                state[t, base + v, k, at] + state[t, base + v, k + 1, at] for v in range(5)
            ]
            jump = [source[t, v, k + 1, at] - source[t, v, k, at] for v in range(5)]
            below, above = face(mean, jump, 2, jnp.where(k == 0, keep_bottom, 1.0))
            for v in range(5):
                gz_terms[0, t, v, k, 8 * r : 8 * r + 8] = below[v]
                gz_terms[1, t, v, k, 8 * r : 8 * r + 8] = above[v]

    for k in range(1, 4):
        z_face(0, 0, adj, k, 5, 7)
    group = lane_full // 32
    for v in range(5):
        joint = state[1, v, 1]
        for z in range(1, 4):
            joint = jnp.where(group == z, state[1, v, z + 1], joint)
        turned[v, :, 0:48] = joint.T
    for v in range(5):
        for level, low_at, high_at in ((0, 9, 12), (1, 8, 13), (2, 10, 11)):
            level_rows(1, level, v, turned.at[v], 32, low_at, high_at)
    levels_copy = remote(16, levels.at[:, 0], levels_z, z_other)
    levels_copy.start()
    sublane8 = lax.broadcasted_iota(jnp.int32, (8, 128), 0)
    is_low = sublane8 % 2 == 0
    sign = jnp.where(is_low, 1.0, -1.0).astype(f32)

    def level(kind, which):
        return [levels[kind, which, v] for v in range(5)]

    rim_adj, rim_state = level(0, 0), level(1, 0)
    inner_adj, inner_state = level(0, 2), level(1, 2)
    lower, upper_share = face(
        [rim_state[v] + inner_state[v] for v in range(5)],
        [sign * (inner_adj[v] - rim_adj[v]) for v in range(5)],
        1,
    )
    for v in range(5):
        packed[8 * v : 8 * v + 8] = upper_share[v]
    inner_share = [jnp.where(is_low, lower[v], upper_share[v]) for v in range(5)]
    back = packed[...].T
    for i in range(20):
        v, z = i // 4, i % 4
        beside[v, z] = pltpu.roll(back[0:48], (128 - 8 * v - 2 * z) % 128, 1)
    outer_adj, outer_state = level(0, 1), level(1, 1)
    lower, upper_share = face(
        [rim_state[v] + outer_state[v] for v in range(5)],
        [sign * (rim_adj[v] - outer_adj[v]) for v in range(5)],
        1,
    )
    rim_middle = [
        rim_adj[v] + inner_share[v] + jnp.where(is_low, upper_share[v], lower[v]) for v in range(5)
    ]
    lower, upper_share = face(
        [rim_state[v] + pltpu.roll(rim_state[v], 127, 1) for v in range(5)],
        [pltpu.roll(rim_adj[v], 127, 1) - rim_adj[v] for v in range(5)],
        0,
    )
    for v in range(5):
        levels[0, 1, v] = rim_middle[v] + lower[v] + pltpu.roll(upper_share[v], 1, 1)
    adj_z.wait()
    state_first.wait()

    for k in (0, 4):
        z_face(0, 0, adj, k, 5, 7)
    mid_z = remote(15, mid.at[0, :, z_side + 1, 8:40], mid.at[0, :, outer, 8:40], z_other)

    def first_plane(j, carry):
        @pl.when(j == 1)
        def _():
            mid_z.start()

        z = jnp.where(gz > 0, j, 3 - j)
        for r in range(5):
            x_face(0, 0, adj, z, r, 6)
        for r in range(5):
            at, rows = slice(7 + 8 * r, 15 + 8 * r), slice(8 * r, 8 * r + 8)
            here = [state[0, v, z + 1, at] for v in range(5)]
            held = [adj[0, v, z + 1, at] for v in range(5)]
            below, above = face(
                [here[v] + ahead(here[v], state[1, v, z + 1, at]) for v in range(5)],
                [ahead(held[v], adj[1, v, z + 1, at]) - held[v] for v in range(5)],
                1,
            )
            for v in range(5):
                mid[0, v, z + 1, at] = (
                    held[v]
                    + below[v]
                    + jnp.where(lane == 0, beside[v, z, at], pltpu.roll(above[v], 1, 1))
                    + gx_terms[0, 0, v, 8 * r + 1 : 8 * r + 9]
                    + gx_terms[1, 0, v, rows]
                    + gz_terms[0, 0, v, z + 1, rows]
                    + gz_terms[1, 0, v, z, rows]
                )
        return carry

    lax.fori_loop(0, 4, first_plane, 0)
    levels_copy.wait()
    state_second.wait()
    for k in range(4):
        z_face(0, 5, mid, gz + k, 4, 8)
    up_part = jnp.where(gz > 0, 0.0, 1.0).astype(f32)
    down_part = 1.0 - up_part

    def next_plane(kind, v):
        tile = levels[kind, 0, v]
        from_other = levels_z[kind, v]
        return (
            jnp.where(sublane8 >= 6, up_part * pltpu.roll(from_other, 6, 0), pltpu.roll(tile, 6, 0)),
            jnp.where(sublane8 < 2, down_part * pltpu.roll(from_other, 2, 0), pltpu.roll(tile, 2, 0)),
        )

    rim_adj, rim_state = level(0, 0), level(1, 0)
    next_adj = [next_plane(0, v) for v in range(5)]
    next_state = [next_plane(1, v) for v in range(5)]
    lower, _ = face(
        [rim_state[v] + next_state[v][0] for v in range(5)],
        [next_adj[v][0] - rim_adj[v] for v in range(5)],
        2,
    )
    _, upper_share = face(
        [rim_state[v] + next_state[v][1] for v in range(5)],
        [rim_adj[v] - next_adj[v][1] for v in range(5)],
        2,
        jnp.where(sublane8 < 2, keep_bottom, 1.0),
    )
    for v in range(5):
        packed[8 * v : 8 * v + 8] = levels[0, 1, v] + lower[v] + upper_share[v]
    back = packed[...].T
    for i in range(20):
        v, z = i // 4, i % 4
        mid[1, v, z + 1, 8:40] = pltpu.roll(back[8:40], (127 - 8 * v - 2 * z) % 128, 1)

    def second_plane(j, carry):
        z = jnp.where(gz > 0, 3 - j, j)

        @pl.when(j == 3)
        def _():
            mid_z.wait()
            z_face(0, 5, mid, 4 - 4 * gz, 4, 8)

        for r in range(5):
            x_face(0, 5, mid, z, r, 7)
        for r in range(4):
            at, rows = slice(8 + 8 * r, 16 + 8 * r), slice(8 * r, 8 * r + 8)
            here = [state[0, 5 + v, z + 1, at] for v in range(5)]
            edge = [state[1, 5 + v, z + 1, at] for v in range(5)]
            held = [mid[0, v, z + 1, at] for v in range(5)]
            held_edge = [mid[1, v, z + 1, at] for v in range(5)]
            adj_up = [ahead(held[v], held_edge[v]) for v in range(5)]
            adj_down = [behind(held[v], held_edge[v]) for v in range(5)]
            below, _ = face(
                [here[v] + ahead(here[v], edge[v]) for v in range(5)],
                [adj_up[v] - held[v] for v in range(5)],
                1,
            )
            _, above = face(
                [here[v] + behind(here[v], edge[v]) for v in range(5)],
                [held[v] - adj_down[v] for v in range(5)],
                1,
            )
            for v in range(5):
                result[v, z, rows] = 0.5 * (
                    adj[0, v, z + 1, at]
                    + held[v]
                    + below[v]
                    + above[v]
                    + gx_terms[0, 0, v, 8 * r + 1 : 8 * r + 9]
                    + gx_terms[1, 0, v, rows]
                    + gz_terms[0, 0, v, z + 1, rows]
                    + gz_terms[1, 0, v, z, rows]
                )
        return carry

    lax.fori_loop(0, 4, second_plane, 0)


def shards(coarse, detail_x1, detail_y1, detail_x2, detail_y2, significance, adjoint):
    operands = [
        pltpu.with_memory_space_constraint(value, pltpu.HBM)
        for value in (
            coarse.reshape(320, 32),
            detail_x1.reshape(320, 32),
            detail_y1.reshape(640, 32),
            detail_x2.reshape(640, 64),
            detail_y2.reshape(1280, 64),
            significance,
            adjoint,
            jnp.asarray(y_matrices()),
            jnp.asarray(small_matrices()),
        )
    ]
    anywhere = pl.BlockSpec(memory_space=pl.ANY)
    return pl.pallas_call(
        kernel,
        out_shape=jax.ShapeDtypeStruct(adjoint.shape, f32),
        in_specs=[anywhere] * 9,
        out_specs=pl.BlockSpec(memory_space=pltpu.VMEM),
        scratch_shapes=[
            pltpu.VMEM((640, 32), bf16),
            pltpu.VMEM((640, 32), bf16),
            pltpu.VMEM((640, 64), bf16),
            pltpu.VMEM((1280, 64), bf16),
            pltpu.VMEM((2, 4, 4, 4), jnp.int32),
            pltpu.VMEM((5, 4, 32, 128), f32),
            pltpu.VMEM((368, 256), bf16),
            pltpu.VMEM((144, 128), bf16),
            pltpu.SemaphoreType.DMA((9,)),
            pltpu.VMEM((2, 4, 8, 64), f32),
            pltpu.VMEM((2, 4, 16, 64), f32),
            pltpu.VMEM((2, 4, 32, 64), f32),
            pltpu.VMEM((3200, 128), f32),
            pltpu.VMEM((96, 128), f32),
            pltpu.VMEM((16, 640), bf16),
            pltpu.VMEM((16, 640), bf16),
            pltpu.VMEM((8, 640), bf16),
            pltpu.VMEM((8, 640), bf16),
            pltpu.VMEM((160, 128), bf16),
            pltpu.VMEM((160, 128), bf16),
            pltpu.VMEM((208, 128), bf16),
            pltpu.VMEM((208, 128), bf16),
            pltpu.VMEM((8, 384), bf16),
            pltpu.VMEM((2, 8, 384), bf16),
            pltpu.VMEM((8, 512), bf16),
            pltpu.VMEM((2, 8, 512), bf16),
            pltpu.VMEM((2, 48, 128), f32),
            pltpu.VMEM((2, 48, 128), bf16),
            pltpu.VMEM((2, 48, 128), bf16),
            pltpu.VMEM((32, 128), bf16),
            pltpu.VMEM((2, 32, 128), bf16),
            pltpu.VMEM((48, 128), f32),
            pltpu.VMEM((40, 64, 256), f32),
            pltpu.VMEM((40, 40, 256), f32),
            pltpu.VMEM((2, 10, 6, 48, 128), f32),
            pltpu.VMEM((2, 5, 6, 48, 128), f32),
            pltpu.VMEM((2, 5, 6, 48, 128), f32),
            pltpu.VMEM((2, 1, 5, 48, 128), f32),
            pltpu.VMEM((2, 1, 5, 5, 40, 128), f32),
            pltpu.VMEM((48, 128), f32),
            pltpu.VMEM((5, 128, 128), f32),
            pltpu.VMEM((128, 128), f32),
            pltpu.VMEM((128, 128), f32),
            pltpu.VMEM((2, 3, 5, 8, 128), f32),
            pltpu.VMEM((2, 5, 8, 128), f32),
            pltpu.VMEM((128, 128), f32),
            pltpu.VMEM((5, 4, 48, 128), f32),
            pltpu.SemaphoreType.DMA((17,)),
            pltpu.SemaphoreType.DMA((17,)),
        ],
        compiler_params=pltpu.CompilerParams(collective_id=0, has_side_effects=True, vmem_limit_bytes=40*2**20),
    )(
        *operands,
    )


def solution(mesh):
    return jax.shard_map(
        shards,
        mesh=mesh,
        in_specs=(
            P(None, None, "gz", "gx", "gy"),
            P(None, None, "gz", "gx", "gy"),
            P(None, None, "gz", "gx", "gy"),
            P(None, None, "gz", "gx", "gy"),
            P(None, None, "gz", "gx", "gy"),
            P(None, "gz", "gx", "gy"),
            P(None, "gz", "gx", "gy"),
        ),
        out_specs=P(None, "gz", "gx", "gy"),
        check_vma=False,
    )
```

```python
import functools

import jax
import jax.numpy as jnp
import ml_dtypes
import numpy as np
from jax import lax
from jax.experimental import pallas as pl
from jax.experimental.pallas import tpu as pltpu
from jax.sharding import PartitionSpec as P

time_step = 0.1
viscosity = 0.2
heat_ratio_less_one = 0.4
f32 = jnp.float32
bf16 = jnp.bfloat16
MESH = pl.DeviceIdType.MESH


def predict(index):
    k = index // 2
    if index % 2 == 0:
        return {("c", k): 1.0}
    return {
        ("d", k): 1.0,
        ("c", k): 9 / 16,
        ("c", k + 1): 9 / 16,
        ("c", k - 1): -1 / 16,
        ("c", k + 2): -1 / 16,
    }


def predict_twice(index):
    whole = {}
    for (kind, k), weight in predict(index).items():
        if kind == "d":
            whole[("e", k)] = weight
            continue
        whole[("m", k)] = weight
        for key, inner in predict(k).items():
            whole[key] = whole.get(key, 0.0) + weight * inner
    return whole


def halo_row(kind, k):
    if kind == "c":
        return k - 32 if k >= 32 else 11 + k
    if kind == "d":
        return 3 if k >= 32 else 11
    if kind == "m":
        return 4 + k - 64 if k >= 64 else 14 + k
    return 7 if k >= 64 else 14


def y_matrices():
    own = np.zeros((4, 64, 256), np.float32)
    halo = np.zeros((5, 16, 256), np.float32)
    corner = np.zeros((4, 8, 256), np.float32)
    columns = [(y, y) for y in range(128)] + [(128, 128), (-1, 255)]
    for z in range(4):
        columns += [(y, 136 + 32 * z + j) for j, y in enumerate((-2, -1, 0, 127, 128, 129))]
    for y, column in columns:
        for (kind, k), weight in predict_twice(y).items():
            role = "cdme".index(kind)
            length = 32 if role < 2 else 64
            if 0 <= k < length:
                own[role, k, column] += weight
                continue
            row = halo_row(kind, k)
            halo[role, row, column] += weight
            if kind == "e":
                halo[4, row + 1, column] += weight
            if k >= length:
                corner[role, k - length, column] += weight
            else:
                corner[role, (5 if length == 32 else 7) + k, column] += weight
    finest = np.concatenate([halo[3, :, 128:], halo[4, :, 128:]], axis=1)
    parts = [own.reshape(256, 256), halo[0:3].reshape(48, 256), finest, corner.reshape(32, 256)]
    return (0.5 * np.concatenate(parts)).astype(ml_dtypes.bfloat16)


def small_matrices():
    mats = np.zeros((144, 128), np.float32)
    for x in range(-2, 34):
        row = x + 8
        for (kind, k), weight in predict_twice(x).items():
            if kind == "c":
                at = 50 + k if k < 0 else (k if k < 8 else 56 + k - 8)
            elif kind == "d":
                at = 50 if k < 0 else (8 + k if k < 8 else 59)
            elif kind == "m":
                at = 53 + k if k < 0 else (16 + k if k < 16 else 60 + k - 16)
            else:
                at = 53 if k < 0 else (32 + k if k < 16 else 63)
            mats[row, at] += weight
    mats[6, 54] = 1.0
    mats[7, 55] = 1.0
    mats[0:48, 64:128] = mats[0:48, 0:64]
    picks = mats[48:128].reshape(5, 16, 128)
    for row, column in ((0, 0), (1, 1), (2, 2), (9, 30), (10, 31)):
        picks[0, row, column] = 1.0
    for row, column in ((3, 0), (11, 31)):
        picks[1, row, column] = 1.0
    for row, column in ((4, 0), (5, 1), (6, 2), (12, 62), (13, 63)):
        picks[2, row, column] = 1.0
    for row, column in ((7, 0), (14, 63)):
        picks[3, row, column] = 1.0
        picks[4, row + 1, column] = 1.0
    for row, column in ((0, 0), (1, 1), (2, 2), (3, 30), (4, 31), (5, 62), (6, 63)):
        mats[128 + row, column] = 1.0
    return mats.astype(ml_dtypes.bfloat16)


def face(mean, jump, k, factor=None):
    q, u, t = mean[0], mean[1:4], mean[4]
    rho = (0.5 * time_step) * jnp.exp(0.5 * q)
    if factor is not None:
        rho = rho * factor
    speed = u[k]
    half_square = 0.5 * (u[0] * u[0] + u[1] * u[1] + u[2] * u[2])
    enthalpy = (1.0 / heat_ratio_less_one + 1.0) * t + half_square
    inner = jump[0] + jump[1] * u[0] + jump[2] * u[1] + jump[3] * u[2] + jump[4] * enthalpy
    flow = rho * speed
    push = rho * jump[1 + k]
    grads = [flow * (jump[1 + j] + jump[4] * u[j]) for j in range(3)]
    grads[k] = grads[k] + rho * inner
    dq = 0.5 * (flow * inner + t * push)
    dt = push + (1.0 / heat_ratio_less_one + 1.0) * (flow * jump[4])
    terms = [dq] + grads + [dt]
    spread = [(viscosity * time_step) * jump[v] for v in range(5)]
    return [terms[v] + spread[v] for v in range(5)], [terms[v] - spread[v] for v in range(5)]


def kernel(
    c_in, x1_in, y1_in, x2_in, y2_in, sig_in, adj_in, ay_in, small_in,
    result,
    cx_ref, y1_ref, x2_ref, y2_ref, sig_ref, adj_ref, ay_ref, small_ref,
    load_sem,
    tiles, mask_x, mask_y, ext, hy2,
    first_send, first_recv, last_send, last_recv, low_send, low_recv, high_send, high_recv,
    corner_low, corner_low_recv, corner_high, corner_high_recv,
    ax_rows, ax_send, ax_recv, ay_send, ay_recv, rim,
    mapped, mapped_y2, state, adj, mid, gx_terms, gz_terms,
    own_cols, turned, rim_turned, own_turned, levels, levels_z, packed, beside, mid_rim,
    send_sem, recv_sem,
):
    gx, gy, gz = lax.axis_index("gx"), lax.axis_index("gy"), lax.axis_index("gz")
    nx, ny = lax.axis_size("gx"), lax.axis_size("gy")
    up_x, down_x = lax.rem(gx + 1, nx), lax.rem(gx + nx - 1, nx)
    up_y, down_y = lax.rem(gy + 1, ny), lax.rem(gy + ny - 1, ny)
    x_up, x_down = {"gx": up_x}, {"gx": down_x}
    y_up, y_down = {"gy": up_y}, {"gy": down_y}
    diagonal = (
        {"gx": up_x, "gy": down_y},
        {"gx": up_x, "gy": up_y},
        {"gx": down_x, "gy": down_y},
        {"gx": down_x, "gy": up_y},
    )
    z_other = {"gz": 1 - gz}
    barrier = pltpu.get_barrier_semaphore()
    for peer in (x_up, x_down, y_up, y_down, z_other) + diagonal:
        pl.semaphore_signal(barrier, inc=1, device_id=peer, device_id_type=MESH)

    pairs = (
        (sig_in, sig_ref), (x2_in, x2_ref), (y2_in, y2_ref), (c_in, cx_ref.at[0:320]),
        (x1_in, cx_ref.at[320:640]), (y1_in, y1_ref), (small_in, small_ref), (adj_in, adj_ref),
        (ay_in, ay_ref),
    )
    loads = [
        pltpu.make_async_copy(source, target, load_sem.at[i])
        for i, (source, target) in enumerate(pairs)
    ]
    for load in loads:
        load.start()

    def remote(index, source, target, peer):
        return pltpu.make_async_remote_copy(
            src_ref=source,
            dst_ref=target,
            send_sem=send_sem.at[index],
            recv_sem=recv_sem.at[index],
            device_id=peer,
            device_id_type=MESH,
        )

    def transposed(left, right):
        return lax.dot_general(left, right, (((1,), (1,)), ((), ())), preferred_element_type=f32)

    lane = lax.broadcasted_iota(jnp.int32, (8, 128), 1)
    lane_wide = lax.broadcasted_iota(jnp.int32, (32, 128), 1)
    lane_full = lax.broadcasted_iota(jnp.int32, (48, 128), 1)

    for load in loads[:8]:
        load.wait()
    lane_tile = lax.broadcasted_iota(jnp.int32, (4, 64), 1) // 16
    row_half = lax.broadcasted_iota(jnp.int32, (8, 64), 0) < 4
    for c in range(2):
        for z in range(4):
            flags = sig_ref[c, z].astype(f32)
            wide = jnp.zeros((4, 64), f32)
            for t in range(4):
                wide = jnp.where(lane_tile == t, flags[:, t : t + 1], wide)
            tiles[c, z, 0:4] = wide
            each = [jnp.broadcast_to(tiles[c, z, t : t + 1], (8, 64)) for t in range(4)]
            for t in range(4):
                mask_y[c, z, 8 * t : 8 * t + 8] = each[t]
            for t in range(2):
                mask_x[c, z, 8 * t : 8 * t + 8] = jnp.where(row_half, each[2 * t], each[2 * t + 1])

    kept_x2 = x2_ref[...].astype(f32).reshape(2, 5, 4, 16, 64) * mask_x[...][:, None]
    kept_y2 = y2_ref[...].astype(f32).reshape(2, 5, 4, 32, 64) * mask_y[...][:, None]
    ext[...] = jnp.zeros_like(ext)
    ext[0:640, 0:32] = cx_ref[...].astype(f32)
    ext[640:1280, 0:32] = y1_ref[...].astype(f32)
    ext[1280:1920, 0:64] = kept_x2.reshape(640, 64)
    ext[1920:3200, 0:64] = kept_y2.reshape(1280, 64)

    def own(begin, end):
        return ext[begin:end, 0:64].astype(bf16)

    starts = (0, 640, 1280, 1920, 2560)
    cols = jnp.zeros((16, 640), f32)
    for which, begin in enumerate(starts):
        pick = small_ref[48 + 16 * which : 64 + 16 * which, 0:64]
        cols = cols + transposed(pick, own(begin, begin + 640))
    first_send[...] = cols.astype(bf16)
    last_send[...] = cols[8:16].astype(bf16)

    coarse_e = ext[0:320].reshape(40, 8, 128)
    x1_e = ext[320:640].reshape(40, 8, 128)
    y1_e = ext[640:1280].reshape(40, 16, 128)
    x2_e = ext[1280:1920].reshape(40, 16, 128)
    y2_e = ext[1920:3200].reshape(40, 32, 128)
    low = jnp.concatenate(
        [coarse_e[:, 6:8], x1_e[:, 7:8], y1_e[:, 14:16], x2_e[:, 15:16], y2_e[:, 30:32]], 1
    ).reshape(320, 128)
    high = jnp.concatenate(
        [coarse_e[:, 0:3], x1_e[:, 0:1], y1_e[:, 0:3], x2_e[:, 0:1]], 1
    ).reshape(320, 128)
    hy2[80:96] = jnp.zeros((16, 128), f32)
    for p in range(40):
        hy2[2 * p : 2 * p + 2] = ext[1920 + 32 * p : 1922 + 32 * p]
    more = hy2[0:48] + pltpu.roll(hy2[48:96], 64, 1)
    low_send[...] = (low[0:160] + pltpu.roll(low[160:320], 64, 1)).astype(bf16)
    high_send[0:160] = (high[0:160] + pltpu.roll(high[160:320], 64, 1)).astype(bf16)
    high_send[160:208] = more.astype(bf16)
    columns = jnp.zeros((32, 128), f32)
    for i in range(20):
        plane = adj_ref[i // 4, i % 4]
        columns = jnp.where(lane_wide // 4 == i, pltpu.roll(plane, 4 * i + 2, 1), columns)
        ax_rows[0, 2 * i : 2 * i + 2] = plane[0:2]
        ax_rows[1, 2 * i : 2 * i + 2] = plane[30:32]
    ax_rows[:, 40:48] = jnp.zeros((2, 8, 128), f32)
    ax_send[...] = ax_rows[...].astype(bf16)
    ay_send[...] = columns.astype(bf16)
    own_cols[8:40] = columns

    last_row = lax.broadcasted_iota(jnp.int32, (8, 128), 0) == 7
    for target, pieces, row in (
        (corner_low, (low, jnp.zeros((64, 128), f32)), columns[31:32]),
        (corner_high, (high, hy2[0:80], jnp.zeros((112, 128), f32)), columns[0:1]),
    ):
        rows = jnp.concatenate(pieces, 0)[:, 0:64].astype(bf16)
        picked = transposed(small_ref[128:144, 0:64], rows)[0:8]
        target[:, 0:128] = jnp.where(last_row, row, picked[:, 0:128]).astype(bf16)
        target[:, 128:] = picked[:, 128:].astype(bf16)

    pl.semaphore_wait(barrier, 9)
    corner_copies = [remote(4 + i, corner_low, corner_low_recv.at[i], diagonal[i]) for i in range(2)]
    corner_copies += [
        remote(6 + i, corner_high, corner_high_recv.at[i], diagonal[2 + i]) for i in range(2)
    ]
    column_copies = [remote(0, first_send, first_recv, y_down), remote(1, last_send, last_recv, y_up)]
    row_copies = [remote(2, low_send, low_recv, x_up), remote(3, high_send, high_recv, x_down)]
    adj_copies = [
        remote(8, ay_send, ay_recv.at[0], y_down),
        remote(9, ay_send, ay_recv.at[1], y_up),
        remote(10, ax_send.at[0], ax_recv.at[1], x_down),
        remote(11, ax_send.at[1], ax_recv.at[0], x_up),
    ]
    for copy in corner_copies + column_copies + adj_copies + row_copies:
        copy.start()

    loads[8].wait()
    for begin, count, role, target, at in (
        (0, 8, 0, mapped, 0),
        (320, 8, 0, mapped, 8),
        (640, 16, 1, mapped, 16),
        (1280, 16, 2, mapped, 32),
        (1920, 32, 3, mapped_y2, 0),
    ):
        product = jnp.dot(
            own(begin, begin + 40 * count),
            ay_ref[64 * role : 64 * role + 64],
            preferred_element_type=f32,
        )
        target[:, at : at + count] = product.reshape(40, count, 256)
    mapped_y2[:, 32:40] = jnp.zeros((40, 8, 256), f32)

    outer = 5 * gz
    z_side = 3 - 3 * gz
    blank = jnp.zeros((48, 128), f32)
    for t in range(2):
        for v in range(5):
            adj[t, v, outer] = blank
            mid[t, v, outer] = blank
        for cv in range(10):
            state[t, cv, outer] = blank
    for i in range(20):
        v, z = i // 4, i % 4
        adj[0, v, z + 1, 0:8] = blank[0:8]
        adj[0, v, z + 1, 40:48] = blank[0:8]
        adj[0, v, z + 1, 8:40] = adj_ref[v, z]
    rim[...] = blank

    for copy in adj_copies:
        copy.wait()
    ax_rows[...] = ax_recv[...].astype(f32)
    for i in range(20):
        v, z = i // 4, i % 4
        adj[0, v, z + 1, 6:8] = ax_rows[0, 2 * i : 2 * i + 2]
        adj[0, v, z + 1, 40:42] = ax_rows[1, 2 * i : 2 * i + 2]
    for begin in (0, 40):
        ends = jnp.zeros((8, 128), f32)
        for i in range(20):
            tile = adj[0, i // 4, i % 4 + 1, begin : begin + 8]
            ends = jnp.where(lane // 4 == i, pltpu.roll(tile, 4 * i + 2, 1), ends)
        own_cols[begin : begin + 8] = ends
    first = lane_wide % 4 >= 2
    rim[8:40] = jnp.where(first, ay_recv[0].astype(f32), ay_recv[1].astype(f32))
    near = (lane_full < 2) | (lane_full >= 126)

    def fill_rim(begin, end):
        part = rim[begin:end]
        for i in range(20):
            adj[1, i // 4, i % 4 + 1, begin:end] = jnp.where(
                near[begin:end], pltpu.roll(part, (126 - 4 * i) % 128, 1), 0.0
            )

    fill_rim(8, 40)

    for copy in column_copies:
        copy.wait()
    firsts, lasts = first_recv[...].astype(f32), last_recv[...].astype(f32)
    top = lax.broadcasted_iota(jnp.int32, (8, 640), 0) == 0
    joined = jnp.concatenate([firsts[0:8], jnp.where(top, firsts[8:16], lasts)], 0).T.astype(bf16)
    halo = [
        jnp.dot(joined, ay_ref[256 + 16 * i : 272 + 16 * i], preferred_element_type=f32)
        for i in range(4)
    ]
    mapped[:, 0:8] += halo[0][0:320].reshape(40, 8, 256)
    mapped[:, 8:16] += halo[0][320:640].reshape(40, 8, 256)
    mapped[:, 16:32] += halo[1].reshape(40, 16, 256)
    mapped[:, 32:48] += halo[2].reshape(40, 16, 256)
    mapped_y2[0:20, 0:32, 128:256] += halo[3][:, 0:128].reshape(20, 32, 128)
    mapped_y2[20:40, 0:32, 128:256] += halo[3][:, 128:256].reshape(20, 32, 128)

    for copy in row_copies:
        copy.wait()
    low_half, high_half = low_recv[...].astype(f32), high_recv[...].astype(f32)

    upper = lane >= 64
    row_kind = lax.broadcasted_iota(jnp.int32, (8, 128), 0)

    def doubled(half):
        turned = pltpu.roll(half, 64, 1).reshape(half.shape[0] // 8, 8, 128)
        half = half.reshape(turned.shape)
        return jnp.concatenate(
            [jnp.where(upper[None], turned, half), jnp.where(upper[None], half, turned)], 0
        )

    for half, bounds, target in (
        (low_half, (3, 5, 6), 48),
        (high_half[0:160], (4, 7, 8), 56),
    ):
        values = doubled(half)
        role = jnp.where(
            row_kind < bounds[0], 0, jnp.where(row_kind < bounds[1], 1, jnp.where(row_kind < bounds[2], 2, 3))
        )
        spot = jnp.where(upper, 1, 0)
        parts = [
            jnp.where((role == spot + 2 * i)[None], values, 0.0).reshape(320, 128) for i in range(2)
        ]
        total = jnp.dot(
            jnp.concatenate(parts, 1).astype(bf16), ay_ref[0:256], preferred_element_type=f32
        )
        mapped[:, target : target + 8] = total.reshape(40, 8, 256)
    more = doubled(high_half[160:208]).reshape(96, 128)[0:80, 0:64].astype(bf16)
    beyond = jnp.dot(more, ay_ref[192:256], preferred_element_type=f32)

    def from_corners(parts, role_of):
        width = parts.shape[2]
        row = lax.broadcasted_iota(jnp.int32, (8, width), 0)
        corners = jnp.where(row < 3, parts[0].astype(f32), parts[1].astype(f32))
        role = role_of(lax.broadcasted_iota(jnp.int32, (8, width), 1))
        stacked = jnp.concatenate([jnp.where(role == r, corners, 0.0) for r in range(4)], 0)
        return jnp.dot(stacked.T.astype(bf16), ay_ref[320:352], preferred_element_type=f32)

    def low_role(place):
        kind = place % 8
        return jnp.where(kind < 3, 0, jnp.where(kind < 5, 1, jnp.where(kind < 6, 2, 3)))

    def high_role(place):
        kind = place % 8
        inner = jnp.where(kind < 4, 0, jnp.where(kind < 7, 1, 2))
        return jnp.where(place < 320, inner, 3)

    for copy in corner_copies:
        copy.wait()
    from_low = from_corners(corner_low_recv, low_role)
    from_high = from_corners(corner_high_recv, high_role)
    mapped[:, 48:56] += from_low[0:320].reshape(40, 8, 256)
    mapped[:, 56:64] += from_high[0:320].reshape(40, 8, 256)
    beyond = beyond + from_high[320:400]
    for p in range(40):
        mapped_y2[p, 32:34] = beyond[2 * p : 2 * p + 2]
    for parts, at in ((corner_low_recv, 7), (corner_high_recv, 40)):
        rows = [parts[i, :, 0:128].astype(f32)[7:8] for i in range(2)]
        rim[at : at + 1] = jnp.where(first[0:1], rows[0], rows[1])
    fill_rim(0, 8)
    fill_rim(40, 48)
    adj_z = remote(12, adj.at[0, :, z_side + 1], adj.at[0, :, outer], z_other)
    adj_z.start()
    rim_turned[:, 0:48] = rim[...].T
    own_turned[:, 0:48] = own_cols[...].T

    def level_rows(kind, level, v, source, step, low_at, high_at):
        levels[kind, level, v, pl.ds(0, 4, stride=2)] = source[pl.ds(low_at, 4, stride=step)]
        levels[kind, level, v, pl.ds(1, 4, stride=2)] = source[pl.ds(high_at, 4, stride=step)]

    for v in range(5):
        for level, source, low_at, high_at in ((0, rim_turned, 1, 2), (1, rim_turned, 0, 3), (2, own_turned, 2, 1)):
            level_rows(0, level, v, source, 4, 16 * v + low_at, 16 * v + high_at)

    def synthesize(order, cv, carry):
        for z in order:
            p = cv * 4 + z
            exact = mapped[p]
            coarse_bits = exact.astype(bf16)
            rest = (exact - coarse_bits.astype(f32)).astype(bf16)
            whole = jnp.dot(
                small_ref[0:48],
                jnp.concatenate([coarse_bits, rest], axis=0),
                preferred_element_type=f32,
            )
            extra = mapped_y2[p]
            for t in range(2):
                at = slice(128 * t, 128 * t + 128)
                state[t, cv, z + 1, 0:8] = whole[0:8, at]
                state[t, cv, z + 1, 8:48] = whole[8:48, at] + extra[:, at]
        return carry

    def synthesize_sides(pair, carry):
        for j in range(5):
            synthesize((z_side,), 5 * pair + j, carry)
        return carry

    for cv in range(10):
        synthesize((z_side,), cv, 0)
    state_first = remote(13, state.at[0, 0:5, z_side + 1], state.at[0, 0:5, outer], z_other)
    state_second = remote(
        14, state.at[0, 5:10, z_side + 1, 8:40], state.at[0, 5:10, outer, 8:40], z_other
    )
    state_first.start()
    state_second.start()
    def synthesize_rest(pair, carry):
        for j in range(5):
            synthesize((gz, gz + 1, gz + 2), 5 * pair + j, carry)
        return carry

    for pair in range(2):
        synthesize_rest(pair, 0)
    keep_bottom = jnp.where(gz > 0, 1.0, 0.0).astype(f32)

    def ahead(a, b):
        return pltpu.roll(jnp.where(lane == 0, b, a), 127, 1)

    def behind(a, b):
        return pltpu.roll(jnp.where(lane == 127, b, a), 1, 1)

    def x_face(t, base, source, z, r, start):
        low_at = slice(start + 8 * r, start + 8 + 8 * r)
        high_at = slice(start + 1 + 8 * r, start + 9 + 8 * r)
        mean = [
            (state[t, base + v, z + 1, low_at] + state[t, base + v, z + 1, high_at])
            for v in range(5)
        ]
        jump = [source[t, v, z + 1, high_at] - source[t, v, z + 1, low_at] for v in range(5)]
        below, above = face(mean, jump, 0)
        for v in range(5):
            gx_terms[0, t, v, 8 * r : 8 * r + 8] = below[v]
            gx_terms[1, t, v, 8 * r : 8 * r + 8] = above[v]

    def z_face(t, base, source, k, count, start):
        for r in range(count):
            at = slice(start + 8 * r, start + 8 + 8 * r)
            mean = [
                state[t, base + v, k, at] + state[t, base + v, k + 1, at] for v in range(5)
            ]
            jump = [source[t, v, k + 1, at] - source[t, v, k, at] for v in range(5)]
            below, above = face(mean, jump, 2, jnp.where(k == 0, keep_bottom, 1.0))
            for v in range(5):
                gz_terms[0, t, v, k, 8 * r : 8 * r + 8] = below[v]
                gz_terms[1, t, v, k, 8 * r : 8 * r + 8] = above[v]

    group = lane_full // 32
    for v in range(5):
        joint = state[1, v, 1]
        for z in range(1, 4):
            joint = jnp.where(group == z, state[1, v, z + 1], joint)
        turned[v, :, 0:48] = joint.T
    for v in range(5):
        for level, low_at, high_at in ((0, 9, 12), (1, 8, 13), (2, 10, 11)):
            level_rows(1, level, v, turned.at[v], 32, low_at, high_at)
    levels_copy = remote(16, levels.at[:, 0], levels_z, z_other)
    levels_copy.start()
    sublane8 = lax.broadcasted_iota(jnp.int32, (8, 128), 0)
    is_low = sublane8 % 2 == 0
    sign = jnp.where(is_low, 1.0, -1.0).astype(f32)

    def level(kind, which):
        return [levels[kind, which, v] for v in range(5)]

    rim_adj, rim_state = level(0, 0), level(1, 0)
    inner_adj, inner_state = level(0, 2), level(1, 2)
    lower, upper_share = face(
        [rim_state[v] + inner_state[v] for v in range(5)],
        [sign * (inner_adj[v] - rim_adj[v]) for v in range(5)],
        1,
    )
    for v in range(5):
        packed[8 * v : 8 * v + 8] = upper_share[v]
    inner_share = [jnp.where(is_low, lower[v], upper_share[v]) for v in range(5)]
    back = packed[...].T
    for i in range(20):
        v, z = i // 4, i % 4
        beside[v, z] = pltpu.roll(back[0:48], (128 - 8 * v - 2 * z) % 128, 1)
    outer_adj, outer_state = level(0, 1), level(1, 1)
    lower, upper_share = face(
        [rim_state[v] + outer_state[v] for v in range(5)],
        [sign * (rim_adj[v] - outer_adj[v]) for v in range(5)],
        1,
    )
    rim_middle = [
        rim_adj[v] + inner_share[v] + jnp.where(is_low, upper_share[v], lower[v]) for v in range(5)
    ]
    lower, upper_share = face(
        [rim_state[v] + pltpu.roll(rim_state[v], 127, 1) for v in range(5)],
        [pltpu.roll(rim_adj[v], 127, 1) - rim_adj[v] for v in range(5)],
        0,
    )
    for v in range(5):
        levels[0, 1, v] = rim_middle[v] + lower[v] + pltpu.roll(upper_share[v], 1, 1)
    for k in range(1, 4):
        z_face(0, 0, adj, k, 5, 7)
    adj_z.wait()
    state_first.wait()

    for k in (0, 4):
        z_face(0, 0, adj, k, 5, 7)
    mid_z = remote(15, mid.at[0, :, z_side + 1, 8:40], mid.at[0, :, outer, 8:40], z_other)

    def first_plane(j, carry):
        @pl.when(j == 1)
        def _():
            mid_z.start()

        z = jnp.where(gz > 0, j, 3 - j)
        for r in range(5):
            x_face(0, 0, adj, z, r, 6)
        for r in range(5):
            at, rows = slice(7 + 8 * r, 15 + 8 * r), slice(8 * r, 8 * r + 8)
            here = [state[0, v, z + 1, at] for v in range(5)]
            held = [adj[0, v, z + 1, at] for v in range(5)]
            below, above = face(
                [here[v] + ahead(here[v], state[1, v, z + 1, at]) for v in range(5)],
                [ahead(held[v], adj[1, v, z + 1, at]) - held[v] for v in range(5)],
                1,
            )
            for v in range(5):
                mid[0, v, z + 1, at] = (
                    held[v]
                    + below[v]
                    + jnp.where(lane == 0, beside[v, z, at], pltpu.roll(above[v], 1, 1))
                    + gx_terms[0, 0, v, 8 * r + 1 : 8 * r + 9]
                    + gx_terms[1, 0, v, rows]
                    + gz_terms[0, 0, v, z + 1, rows]
                    + gz_terms[1, 0, v, z, rows]
                )
        return carry

    lax.fori_loop(0, 4, first_plane, 0)
    levels_copy.wait()
    state_second.wait()
    up_part = jnp.where(gz > 0, 0.0, 1.0).astype(f32)
    down_part = 1.0 - up_part

    def next_plane(kind, v):
        tile = levels[kind, 0, v]
        from_other = levels_z[kind, v]
        return (
            jnp.where(sublane8 >= 6, up_part * pltpu.roll(from_other, 6, 0), pltpu.roll(tile, 6, 0)),
            jnp.where(sublane8 < 2, down_part * pltpu.roll(from_other, 2, 0), pltpu.roll(tile, 2, 0)),
        )

    rim_adj, rim_state = level(0, 0), level(1, 0)
    next_adj = [next_plane(0, v) for v in range(5)]
    next_state = [next_plane(1, v) for v in range(5)]
    lower, _ = face(
        [rim_state[v] + next_state[v][0] for v in range(5)],
        [next_adj[v][0] - rim_adj[v] for v in range(5)],
        2,
    )
    _, upper_share = face(
        [rim_state[v] + next_state[v][1] for v in range(5)],
        [rim_adj[v] - next_adj[v][1] for v in range(5)],
        2,
        jnp.where(sublane8 < 2, keep_bottom, 1.0),
    )
    for v in range(5):
        packed[8 * v : 8 * v + 8] = levels[0, 1, v] + lower[v] + upper_share[v]
    back = packed[...].T
    for i in range(20):
        v, z = i // 4, i % 4
        mid_rim[v, z, :] = pltpu.roll(back[8:40], (127 - 8 * v - 2 * z) % 128, 1)
    for k in range(4):
        z_face(0, 5, mid, gz + k, 4, 8)

    def second_plane(j, carry):
        z = jnp.where(gz > 0, 3 - j, j)

        @pl.when(j == 3)
        def _():
            mid_z.wait()
            z_face(0, 5, mid, 4 - 4 * gz, 4, 8)

        for r in range(5):
            x_face(0, 5, mid, z, r, 7)
        for r in range(4):
            at, rows = slice(8 + 8 * r, 16 + 8 * r), slice(8 * r, 8 * r + 8)
            here = [state[0, 5 + v, z + 1, at] for v in range(5)]
            edge = [state[1, 5 + v, z + 1, at] for v in range(5)]
            held = [mid[0, v, z + 1, at] for v in range(5)]
            held_edge = [mid_rim[v, z, rows] for v in range(5)]
            adj_up = [ahead(held[v], held_edge[v]) for v in range(5)]
            adj_down = [behind(held[v], held_edge[v]) for v in range(5)]
            below, _ = face(
                [here[v] + ahead(here[v], edge[v]) for v in range(5)],
                [adj_up[v] - held[v] for v in range(5)],
                1,
            )
            _, above = face(
                [here[v] + behind(here[v], edge[v]) for v in range(5)],
                [held[v] - adj_down[v] for v in range(5)],
                1,
            )
            for v in range(5):
                result[v, z, rows] = 0.5 * (
                    adj[0, v, z + 1, at]
                    + held[v]
                    + below[v]
                    + above[v]
                    + gx_terms[0, 0, v, 8 * r + 1 : 8 * r + 9]
                    + gx_terms[1, 0, v, rows]
                    + gz_terms[0, 0, v, z + 1, rows]
                    + gz_terms[1, 0, v, z, rows]
                )
        return carry

    lax.fori_loop(0, 4, second_plane, 0)


def shards(coarse, detail_x1, detail_y1, detail_x2, detail_y2, significance, adjoint):
    operands = [
        pltpu.with_memory_space_constraint(value, pltpu.HBM)
        for value in (
            coarse.reshape(320, 32),
            detail_x1.reshape(320, 32),
            detail_y1.reshape(640, 32),
            detail_x2.reshape(640, 64),
            detail_y2.reshape(1280, 64),
            significance,
            adjoint,
            jnp.asarray(y_matrices()),
            jnp.asarray(small_matrices()),
        )
    ]
    anywhere = pl.BlockSpec(memory_space=pl.ANY)
    return pl.pallas_call(
        kernel,
        out_shape=jax.ShapeDtypeStruct(adjoint.shape, f32),
        in_specs=[anywhere] * 9,
        out_specs=pl.BlockSpec(memory_space=pltpu.VMEM),
        scratch_shapes=[
            pltpu.VMEM((640, 32), bf16),
            pltpu.VMEM((640, 32), bf16),
            pltpu.VMEM((640, 64), bf16),
            pltpu.VMEM((1280, 64), bf16),
            pltpu.VMEM((2, 4, 4, 4), jnp.int32),
            pltpu.VMEM((5, 4, 32, 128), f32),
            pltpu.VMEM((352, 256), bf16),
            pltpu.VMEM((144, 128), bf16),
            pltpu.SemaphoreType.DMA((9,)),
            pltpu.VMEM((2, 4, 8, 64), f32),
            pltpu.VMEM((2, 4, 16, 64), f32),
            pltpu.VMEM((2, 4, 32, 64), f32),
            pltpu.VMEM((3200, 128), f32),
            pltpu.VMEM((96, 128), f32),
            pltpu.VMEM((16, 640), bf16),
            pltpu.VMEM((16, 640), bf16),
            pltpu.VMEM((8, 640), bf16),
            pltpu.VMEM((8, 640), bf16),
            pltpu.VMEM((160, 128), bf16),
            pltpu.VMEM((160, 128), bf16),
            pltpu.VMEM((208, 128), bf16),
            pltpu.VMEM((208, 128), bf16),
            pltpu.VMEM((8, 384), bf16),
            pltpu.VMEM((2, 8, 384), bf16),
            pltpu.VMEM((8, 512), bf16),
            pltpu.VMEM((2, 8, 512), bf16),
            pltpu.VMEM((2, 48, 128), f32),
            pltpu.VMEM((2, 48, 128), bf16),
            pltpu.VMEM((2, 48, 128), bf16),
            pltpu.VMEM((32, 128), bf16),
            pltpu.VMEM((2, 32, 128), bf16),
            pltpu.VMEM((48, 128), f32),
            pltpu.VMEM((40, 64, 256), f32),
            pltpu.VMEM((40, 40, 256), f32),
            pltpu.VMEM((2, 10, 6, 48, 128), f32),
            pltpu.VMEM((2, 5, 6, 48, 128), f32),
            pltpu.VMEM((2, 5, 6, 48, 128), f32),
            pltpu.VMEM((2, 1, 5, 48, 128), f32),
            pltpu.VMEM((2, 1, 5, 5, 40, 128), f32),
            pltpu.VMEM((48, 128), f32),
            pltpu.VMEM((5, 128, 128), f32),
            pltpu.VMEM((128, 128), f32),
            pltpu.VMEM((128, 128), f32),
            pltpu.VMEM((2, 3, 5, 8, 128), f32),
            pltpu.VMEM((2, 5, 8, 128), f32),
            pltpu.VMEM((128, 128), f32),
            pltpu.VMEM((5, 4, 48, 128), f32),
            pltpu.VMEM((5, 4, 32, 128), f32),
            pltpu.SemaphoreType.DMA((17,)),
            pltpu.SemaphoreType.DMA((17,)),
        ],
        compiler_params=pltpu.CompilerParams(collective_id=0, has_side_effects=True, vmem_limit_bytes=40*2**20),
    )(
        *operands,
    )


def solution(mesh):
    return jax.shard_map(
        shards,
        mesh=mesh,
        in_specs=(
            P(None, None, "gz", "gx", "gy"),
            P(None, None, "gz", "gx", "gy"),
            P(None, None, "gz", "gx", "gy"),
            P(None, None, "gz", "gx", "gy"),
            P(None, None, "gz", "gx", "gy"),
            P(None, "gz", "gx", "gy"),
            P(None, "gz", "gx", "gy"),
        ),
        out_specs=P(None, "gz", "gx", "gy"),
        check_vma=False,
    )
```

```python
import functools

import jax
import jax.numpy as jnp
import ml_dtypes
import numpy as np
from jax import lax
from jax.experimental import pallas as pl
from jax.experimental.pallas import tpu as pltpu
from jax.sharding import PartitionSpec as P

time_step = 0.1
viscosity = 0.2
heat_ratio_less_one = 0.4
f32 = jnp.float32
bf16 = jnp.bfloat16
MESH = pl.DeviceIdType.MESH


def predict(index):
    k = index // 2
    if index % 2 == 0:
        return {("c", k): 1.0}
    return {
        ("d", k): 1.0,
        ("c", k): 9 / 16,
        ("c", k + 1): 9 / 16,
        ("c", k - 1): -1 / 16,
        ("c", k + 2): -1 / 16,
    }


def predict_twice(index):
    whole = {}
    for (kind, k), weight in predict(index).items():
        if kind == "d":
            whole[("e", k)] = weight
            continue
        whole[("m", k)] = weight
        for key, inner in predict(k).items():
            whole[key] = whole.get(key, 0.0) + weight * inner
    return whole


def halo_row(kind, k):
    if kind == "c":
        return k - 32 if k >= 32 else 11 + k
    if kind == "d":
        return 3 if k >= 32 else 11
    if kind == "m":
        return 4 + k - 64 if k >= 64 else 14 + k
    return 7 if k >= 64 else 14


def y_matrices():
    own = np.zeros((4, 64, 256), np.float32)
    halo = np.zeros((5, 16, 256), np.float32)
    corner = np.zeros((4, 8, 256), np.float32)
    columns = [(y, y) for y in range(128)] + [(128, 128), (-1, 255)]
    for z in range(4):
        columns += [(y, 136 + 32 * z + j) for j, y in enumerate((-2, -1, 0, 127, 128, 129))]
    for y, column in columns:
        for (kind, k), weight in predict_twice(y).items():
            role = "cdme".index(kind)
            length = 32 if role < 2 else 64
            if 0 <= k < length:
                own[role, k, column] += weight
                continue
            row = halo_row(kind, k)
            halo[role, row, column] += weight
            if kind == "e":
                halo[4, row + 1, column] += weight
            if k >= length:
                corner[role, k - length, column] += weight
            else:
                corner[role, (5 if length == 32 else 7) + k, column] += weight
    finest = np.concatenate([halo[3, :, 128:], halo[4, :, 128:]], axis=1)
    parts = [own.reshape(256, 256), halo[0:3].reshape(48, 256), finest, corner.reshape(32, 256)]
    return (0.5 * np.concatenate(parts)).astype(ml_dtypes.bfloat16)


def small_matrices():
    mats = np.zeros((192, 128), np.float32)
    for x in range(-2, 34):
        row = x + 8
        for (kind, k), weight in predict_twice(x).items():
            if kind == "c":
                at = 50 + k if k < 0 else (k if k < 8 else 56 + k - 8)
            elif kind == "d":
                at = 50 if k < 0 else (8 + k if k < 8 else 59)
            elif kind == "m":
                at = 53 + k if k < 0 else (16 + k if k < 16 else 60 + k - 16)
            else:
                at = 53 if k < 0 else (32 + k if k < 16 else 63)
            mats[row, at] += weight
    mats[6, 54] = 1.0
    mats[7, 55] = 1.0
    mats[0:48, 64:80] = mats[0:48, 48:64]
    mats[48:96, 0:48] = mats[0:48, 0:48]
    mats[48:96, 48:96] = mats[0:48, 0:48]
    picks = mats[96:176].reshape(5, 16, 128)
    for row, column in ((0, 0), (1, 1), (2, 2), (9, 30), (10, 31)):
        picks[0, row, column] = 1.0
    for row, column in ((3, 0), (11, 31)):
        picks[1, row, column] = 1.0
    for row, column in ((4, 0), (5, 1), (6, 2), (12, 62), (13, 63)):
        picks[2, row, column] = 1.0
    for row, column in ((7, 0), (14, 63)):
        picks[3, row, column] = 1.0
        picks[4, row + 1, column] = 1.0
    for row, column in ((0, 0), (1, 1), (2, 2), (3, 30), (4, 31), (5, 62), (6, 63)):
        mats[176 + row, column] = 1.0
    return mats.astype(ml_dtypes.bfloat16)


def face(mean, jump, k, factor=None):
    q, u, t = mean[0], mean[1:4], mean[4]
    rho = (0.5 * time_step) * jnp.exp(0.5 * q)
    if factor is not None:
        rho = rho * factor
    speed = u[k]
    half_square = 0.5 * (u[0] * u[0] + u[1] * u[1] + u[2] * u[2])
    enthalpy = (1.0 / heat_ratio_less_one + 1.0) * t + half_square
    inner = jump[0] + jump[1] * u[0] + jump[2] * u[1] + jump[3] * u[2] + jump[4] * enthalpy
    flow = rho * speed
    push = rho * jump[1 + k]
    grads = [flow * (jump[1 + j] + jump[4] * u[j]) for j in range(3)]
    grads[k] = grads[k] + rho * inner
    dq = 0.5 * (flow * inner + t * push)
    dt = push + (1.0 / heat_ratio_less_one + 1.0) * (flow * jump[4])
    terms = [dq] + grads + [dt]
    spread = [(viscosity * time_step) * jump[v] for v in range(5)]
    return [terms[v] + spread[v] for v in range(5)], [terms[v] - spread[v] for v in range(5)]


def kernel(
    c_in, x1_in, y1_in, x2_in, y2_in, sig_in, adj_in, ay_in, small_in,
    result,
    cx_ref, y1_ref, x2_ref, y2_ref, sig_ref, adj_ref, ay_ref, small_ref,
    load_sem,
    tiles, mask_x, mask_y, ext, hy2,
    first_send, first_recv, last_send, last_recv, low_send, low_recv, high_send, high_recv,
    corner_low, corner_low_recv, corner_high, corner_high_recv,
    ax_rows, ax_send, ax_recv, ay_send, ay_recv, rim,
    mapped, mapped_y2, mapped_rows, mapped_halo, finest_halo, beyond_rows, state, adj, mid, gx_terms, gz_terms,
    own_cols, turned, rim_turned, own_turned, levels, levels_z, packed, beside, mid_rim,
    send_sem, recv_sem,
):
    gx, gy, gz = lax.axis_index("gx"), lax.axis_index("gy"), lax.axis_index("gz")
    nx, ny = lax.axis_size("gx"), lax.axis_size("gy")
    up_x, down_x = lax.rem(gx + 1, nx), lax.rem(gx + nx - 1, nx)
    up_y, down_y = lax.rem(gy + 1, ny), lax.rem(gy + ny - 1, ny)
    x_up, x_down = {"gx": up_x}, {"gx": down_x}
    y_up, y_down = {"gy": up_y}, {"gy": down_y}
    diagonal = (
        {"gx": up_x, "gy": down_y},
        {"gx": up_x, "gy": up_y},
        {"gx": down_x, "gy": down_y},
        {"gx": down_x, "gy": up_y},
    )
    z_other = {"gz": 1 - gz}
    barrier = pltpu.get_barrier_semaphore()
    for peer in (x_up, x_down, y_up, y_down, z_other) + diagonal:
        pl.semaphore_signal(barrier, inc=1, device_id=peer, device_id_type=MESH)

    pairs = (
        (sig_in, sig_ref), (x2_in, x2_ref), (y2_in, y2_ref), (c_in, cx_ref.at[0:320]),
        (x1_in, cx_ref.at[320:640]), (y1_in, y1_ref), (small_in, small_ref), (adj_in, adj_ref),
        (ay_in, ay_ref),
    )
    loads = [
        pltpu.make_async_copy(source, target, load_sem.at[i])
        for i, (source, target) in enumerate(pairs)
    ]
    for load in loads:
        load.start()

    def remote(index, source, target, peer):
        return pltpu.make_async_remote_copy(
            src_ref=source,
            dst_ref=target,
            send_sem=send_sem.at[index],
            recv_sem=recv_sem.at[index],
            device_id=peer,
            device_id_type=MESH,
        )

    def transposed(left, right):
        return lax.dot_general(left, right, (((1,), (1,)), ((), ())), preferred_element_type=f32)

    lane = lax.broadcasted_iota(jnp.int32, (8, 128), 1)
    lane_wide = lax.broadcasted_iota(jnp.int32, (32, 128), 1)
    lane_full = lax.broadcasted_iota(jnp.int32, (48, 128), 1)

    ext[...] = jnp.zeros_like(ext)
    hy2[80:96] = jnp.zeros((16, 128), f32)
    ax_rows[:, 40:48] = jnp.zeros((2, 8, 128), f32)
    loads[0].wait()
    lane_tile = lax.broadcasted_iota(jnp.int32, (4, 64), 1) // 16
    row_half = lax.broadcasted_iota(jnp.int32, (8, 64), 0) < 4
    for c in range(2):
        for z in range(4):
            flags = sig_ref[c, z].astype(f32)
            wide = jnp.zeros((4, 64), f32)
            for t in range(4):
                wide = jnp.where(lane_tile == t, flags[:, t : t + 1], wide)
            tiles[c, z, 0:4] = wide
            each = [jnp.broadcast_to(tiles[c, z, t : t + 1], (8, 64)) for t in range(4)]
            for t in range(4):
                mask_y[c, z, 8 * t : 8 * t + 8] = each[t]
            for t in range(2):
                mask_x[c, z, 8 * t : 8 * t + 8] = jnp.where(row_half, each[2 * t], each[2 * t + 1])

    for load in loads[1:8]:
        load.wait()
    kept_x2 = x2_ref[...].astype(f32).reshape(2, 5, 4, 16, 64) * mask_x[...][:, None]
    kept_y2 = y2_ref[...].astype(f32).reshape(2, 5, 4, 32, 64) * mask_y[...][:, None]
    ext[0:640, 0:32] = cx_ref[...].astype(f32)
    ext[640:1280, 0:32] = y1_ref[...].astype(f32)
    ext[1280:1920, 0:64] = kept_x2.reshape(640, 64)
    ext[1920:3200, 0:64] = kept_y2.reshape(1280, 64)

    def own(begin, end):
        return ext[begin:end, 0:64].astype(bf16)

    starts = (0, 640, 1280, 1920, 2560)
    cols = jnp.zeros((16, 640), f32)
    for which, begin in enumerate(starts):
        pick = small_ref[96 + 16 * which : 112 + 16 * which, 0:64]
        cols = cols + transposed(pick, own(begin, begin + 640))
    first_send[...] = cols.astype(bf16)
    last_send[...] = cols[8:16].astype(bf16)

    coarse_e = ext[0:320].reshape(40, 8, 128)
    x1_e = ext[320:640].reshape(40, 8, 128)
    y1_e = ext[640:1280].reshape(40, 16, 128)
    x2_e = ext[1280:1920].reshape(40, 16, 128)
    y2_e = ext[1920:3200].reshape(40, 32, 128)
    low = jnp.concatenate(
        [coarse_e[:, 6:8], x1_e[:, 7:8], y1_e[:, 14:16], x2_e[:, 15:16], y2_e[:, 30:32]], 1
    ).reshape(320, 128)
    high = jnp.concatenate(
        [coarse_e[:, 0:3], x1_e[:, 0:1], y1_e[:, 0:3], x2_e[:, 0:1]], 1
    ).reshape(320, 128)
    for p in range(40):
        hy2[2 * p : 2 * p + 2] = ext[1920 + 32 * p : 1922 + 32 * p]
    more = hy2[0:48] + pltpu.roll(hy2[48:96], 64, 1)
    low_send[...] = (low[0:160] + pltpu.roll(low[160:320], 64, 1)).astype(bf16)
    high_send[0:160] = (high[0:160] + pltpu.roll(high[160:320], 64, 1)).astype(bf16)
    high_send[160:208] = more.astype(bf16)
    columns = jnp.zeros((32, 128), f32)
    for i in range(20):
        plane = adj_ref[i // 4, i % 4]
        columns = jnp.where(lane_wide // 4 == i, pltpu.roll(plane, 4 * i + 2, 1), columns)
        ax_rows[0, 2 * i : 2 * i + 2] = plane[0:2]
        ax_rows[1, 2 * i : 2 * i + 2] = plane[30:32]
    ax_send[...] = ax_rows[...].astype(bf16)
    ay_send[...] = columns.astype(bf16)
    own_cols[8:40] = columns

    last_row = lax.broadcasted_iota(jnp.int32, (8, 128), 0) == 7
    for target, pieces, row in (
        (corner_low, (low, jnp.zeros((64, 128), f32)), columns[31:32]),
        (corner_high, (high, hy2[0:80], jnp.zeros((112, 128), f32)), columns[0:1]),
    ):
        rows = jnp.concatenate(pieces, 0)[:, 0:64].astype(bf16)
        picked = transposed(small_ref[176:192, 0:64], rows)[0:8]
        target[:, 0:128] = jnp.where(last_row, row, picked[:, 0:128]).astype(bf16)
        target[:, 128:] = picked[:, 128:].astype(bf16)

    pl.semaphore_wait(barrier, 9)
    corner_copies = [remote(4 + i, corner_low, corner_low_recv.at[i], diagonal[i]) for i in range(2)]
    corner_copies += [
        remote(6 + i, corner_high, corner_high_recv.at[i], diagonal[2 + i]) for i in range(2)
    ]
    column_copies = [remote(0, first_send, first_recv, y_down), remote(1, last_send, last_recv, y_up)]
    row_copies = [remote(2, low_send, low_recv, x_up), remote(3, high_send, high_recv, x_down)]
    adj_copies = [
        remote(8, ay_send, ay_recv.at[0], y_down),
        remote(9, ay_send, ay_recv.at[1], y_up),
        remote(10, ax_send.at[0], ax_recv.at[1], x_down),
        remote(11, ax_send.at[1], ax_recv.at[0], x_up),
    ]
    for copy in corner_copies + column_copies + adj_copies + row_copies:
        copy.start()

    loads[8].wait()
    for begin, count, role, target, at in (
        (0, 8, 0, mapped, 0),
        (320, 8, 0, mapped, 8),
        (640, 16, 1, mapped, 16),
        (1280, 16, 2, mapped, 32),
        (1920, 32, 3, mapped_y2, 0),
    ):
        product = jnp.dot(
            own(begin, begin + 40 * count),
            ay_ref[64 * role : 64 * role + 64],
            preferred_element_type=f32,
        )
        target[:, at : at + count] = product.reshape(40, count, 256)
    beyond_rows[...] = jnp.zeros((40, 8, 256), f32)

    def synthesize_own(cv, carry):
        for z in range(4):
            p = cv * 4 + z
            exact = mapped[p]
            coarse_bits = exact.astype(bf16)
            rest = (exact - coarse_bits.astype(f32)).astype(bf16)
            whole = jnp.dot(
                small_ref[48:96, 0:96],
                jnp.concatenate([coarse_bits, rest], axis=0),
                preferred_element_type=f32,
            )
            for t in range(2):
                at = slice(128 * t, 128 * t + 128)
                state[t, cv, z + 1, 0:8] = whole[0:8, at]
                state[t, cv, z + 1, 8:40] = whole[8:40, at] + mapped_y2[p, :, at]
                state[t, cv, z + 1, 40:48] = whole[40:48, at]
        return carry

    lax.fori_loop(0, 10, synthesize_own, 0)

    outer = 5 * gz
    z_side = 3 - 3 * gz
    blank = jnp.zeros((48, 128), f32)
    for t in range(2):
        for v in range(5):
            adj[t, v, outer] = blank
            mid[t, v, outer] = blank
        for cv in range(10):
            state[t, cv, outer] = blank
    for i in range(20):
        v, z = i // 4, i % 4
        adj[0, v, z + 1, 0:8] = blank[0:8]
        adj[0, v, z + 1, 40:48] = blank[0:8]
        adj[0, v, z + 1, 8:40] = adj_ref[v, z]
    rim[...] = blank

    for copy in adj_copies:
        copy.wait()
    ax_rows[...] = ax_recv[...].astype(f32)
    for i in range(20):
        v, z = i // 4, i % 4
        adj[0, v, z + 1, 6:8] = ax_rows[0, 2 * i : 2 * i + 2]
        adj[0, v, z + 1, 40:42] = ax_rows[1, 2 * i : 2 * i + 2]
    for begin in (0, 40):
        ends = jnp.zeros((8, 128), f32)
        for i in range(20):
            tile = adj[0, i // 4, i % 4 + 1, begin : begin + 8]
            ends = jnp.where(lane // 4 == i, pltpu.roll(tile, 4 * i + 2, 1), ends)
        own_cols[begin : begin + 8] = ends
    first = lane_wide % 4 >= 2
    rim[8:40] = jnp.where(first, ay_recv[0].astype(f32), ay_recv[1].astype(f32))
    near = (lane_full < 2) | (lane_full >= 126)

    def fill_rim(begin, end):
        part = rim[begin:end]
        for i in range(20):
            adj[1, i // 4, i % 4 + 1, begin:end] = jnp.where(
                near[begin:end], pltpu.roll(part, (126 - 4 * i) % 128, 1), 0.0
            )

    fill_rim(8, 40)

    for copy in column_copies:
        copy.wait()
    firsts, lasts = first_recv[...].astype(f32), last_recv[...].astype(f32)
    top = lax.broadcasted_iota(jnp.int32, (8, 640), 0) == 0
    joined = jnp.concatenate([firsts[0:8], jnp.where(top, firsts[8:16], lasts)], 0).T.astype(bf16)
    halo = [
        jnp.dot(joined, ay_ref[256 + 16 * i : 272 + 16 * i], preferred_element_type=f32)
        for i in range(4)
    ]
    near_both = [halo[0][320 * i : 320 * i + 320].reshape(40, 8, 256) for i in range(2)]
    mapped_halo[:, 0:16] = jnp.concatenate(near_both, 1).astype(bf16)
    mapped_halo[:, 16:32] = halo[1].reshape(40, 16, 256).astype(bf16)
    mapped_halo[:, 32:48] = halo[2].reshape(40, 16, 256).astype(bf16)
    finest_halo[0:20] = halo[3][:, 0:128].reshape(20, 32, 128)
    finest_halo[20:40] = halo[3][:, 128:256].reshape(20, 32, 128)

    def from_corners(parts, role_of):
        width = parts.shape[2]
        row = lax.broadcasted_iota(jnp.int32, (8, width), 0)
        corners = jnp.where(row < 3, parts[0].astype(f32), parts[1].astype(f32))
        role = role_of(lax.broadcasted_iota(jnp.int32, (8, width), 1))
        stacked = jnp.concatenate([jnp.where(role == r, corners, 0.0) for r in range(4)], 0)
        return jnp.dot(stacked.T.astype(bf16), ay_ref[320:352], preferred_element_type=f32)

    def low_role(place):
        kind = place % 8
        return jnp.where(kind < 3, 0, jnp.where(kind < 5, 1, jnp.where(kind < 6, 2, 3)))

    def high_role(place):
        kind = place % 8
        inner = jnp.where(kind < 4, 0, jnp.where(kind < 7, 1, 2))
        return jnp.where(place < 320, inner, 3)

    for copy in corner_copies:
        copy.wait()
    from_low = from_corners(corner_low_recv, low_role)
    from_high = from_corners(corner_high_recv, high_role)
    for parts, at in ((corner_low_recv, 7), (corner_high_recv, 40)):
        rows = [parts[i, :, 0:128].astype(f32)[7:8] for i in range(2)]
        rim[at : at + 1] = jnp.where(first[0:1], rows[0], rows[1])
    fill_rim(0, 8)
    fill_rim(40, 48)
    adj_z = remote(12, adj.at[0, :, z_side + 1], adj.at[0, :, outer], z_other)
    adj_z.start()
    rim_turned[:, 0:48] = rim[...].T
    own_turned[:, 0:48] = own_cols[...].T

    def level_rows(kind, level, v, source, step, low_at, high_at):
        levels[kind, level, v, pl.ds(0, 4, stride=2)] = source[pl.ds(low_at, 4, stride=step)]
        levels[kind, level, v, pl.ds(1, 4, stride=2)] = source[pl.ds(high_at, 4, stride=step)]

    for v in range(5):
        for level, source, low_at, high_at in ((0, rim_turned, 1, 2), (1, rim_turned, 0, 3), (2, own_turned, 2, 1)):
            level_rows(0, level, v, source, 4, 16 * v + low_at, 16 * v + high_at)

    for copy in row_copies:
        copy.wait()
    low_half, high_half = low_recv[...].astype(f32), high_recv[...].astype(f32)

    upper = lane >= 64
    row_kind = lax.broadcasted_iota(jnp.int32, (8, 128), 0)

    def doubled(half):
        turned = pltpu.roll(half, 64, 1).reshape(half.shape[0] // 8, 8, 128)
        half = half.reshape(turned.shape)
        return jnp.concatenate(
            [jnp.where(upper[None], turned, half), jnp.where(upper[None], half, turned)], 0
        )

    for half, bounds, target in (
        (low_half, (3, 5, 6), 0),
        (high_half[0:160], (4, 7, 8), 8),
    ):
        values = doubled(half)
        role = jnp.where(
            row_kind < bounds[0], 0, jnp.where(row_kind < bounds[1], 1, jnp.where(row_kind < bounds[2], 2, 3))
        )
        spot = jnp.where(upper, 1, 0)
        parts = [
            jnp.where((role == spot + 2 * i)[None], values, 0.0).reshape(320, 128) for i in range(2)
        ]
        total = jnp.dot(
            jnp.concatenate(parts, 1).astype(bf16), ay_ref[0:256], preferred_element_type=f32
        )
        mapped_rows[:, target : target + 8] = total.reshape(40, 8, 256)
    more = doubled(high_half[160:208]).reshape(96, 128)[0:80, 0:64].astype(bf16)
    beyond = jnp.dot(more, ay_ref[192:256], preferred_element_type=f32)

    from_both = [part[0:320].reshape(40, 8, 256) for part in (from_low, from_high)]
    all_rows = mapped_rows[...] + jnp.concatenate(from_both, 1)
    rows_bits = all_rows.astype(bf16)
    mapped_halo[:, 48:64] = rows_bits
    mapped_halo[:, 64:80] = (all_rows - rows_bits.astype(f32)).astype(bf16)
    beyond = beyond + from_high[320:400]
    for p in range(40):
        beyond_rows[p, 0:2] = beyond[2 * p : 2 * p + 2]
    def synthesize(order, cv, carry):
        for z in order:
            p = cv * 4 + z
            whole = jnp.dot(small_ref[0:48, 0:80], mapped_halo[p], preferred_element_type=f32)
            for t in range(2):
                at = slice(128 * t, 128 * t + 128)
                state[t, cv, z + 1, 0:8] += whole[0:8, at]
                inside = whole[8:40, at]
                state[t, cv, z + 1, 8:40] += inside if t == 0 else inside + finest_halo[p]
                state[t, cv, z + 1, 40:48] += whole[40:48, at] + beyond_rows[p, :, at]
        return carry

    def synthesize_sides(pair, carry):
        for j in range(5):
            synthesize((z_side,), 5 * pair + j, carry)
        return carry

    for cv in range(10):
        synthesize((z_side,), cv, 0)
    state_first = remote(13, state.at[0, 0:5, z_side + 1], state.at[0, 0:5, outer], z_other)
    state_second = remote(
        14, state.at[0, 5:10, z_side + 1, 8:40], state.at[0, 5:10, outer, 8:40], z_other
    )
    state_first.start()
    state_second.start()
    def synthesize_rest(pair, carry):
        for j in range(5):
            synthesize((gz, gz + 1, gz + 2), 5 * pair + j, carry)
        return carry

    for pair in range(2):
        synthesize_rest(pair, 0)
    keep_bottom = jnp.where(gz > 0, 1.0, 0.0).astype(f32)

    def ahead(a, b):
        return pltpu.roll(jnp.where(lane == 0, b, a), 127, 1)

    def behind(a, b):
        return pltpu.roll(jnp.where(lane == 127, b, a), 1, 1)

    def x_face(t, base, source, z, r, start):
        low_at = slice(start + 8 * r, start + 8 + 8 * r)
        high_at = slice(start + 1 + 8 * r, start + 9 + 8 * r)
        mean = [
            (state[t, base + v, z + 1, low_at] + state[t, base + v, z + 1, high_at])
            for v in range(5)
        ]
        jump = [source[t, v, z + 1, high_at] - source[t, v, z + 1, low_at] for v in range(5)]
        below, above = face(mean, jump, 0)
        for v in range(5):
            gx_terms[0, t, v, 8 * r : 8 * r + 8] = below[v]
            gx_terms[1, t, v, 8 * r : 8 * r + 8] = above[v]

    def z_face(t, base, source, k, count, start):
        for r in range(count):
            at = slice(start + 8 * r, start + 8 + 8 * r)
            mean = [
                state[t, base + v, k, at] + state[t, base + v, k + 1, at] for v in range(5)
            ]
            jump = [source[t, v, k + 1, at] - source[t, v, k, at] for v in range(5)]
            below, above = face(mean, jump, 2, jnp.where(k == 0, keep_bottom, 1.0))
            for v in range(5):
                gz_terms[0, t, v, k, 8 * r : 8 * r + 8] = below[v]
                gz_terms[1, t, v, k, 8 * r : 8 * r + 8] = above[v]

    group = lane_full // 32
    for v in range(5):
        joint = state[1, v, 1]
        for z in range(1, 4):
            joint = jnp.where(group == z, state[1, v, z + 1], joint)
        turned[v, :, 0:48] = joint.T
    for v in range(5):
        for level, low_at, high_at in ((0, 9, 12), (1, 8, 13), (2, 10, 11)):
            level_rows(1, level, v, turned.at[v], 32, low_at, high_at)
    levels_copy = remote(16, levels.at[:, 0], levels_z, z_other)
    levels_copy.start()
    sublane8 = lax.broadcasted_iota(jnp.int32, (8, 128), 0)
    is_low = sublane8 % 2 == 0
    sign = jnp.where(is_low, 1.0, -1.0).astype(f32)

    def level(kind, which):
        return [levels[kind, which, v] for v in range(5)]

    rim_adj, rim_state = level(0, 0), level(1, 0)
    inner_adj, inner_state = level(0, 2), level(1, 2)
    lower, upper_share = face(
        [rim_state[v] + inner_state[v] for v in range(5)],
        [sign * (inner_adj[v] - rim_adj[v]) for v in range(5)],
        1,
    )
    for v in range(5):
        packed[8 * v : 8 * v + 8] = upper_share[v]
    inner_share = [jnp.where(is_low, lower[v], upper_share[v]) for v in range(5)]
    back = packed[...].T
    for i in range(20):
        v, z = i // 4, i % 4
        beside[v, z] = pltpu.roll(back[0:48], (128 - 8 * v - 2 * z) % 128, 1)
    outer_adj, outer_state = level(0, 1), level(1, 1)
    lower, upper_share = face(
        [rim_state[v] + outer_state[v] for v in range(5)],
        [sign * (rim_adj[v] - outer_adj[v]) for v in range(5)],
        1,
    )
    rim_middle = [
        rim_adj[v] + inner_share[v] + jnp.where(is_low, upper_share[v], lower[v]) for v in range(5)
    ]
    lower, upper_share = face(
        [rim_state[v] + pltpu.roll(rim_state[v], 127, 1) for v in range(5)],
        [pltpu.roll(rim_adj[v], 127, 1) - rim_adj[v] for v in range(5)],
        0,
    )
    for v in range(5):
        levels[0, 1, v] = rim_middle[v] + lower[v] + pltpu.roll(upper_share[v], 1, 1)
    for k in range(1, 4):
        z_face(0, 0, adj, k, 5, 7)
    adj_z.wait()
    state_first.wait()

    for k in (0, 4):
        z_face(0, 0, adj, k, 5, 7)
    mid_z = remote(15, mid.at[0, :, z_side + 1, 8:40], mid.at[0, :, outer, 8:40], z_other)

    def first_plane(j, carry):
        @pl.when(j == 1)
        def _():
            mid_z.start()

        z = jnp.where(gz > 0, j, 3 - j)
        for r in range(5):
            x_face(0, 0, adj, z, r, 6)
        for r in range(5):
            at, rows = slice(7 + 8 * r, 15 + 8 * r), slice(8 * r, 8 * r + 8)
            here = [state[0, v, z + 1, at] for v in range(5)]
            held = [adj[0, v, z + 1, at] for v in range(5)]
            below, above = face(
                [here[v] + ahead(here[v], state[1, v, z + 1, at]) for v in range(5)],
                [ahead(held[v], adj[1, v, z + 1, at]) - held[v] for v in range(5)],
                1,
            )
            for v in range(5):
                mid[0, v, z + 1, at] = (
                    held[v]
                    + below[v]
                    + jnp.where(lane == 0, beside[v, z, at], pltpu.roll(above[v], 1, 1))
                    + gx_terms[0, 0, v, 8 * r + 1 : 8 * r + 9]
                    + gx_terms[1, 0, v, rows]
                    + gz_terms[0, 0, v, z + 1, rows]
                    + gz_terms[1, 0, v, z, rows]
                )
        return carry

    lax.fori_loop(0, 4, first_plane, 0)
    levels_copy.wait()
    state_second.wait()
    up_part = jnp.where(gz > 0, 0.0, 1.0).astype(f32)
    down_part = 1.0 - up_part

    def next_plane(kind, v):
        tile = levels[kind, 0, v]
        from_other = levels_z[kind, v]
        return (
            jnp.where(sublane8 >= 6, up_part * pltpu.roll(from_other, 6, 0), pltpu.roll(tile, 6, 0)),
            jnp.where(sublane8 < 2, down_part * pltpu.roll(from_other, 2, 0), pltpu.roll(tile, 2, 0)),
        )

    rim_adj, rim_state = level(0, 0), level(1, 0)
    next_adj = [next_plane(0, v) for v in range(5)]
    next_state = [next_plane(1, v) for v in range(5)]
    lower, _ = face(
        [rim_state[v] + next_state[v][0] for v in range(5)],
        [next_adj[v][0] - rim_adj[v] for v in range(5)],
        2,
    )
    _, upper_share = face(
        [rim_state[v] + next_state[v][1] for v in range(5)],
        [rim_adj[v] - next_adj[v][1] for v in range(5)],
        2,
        jnp.where(sublane8 < 2, keep_bottom, 1.0),
    )
    for v in range(5):
        packed[8 * v : 8 * v + 8] = levels[0, 1, v] + lower[v] + upper_share[v]
    back = packed[...].T
    for i in range(20):
        v, z = i // 4, i % 4
        mid_rim[v, z, :] = pltpu.roll(back[8:40], (127 - 8 * v - 2 * z) % 128, 1)
    for k in range(4):
        z_face(0, 5, mid, gz + k, 4, 8)

    def second_plane(j, carry):
        z = jnp.where(gz > 0, 3 - j, j)

        @pl.when(j == 3)
        def _():
            mid_z.wait()
            z_face(0, 5, mid, 4 - 4 * gz, 4, 8)

        for r in range(5):
            x_face(0, 5, mid, z, r, 7)
        for r in range(4):
            at, rows = slice(8 + 8 * r, 16 + 8 * r), slice(8 * r, 8 * r + 8)
            here = [state[0, 5 + v, z + 1, at] for v in range(5)]
            edge = [state[1, 5 + v, z + 1, at] for v in range(5)]
            held = [mid[0, v, z + 1, at] for v in range(5)]
            held_edge = [mid_rim[v, z, rows] for v in range(5)]
            adj_up = [ahead(held[v], held_edge[v]) for v in range(5)]
            adj_down = [behind(held[v], held_edge[v]) for v in range(5)]
            below, _ = face(
                [here[v] + ahead(here[v], edge[v]) for v in range(5)],
                [adj_up[v] - held[v] for v in range(5)],
                1,
            )
            _, above = face(
                [here[v] + behind(here[v], edge[v]) for v in range(5)],
                [held[v] - adj_down[v] for v in range(5)],
                1,
            )
            for v in range(5):
                result[v, z, rows] = 0.5 * (
                    adj[0, v, z + 1, at]
                    + held[v]
                    + below[v]
                    + above[v]
                    + gx_terms[0, 0, v, 8 * r + 1 : 8 * r + 9]
                    + gx_terms[1, 0, v, rows]
                    + gz_terms[0, 0, v, z + 1, rows]
                    + gz_terms[1, 0, v, z, rows]
                )
        return carry

    lax.fori_loop(0, 4, second_plane, 0)


def shards(coarse, detail_x1, detail_y1, detail_x2, detail_y2, significance, adjoint):
    operands = [
        pltpu.with_memory_space_constraint(value, pltpu.HBM)
        for value in (
            coarse.reshape(320, 32),
            detail_x1.reshape(320, 32),
            detail_y1.reshape(640, 32),
            detail_x2.reshape(640, 64),
            detail_y2.reshape(1280, 64),
            significance,
            adjoint,
            jnp.asarray(y_matrices()),
            jnp.asarray(small_matrices()),
        )
    ]
    anywhere = pl.BlockSpec(memory_space=pl.ANY)
    return pl.pallas_call(
        kernel,
        out_shape=jax.ShapeDtypeStruct(adjoint.shape, f32),
        in_specs=[anywhere] * 9,
        out_specs=pl.BlockSpec(memory_space=pltpu.VMEM),
        scratch_shapes=[
            pltpu.VMEM((640, 32), bf16),
            pltpu.VMEM((640, 32), bf16),
            pltpu.VMEM((640, 64), bf16),
            pltpu.VMEM((1280, 64), bf16),
            pltpu.VMEM((2, 4, 4, 4), jnp.int32),
            pltpu.VMEM((5, 4, 32, 128), f32),
            pltpu.VMEM((352, 256), bf16),
            pltpu.VMEM((192, 128), bf16),
            pltpu.SemaphoreType.DMA((9,)),
            pltpu.VMEM((2, 4, 8, 64), f32),
            pltpu.VMEM((2, 4, 16, 64), f32),
            pltpu.VMEM((2, 4, 32, 64), f32),
            pltpu.VMEM((3200, 128), f32),
            pltpu.VMEM((96, 128), f32),
            pltpu.VMEM((16, 640), bf16),
            pltpu.VMEM((16, 640), bf16),
            pltpu.VMEM((8, 640), bf16),
            pltpu.VMEM((8, 640), bf16),
            pltpu.VMEM((160, 128), bf16),
            pltpu.VMEM((160, 128), bf16),
            pltpu.VMEM((208, 128), bf16),
            pltpu.VMEM((208, 128), bf16),
            pltpu.VMEM((8, 384), bf16),
            pltpu.VMEM((2, 8, 384), bf16),
            pltpu.VMEM((8, 512), bf16),
            pltpu.VMEM((2, 8, 512), bf16),
            pltpu.VMEM((2, 48, 128), f32),
            pltpu.VMEM((2, 48, 128), bf16),
            pltpu.VMEM((2, 48, 128), bf16),
            pltpu.VMEM((32, 128), bf16),
            pltpu.VMEM((2, 32, 128), bf16),
            pltpu.VMEM((48, 128), f32),
            pltpu.VMEM((40, 48, 256), f32),
            pltpu.VMEM((40, 32, 256), f32),
            pltpu.VMEM((40, 16, 256), f32),
            pltpu.VMEM((40, 80, 256), bf16),
            pltpu.VMEM((40, 32, 128), f32),
            pltpu.VMEM((40, 8, 256), f32),
            pltpu.VMEM((2, 10, 6, 48, 128), f32),
            pltpu.VMEM((2, 5, 6, 48, 128), f32),
            pltpu.VMEM((2, 5, 6, 48, 128), f32),
            pltpu.VMEM((2, 1, 5, 48, 128), f32),
            pltpu.VMEM((2, 1, 5, 5, 40, 128), f32),
            pltpu.VMEM((48, 128), f32),
            pltpu.VMEM((5, 128, 128), f32),
            pltpu.VMEM((128, 128), f32),
            pltpu.VMEM((128, 128), f32),
            pltpu.VMEM((2, 3, 5, 8, 128), f32),
            pltpu.VMEM((2, 5, 8, 128), f32),
            pltpu.VMEM((128, 128), f32),
            pltpu.VMEM((5, 4, 48, 128), f32),
            pltpu.VMEM((5, 4, 32, 128), f32),
            pltpu.SemaphoreType.DMA((17,)),
            pltpu.SemaphoreType.DMA((17,)),
        ],
        compiler_params=pltpu.CompilerParams(collective_id=0, has_side_effects=True, vmem_limit_bytes=40*2**20),
    )(
        *operands,
    )


def solution(mesh):
    return jax.shard_map(
        shards,
        mesh=mesh,
        in_specs=(
            P(None, None, "gz", "gx", "gy"),
            P(None, None, "gz", "gx", "gy"),
            P(None, None, "gz", "gx", "gy"),
            P(None, None, "gz", "gx", "gy"),
            P(None, None, "gz", "gx", "gy"),
            P(None, "gz", "gx", "gy"),
            P(None, "gz", "gx", "gy"),
        ),
        out_specs=P(None, "gz", "gx", "gy"),
        check_vma=False,
    )
```

```python
import functools

import jax
import jax.numpy as jnp
import ml_dtypes
import numpy as np
from jax import lax
from jax.experimental import pallas as pl
from jax.experimental.pallas import tpu as pltpu
from jax.sharding import PartitionSpec as P

time_step = 0.1
viscosity = 0.2
heat_ratio_less_one = 0.4
f32 = jnp.float32
bf16 = jnp.bfloat16
MESH = pl.DeviceIdType.MESH


def predict(index):
    k = index // 2
    if index % 2 == 0:
        return {("c", k): 1.0}
    return {
        ("d", k): 1.0,
        ("c", k): 9 / 16,
        ("c", k + 1): 9 / 16,
        ("c", k - 1): -1 / 16,
        ("c", k + 2): -1 / 16,
    }


def predict_twice(index):
    whole = {}
    for (kind, k), weight in predict(index).items():
        if kind == "d":
            whole[("e", k)] = weight
            continue
        whole[("m", k)] = weight
        for key, inner in predict(k).items():
            whole[key] = whole.get(key, 0.0) + weight * inner
    return whole


def halo_row(kind, k):
    if kind == "c":
        return k - 32 if k >= 32 else 11 + k
    if kind == "d":
        return 3 if k >= 32 else 11
    if kind == "m":
        return 4 + k - 64 if k >= 64 else 14 + k
    return 7 if k >= 64 else 14


def y_matrices():
    own = np.zeros((4, 64, 256), np.float32)
    halo = np.zeros((5, 16, 256), np.float32)
    corner = np.zeros((4, 8, 256), np.float32)
    columns = [(y, y) for y in range(128)] + [(128, 128), (-1, 255)]
    for z in range(4):
        columns += [(y, 136 + 32 * z + j) for j, y in enumerate((-2, -1, 0, 127, 128, 129))]
    for y, column in columns:
        for (kind, k), weight in predict_twice(y).items():
            role = "cdme".index(kind)
            length = 32 if role < 2 else 64
            if 0 <= k < length:
                own[role, k, column] += weight
                continue
            row = halo_row(kind, k)
            halo[role, row, column] += weight
            if kind == "e":
                halo[4, row + 1, column] += weight
            if k >= length:
                corner[role, k - length, column] += weight
            else:
                corner[role, (5 if length == 32 else 7) + k, column] += weight
    finest = np.concatenate([halo[3, :, 128:], halo[4, :, 128:]], axis=1)
    parts = [own.reshape(256, 256), halo[0:3].reshape(48, 256), finest, corner.reshape(32, 256)]
    return (0.5 * np.concatenate(parts)).astype(ml_dtypes.bfloat16)


def small_matrices():
    mats = np.zeros((192, 128), np.float32)
    for x in range(-2, 34):
        row = x + 8
        for (kind, k), weight in predict_twice(x).items():
            if kind == "c":
                at = 50 + k if k < 0 else (k if k < 8 else 56 + k - 8)
            elif kind == "d":
                at = 50 if k < 0 else (8 + k if k < 8 else 59)
            elif kind == "m":
                at = 53 + k if k < 0 else (16 + k if k < 16 else 60 + k - 16)
            else:
                at = 53 if k < 0 else (32 + k if k < 16 else 63)
            mats[row, at] += weight
    mats[6, 54] = 1.0
    mats[7, 55] = 1.0
    mats[0:48, 64:80] = mats[0:48, 48:64]
    mats[48:96, 0:48] = mats[0:48, 0:48]
    mats[48:96, 48:96] = mats[0:48, 0:48]
    picks = mats[96:176].reshape(5, 16, 128)
    for row, column in ((0, 0), (1, 1), (2, 2), (9, 30), (10, 31)):
        picks[0, row, column] = 1.0
    for row, column in ((3, 0), (11, 31)):
        picks[1, row, column] = 1.0
    for row, column in ((4, 0), (5, 1), (6, 2), (12, 62), (13, 63)):
        picks[2, row, column] = 1.0
    for row, column in ((7, 0), (14, 63)):
        picks[3, row, column] = 1.0
        picks[4, row + 1, column] = 1.0
    for row, column in ((0, 0), (1, 1), (2, 2), (3, 30), (4, 31), (5, 62), (6, 63)):
        mats[176 + row, column] = 1.0
    return mats.astype(ml_dtypes.bfloat16)


def face(mean, jump, k, factor=None):
    q, u, t = mean[0], mean[1:4], mean[4]
    rho = (0.5 * time_step) * jnp.exp(0.5 * q)
    if factor is not None:
        rho = rho * factor
    speed = u[k]
    half_square = 0.5 * (u[0] * u[0] + u[1] * u[1] + u[2] * u[2])
    enthalpy = (1.0 / heat_ratio_less_one + 1.0) * t + half_square
    inner = jump[0] + jump[1] * u[0] + jump[2] * u[1] + jump[3] * u[2] + jump[4] * enthalpy
    flow = rho * speed
    push = rho * jump[1 + k]
    grads = [flow * (jump[1 + j] + jump[4] * u[j]) for j in range(3)]
    grads[k] = grads[k] + rho * inner
    dq = 0.5 * (flow * inner + t * push)
    dt = push + (1.0 / heat_ratio_less_one + 1.0) * (flow * jump[4])
    terms = [dq] + grads + [dt]
    spread = [(viscosity * time_step) * jump[v] for v in range(5)]
    return [terms[v] + spread[v] for v in range(5)], [terms[v] - spread[v] for v in range(5)]


def kernel(
    c_in, x1_in, y1_in, x2_in, y2_in, sig_in, adj_in, ay_in, small_in,
    result,
    cx_ref, y1_ref, x2_ref, y2_ref, sig_ref, adj_ref, ay_ref, small_ref,
    load_sem,
    tiles, mask_x, mask_y, ext, hy2,
    first_send, first_recv, last_send, last_recv, low_send, low_recv, high_send, high_recv,
    corner_low, corner_low_recv, corner_high, corner_high_recv,
    ax_rows, ax_send, ax_recv, ay_send, ay_recv, rim,
    mapped, mapped_y2, mapped_rows, mapped_halo, finest_halo, beyond_rows, state, adj, mid, gx_terms, gz_terms,
    own_cols, turned, rim_turned, own_turned, levels, levels_z, packed, beside, mid_rim,
    send_sem, recv_sem,
):
    gx, gy, gz = lax.axis_index("gx"), lax.axis_index("gy"), lax.axis_index("gz")
    nx, ny = lax.axis_size("gx"), lax.axis_size("gy")
    up_x, down_x = lax.rem(gx + 1, nx), lax.rem(gx + nx - 1, nx)
    up_y, down_y = lax.rem(gy + 1, ny), lax.rem(gy + ny - 1, ny)
    x_up, x_down = {"gx": up_x}, {"gx": down_x}
    y_up, y_down = {"gy": up_y}, {"gy": down_y}
    diagonal = (
        {"gx": up_x, "gy": down_y},
        {"gx": up_x, "gy": up_y},
        {"gx": down_x, "gy": down_y},
        {"gx": down_x, "gy": up_y},
    )
    z_other = {"gz": 1 - gz}
    barrier = pltpu.get_barrier_semaphore()
    for peer in (x_up, x_down, y_up, y_down, z_other) + diagonal:
        pl.semaphore_signal(barrier, inc=1, device_id=peer, device_id_type=MESH)

    pairs = (
        (sig_in, sig_ref), (x2_in, x2_ref), (y2_in, y2_ref), (c_in, cx_ref.at[0:320]),
        (x1_in, cx_ref.at[320:640]), (y1_in, y1_ref), (small_in, small_ref), (adj_in, adj_ref),
        (ay_in, ay_ref),
    )
    loads = [
        pltpu.make_async_copy(source, target, load_sem.at[i])
        for i, (source, target) in enumerate(pairs)
    ]
    for load in loads:
        load.start()

    def remote(index, source, target, peer):
        return pltpu.make_async_remote_copy(
            src_ref=source,
            dst_ref=target,
            send_sem=send_sem.at[index],
            recv_sem=recv_sem.at[index],
            device_id=peer,
            device_id_type=MESH,
        )

    def transposed(left, right):
        return lax.dot_general(left, right, (((1,), (1,)), ((), ())), preferred_element_type=f32)

    lane = lax.broadcasted_iota(jnp.int32, (8, 128), 1)
    lane_wide = lax.broadcasted_iota(jnp.int32, (32, 128), 1)
    lane_full = lax.broadcasted_iota(jnp.int32, (48, 128), 1)

    ext[...] = jnp.zeros_like(ext)
    hy2[80:96] = jnp.zeros((16, 128), f32)
    ax_rows[:, 40:48] = jnp.zeros((2, 8, 128), f32)
    loads[0].wait()
    lane_tile = lax.broadcasted_iota(jnp.int32, (4, 64), 1) // 16
    row_half = lax.broadcasted_iota(jnp.int32, (8, 64), 0) < 4
    for c in range(2):
        for z in range(4):
            flags = sig_ref[c, z].astype(f32)
            wide = jnp.zeros((4, 64), f32)
            for t in range(4):
                wide = jnp.where(lane_tile == t, flags[:, t : t + 1], wide)
            tiles[c, z, 0:4] = wide
            each = [jnp.broadcast_to(tiles[c, z, t : t + 1], (8, 64)) for t in range(4)]
            for t in range(4):
                mask_y[c, z, 8 * t : 8 * t + 8] = each[t]
            for t in range(2):
                mask_x[c, z, 8 * t : 8 * t + 8] = jnp.where(row_half, each[2 * t], each[2 * t + 1])

    for load in loads[1:8]:
        load.wait()
    kept_x2 = x2_ref[...].astype(f32).reshape(2, 5, 4, 16, 64) * mask_x[...][:, None]
    kept_y2 = y2_ref[...].astype(f32).reshape(2, 5, 4, 32, 64) * mask_y[...][:, None]
    ext[0:640, 0:32] = cx_ref[...].astype(f32)
    ext[640:1280, 0:32] = y1_ref[...].astype(f32)
    ext[1280:1920, 0:64] = kept_x2.reshape(640, 64)
    ext[1920:3200, 0:64] = kept_y2.reshape(1280, 64)

    def own(begin, end):
        return ext[begin:end, 0:64].astype(bf16)

    starts = (0, 640, 1280, 1920, 2560)
    cols = jnp.zeros((16, 640), f32)
    for which, begin in enumerate(starts):
        pick = small_ref[96 + 16 * which : 112 + 16 * which, 0:64]
        cols = cols + transposed(pick, own(begin, begin + 640))
    first_send[...] = cols.astype(bf16)
    last_send[...] = cols[8:16].astype(bf16)

    coarse_e = ext[0:320].reshape(40, 8, 128)
    x1_e = ext[320:640].reshape(40, 8, 128)
    y1_e = ext[640:1280].reshape(40, 16, 128)
    x2_e = ext[1280:1920].reshape(40, 16, 128)
    y2_e = ext[1920:3200].reshape(40, 32, 128)
    low = jnp.concatenate(
        [coarse_e[:, 6:8], x1_e[:, 7:8], y1_e[:, 14:16], x2_e[:, 15:16], y2_e[:, 30:32]], 1
    ).reshape(320, 128)
    high = jnp.concatenate(
        [coarse_e[:, 0:3], x1_e[:, 0:1], y1_e[:, 0:3], x2_e[:, 0:1]], 1
    ).reshape(320, 128)
    for p in range(40):
        hy2[2 * p : 2 * p + 2] = ext[1920 + 32 * p : 1922 + 32 * p]
    more = hy2[0:48] + pltpu.roll(hy2[48:96], 64, 1)
    low_send[...] = (low[0:160] + pltpu.roll(low[160:320], 64, 1)).astype(bf16)
    high_send[0:160] = (high[0:160] + pltpu.roll(high[160:320], 64, 1)).astype(bf16)
    high_send[160:208] = more.astype(bf16)
    columns = jnp.zeros((32, 128), f32)
    for i in range(20):
        plane = adj_ref[i // 4, i % 4]
        columns = jnp.where(lane_wide // 4 == i, pltpu.roll(plane, 4 * i + 2, 1), columns)
        ax_rows[0, 2 * i : 2 * i + 2] = plane[0:2]
        ax_rows[1, 2 * i : 2 * i + 2] = plane[30:32]
    ax_send[...] = ax_rows[...].astype(bf16)
    ay_send[...] = columns.astype(bf16)
    own_cols[8:40] = columns

    last_row = lax.broadcasted_iota(jnp.int32, (8, 128), 0) == 7
    for target, pieces, row in (
        (corner_low, (low, jnp.zeros((64, 128), f32)), columns[31:32]),
        (corner_high, (high, hy2[0:80], jnp.zeros((112, 128), f32)), columns[0:1]),
    ):
        rows = jnp.concatenate(pieces, 0)[:, 0:64].astype(bf16)
        picked = transposed(small_ref[176:192, 0:64], rows)[0:8]
        target[:, 0:128] = jnp.where(last_row, row, picked[:, 0:128]).astype(bf16)
        target[:, 128:] = picked[:, 128:].astype(bf16)

    pl.semaphore_wait(barrier, 9)
    corner_copies = [remote(4 + i, corner_low, corner_low_recv.at[i], diagonal[i]) for i in range(2)]
    corner_copies += [
        remote(6 + i, corner_high, corner_high_recv.at[i], diagonal[2 + i]) for i in range(2)
    ]
    column_copies = [remote(0, first_send, first_recv, y_down), remote(1, last_send, last_recv, y_up)]
    row_copies = [remote(2, low_send, low_recv, x_up), remote(3, high_send, high_recv, x_down)]
    adj_copies = [
        remote(8, ay_send, ay_recv.at[0], y_down),
        remote(9, ay_send, ay_recv.at[1], y_up),
        remote(10, ax_send.at[0], ax_recv.at[1], x_down),
        remote(11, ax_send.at[1], ax_recv.at[0], x_up),
    ]
    for copy in corner_copies + column_copies + adj_copies + row_copies:
        copy.start()

    loads[8].wait()
    for begin, count, role, target, at in (
        (0, 8, 0, mapped, 0),
        (320, 8, 0, mapped, 8),
        (640, 16, 1, mapped, 16),
        (1280, 16, 2, mapped, 32),
        (1920, 32, 3, mapped_y2, 0),
    ):
        product = jnp.dot(
            own(begin, begin + 40 * count),
            ay_ref[64 * role : 64 * role + 64],
            preferred_element_type=f32,
        )
        target[:, at : at + count] = product.reshape(40, count, 256)
    beyond_rows[...] = jnp.zeros((40, 8, 256), f32)

    def synthesize_own(cv, carry):
        for z in range(4):
            p = cv * 4 + z
            exact = mapped[p]
            coarse_bits = exact.astype(bf16)
            rest = (exact - coarse_bits.astype(f32)).astype(bf16)
            whole = jnp.dot(
                small_ref[48:96, 0:96],
                jnp.concatenate([coarse_bits, rest], axis=0),
                preferred_element_type=f32,
            )
            for t in range(2):
                at = slice(128 * t, 128 * t + 128)
                state[t, cv, z + 1, 0:8] = whole[0:8, at]
                state[t, cv, z + 1, 8:40] = whole[8:40, at] + mapped_y2[p, :, at]
                state[t, cv, z + 1, 40:48] = whole[40:48, at]
        return carry

    lax.fori_loop(0, 10, synthesize_own, 0)

    outer = 5 * gz
    z_side = 3 - 3 * gz
    blank = jnp.zeros((48, 128), f32)
    for t in range(2):
        for v in range(5):
            adj[t, v, outer] = blank
            mid[t, v, outer] = blank
        for cv in range(10):
            state[t, cv, outer] = blank
    for i in range(20):
        v, z = i // 4, i % 4
        adj[0, v, z + 1, 0:8] = blank[0:8]
        adj[0, v, z + 1, 40:48] = blank[0:8]
        adj[0, v, z + 1, 8:40] = adj_ref[v, z]
    rim[...] = blank

    for copy in adj_copies + column_copies:
        copy.wait()
    ax_rows[...] = ax_recv[...].astype(f32)
    for i in range(20):
        v, z = i // 4, i % 4
        adj[0, v, z + 1, 6:8] = ax_rows[0, 2 * i : 2 * i + 2]
        adj[0, v, z + 1, 40:42] = ax_rows[1, 2 * i : 2 * i + 2]
    for begin in (0, 40):
        ends = jnp.zeros((8, 128), f32)
        for i in range(20):
            tile = adj[0, i // 4, i % 4 + 1, begin : begin + 8]
            ends = jnp.where(lane // 4 == i, pltpu.roll(tile, 4 * i + 2, 1), ends)
        own_cols[begin : begin + 8] = ends
    first = lane_wide % 4 >= 2
    rim[8:40] = jnp.where(first, ay_recv[0].astype(f32), ay_recv[1].astype(f32))
    near = (lane_full < 2) | (lane_full >= 126)

    def fill_rim(begin, end):
        part = rim[begin:end]
        for i in range(20):
            adj[1, i // 4, i % 4 + 1, begin:end] = jnp.where(
                near[begin:end], pltpu.roll(part, (126 - 4 * i) % 128, 1), 0.0
            )

    fill_rim(8, 40)

    firsts, lasts = first_recv[...].astype(f32), last_recv[...].astype(f32)
    top = lax.broadcasted_iota(jnp.int32, (8, 640), 0) == 0
    joined = jnp.concatenate([firsts[0:8], jnp.where(top, firsts[8:16], lasts)], 0).T.astype(bf16)
    halo = [
        jnp.dot(joined, ay_ref[256 + 16 * i : 272 + 16 * i], preferred_element_type=f32)
        for i in range(4)
    ]
    near_both = [halo[0][320 * i : 320 * i + 320].reshape(40, 8, 256) for i in range(2)]
    mapped_halo[:, 0:16] = jnp.concatenate(near_both, 1).astype(bf16)
    mapped_halo[:, 16:32] = halo[1].reshape(40, 16, 256).astype(bf16)
    mapped_halo[:, 32:48] = halo[2].reshape(40, 16, 256).astype(bf16)
    finest_halo[0:20] = halo[3][:, 0:128].reshape(20, 32, 128)
    finest_halo[20:40] = halo[3][:, 128:256].reshape(20, 32, 128)

    def from_corners(parts, role_of):
        width = parts.shape[2]
        row = lax.broadcasted_iota(jnp.int32, (8, width), 0)
        corners = jnp.where(row < 3, parts[0].astype(f32), parts[1].astype(f32))
        role = role_of(lax.broadcasted_iota(jnp.int32, (8, width), 1))
        stacked = jnp.concatenate([jnp.where(role == r, corners, 0.0) for r in range(4)], 0)
        return jnp.dot(stacked.T.astype(bf16), ay_ref[320:352], preferred_element_type=f32)

    def low_role(place):
        kind = place % 8
        return jnp.where(kind < 3, 0, jnp.where(kind < 5, 1, jnp.where(kind < 6, 2, 3)))

    def high_role(place):
        kind = place % 8
        inner = jnp.where(kind < 4, 0, jnp.where(kind < 7, 1, 2))
        return jnp.where(place < 320, inner, 3)

    for copy in corner_copies:
        copy.wait()
    from_low = from_corners(corner_low_recv, low_role)
    from_high = from_corners(corner_high_recv, high_role)
    for parts, at in ((corner_low_recv, 7), (corner_high_recv, 40)):
        rows = [parts[i, :, 0:128].astype(f32)[7:8] for i in range(2)]
        rim[at : at + 1] = jnp.where(first[0:1], rows[0], rows[1])
    fill_rim(0, 8)
    fill_rim(40, 48)
    adj_z = remote(12, adj.at[0, :, z_side + 1], adj.at[0, :, outer], z_other)
    adj_z.start()
    rim_turned[:, 0:48] = rim[...].T
    own_turned[:, 0:48] = own_cols[...].T

    def level_rows(kind, level, v, source, step, low_at, high_at):
        levels[kind, level, v, pl.ds(0, 4, stride=2)] = source[pl.ds(low_at, 4, stride=step)]
        levels[kind, level, v, pl.ds(1, 4, stride=2)] = source[pl.ds(high_at, 4, stride=step)]

    for v in range(5):
        for level, source, low_at, high_at in ((0, rim_turned, 1, 2), (1, rim_turned, 0, 3), (2, own_turned, 2, 1)):
            level_rows(0, level, v, source, 4, 16 * v + low_at, 16 * v + high_at)

    for copy in row_copies:
        copy.wait()
    low_half, high_half = low_recv[...].astype(f32), high_recv[...].astype(f32)

    upper = lane >= 64
    row_kind = lax.broadcasted_iota(jnp.int32, (8, 128), 0)

    def doubled(half):
        turned = pltpu.roll(half, 64, 1).reshape(half.shape[0] // 8, 8, 128)
        half = half.reshape(turned.shape)
        return jnp.concatenate(
            [jnp.where(upper[None], turned, half), jnp.where(upper[None], half, turned)], 0
        )

    for half, bounds, target in (
        (low_half, (3, 5, 6), 0),
        (high_half[0:160], (4, 7, 8), 8),
    ):
        values = doubled(half)
        role = jnp.where(
            row_kind < bounds[0], 0, jnp.where(row_kind < bounds[1], 1, jnp.where(row_kind < bounds[2], 2, 3))
        )
        spot = jnp.where(upper, 1, 0)
        parts = [
            jnp.where((role == spot + 2 * i)[None], values, 0.0).reshape(320, 128) for i in range(2)
        ]
        total = jnp.dot(
            jnp.concatenate(parts, 1).astype(bf16), ay_ref[0:256], preferred_element_type=f32
        )
        mapped_rows[:, target : target + 8] = total.reshape(40, 8, 256)
    more = doubled(high_half[160:208]).reshape(96, 128)[0:80, 0:64].astype(bf16)
    beyond = jnp.dot(more, ay_ref[192:256], preferred_element_type=f32)

    from_both = [part[0:320].reshape(40, 8, 256) for part in (from_low, from_high)]
    all_rows = mapped_rows[...] + jnp.concatenate(from_both, 1)
    rows_bits = all_rows.astype(bf16)
    mapped_halo[:, 48:64] = rows_bits
    mapped_halo[:, 64:80] = (all_rows - rows_bits.astype(f32)).astype(bf16)
    beyond = beyond + from_high[320:400]
    for p in range(40):
        beyond_rows[p, 0:2] = beyond[2 * p : 2 * p + 2]
    def synthesize(order, cv, carry):
        for z in order:
            p = cv * 4 + z
            whole = jnp.dot(small_ref[0:48, 0:80], mapped_halo[p], preferred_element_type=f32)
            for t in range(2):
                at = slice(128 * t, 128 * t + 128)
                state[t, cv, z + 1, 0:8] += whole[0:8, at]
                inside = whole[8:40, at]
                state[t, cv, z + 1, 8:40] += inside if t == 0 else inside + finest_halo[p]
                state[t, cv, z + 1, 40:48] += whole[40:48, at] + beyond_rows[p, :, at]
        return carry

    def synthesize_sides(pair, carry):
        for j in range(5):
            synthesize((z_side,), 5 * pair + j, carry)
        return carry

    for cv in range(10):
        synthesize((z_side,), cv, 0)
    state_first = remote(13, state.at[0, 0:5, z_side + 1], state.at[0, 0:5, outer], z_other)
    state_second = remote(
        14, state.at[0, 5:10, z_side + 1, 8:40], state.at[0, 5:10, outer, 8:40], z_other
    )
    state_first.start()
    state_second.start()
    def synthesize_rest(pair, carry):
        for j in range(5):
            synthesize((gz, gz + 1, gz + 2), 5 * pair + j, carry)
        return carry

    for pair in range(2):
        synthesize_rest(pair, 0)
    keep_bottom = jnp.where(gz > 0, 1.0, 0.0).astype(f32)

    def ahead(a, b):
        return pltpu.roll(jnp.where(lane == 0, b, a), 127, 1)

    def behind(a, b):
        return pltpu.roll(jnp.where(lane == 127, b, a), 1, 1)

    def x_face(t, base, source, z, r, start):
        low_at = slice(start + 8 * r, start + 8 + 8 * r)
        high_at = slice(start + 1 + 8 * r, start + 9 + 8 * r)
        mean = [
            (state[t, base + v, z + 1, low_at] + state[t, base + v, z + 1, high_at])
            for v in range(5)
        ]
        jump = [source[t, v, z + 1, high_at] - source[t, v, z + 1, low_at] for v in range(5)]
        below, above = face(mean, jump, 0)
        for v in range(5):
            gx_terms[0, t, v, 8 * r : 8 * r + 8] = below[v]
            gx_terms[1, t, v, 8 * r : 8 * r + 8] = above[v]

    def z_face(t, base, source, k, count, start):
        for r in range(count):
            at = slice(start + 8 * r, start + 8 + 8 * r)
            mean = [
                state[t, base + v, k, at] + state[t, base + v, k + 1, at] for v in range(5)
            ]
            jump = [source[t, v, k + 1, at] - source[t, v, k, at] for v in range(5)]
            below, above = face(mean, jump, 2, jnp.where(k == 0, keep_bottom, 1.0))
            for v in range(5):
                gz_terms[0, t, v, k, 8 * r : 8 * r + 8] = below[v]
                gz_terms[1, t, v, k, 8 * r : 8 * r + 8] = above[v]

    group = lane_full // 32
    for v in range(5):
        joint = state[1, v, 1]
        for z in range(1, 4):
            joint = jnp.where(group == z, state[1, v, z + 1], joint)
        turned[v, :, 0:48] = joint.T
    for v in range(5):
        for level, low_at, high_at in ((0, 9, 12), (1, 8, 13), (2, 10, 11)):
            level_rows(1, level, v, turned.at[v], 32, low_at, high_at)
    levels_copy = remote(16, levels.at[:, 0], levels_z, z_other)
    levels_copy.start()
    sublane8 = lax.broadcasted_iota(jnp.int32, (8, 128), 0)
    is_low = sublane8 % 2 == 0
    sign = jnp.where(is_low, 1.0, -1.0).astype(f32)

    def level(kind, which):
        return [levels[kind, which, v] for v in range(5)]

    rim_adj, rim_state = level(0, 0), level(1, 0)
    inner_adj, inner_state = level(0, 2), level(1, 2)
    lower, upper_share = face(
        [rim_state[v] + inner_state[v] for v in range(5)],
        [sign * (inner_adj[v] - rim_adj[v]) for v in range(5)],
        1,
    )
    for v in range(5):
        packed[8 * v : 8 * v + 8] = upper_share[v]
    inner_share = [jnp.where(is_low, lower[v], upper_share[v]) for v in range(5)]
    back = packed[...].T
    for i in range(20):
        v, z = i // 4, i % 4
        beside[v, z] = pltpu.roll(back[0:48], (128 - 8 * v - 2 * z) % 128, 1)
    outer_adj, outer_state = level(0, 1), level(1, 1)
    lower, upper_share = face(
        [rim_state[v] + outer_state[v] for v in range(5)],
        [sign * (rim_adj[v] - outer_adj[v]) for v in range(5)],
        1,
    )
    rim_middle = [
        rim_adj[v] + inner_share[v] + jnp.where(is_low, upper_share[v], lower[v]) for v in range(5)
    ]
    lower, upper_share = face(
        [rim_state[v] + pltpu.roll(rim_state[v], 127, 1) for v in range(5)],
        [pltpu.roll(rim_adj[v], 127, 1) - rim_adj[v] for v in range(5)],
        0,
    )
    for v in range(5):
        levels[0, 1, v] = rim_middle[v] + lower[v] + pltpu.roll(upper_share[v], 1, 1)
    for k in range(1, 4):
        z_face(0, 0, adj, k, 5, 7)
    adj_z.wait()
    state_first.wait()

    for k in (0, 4):
        z_face(0, 0, adj, k, 5, 7)
    mid_z = remote(15, mid.at[0, :, z_side + 1, 8:40], mid.at[0, :, outer, 8:40], z_other)

    def first_plane(j, carry):
        @pl.when(j == 1)
        def _():
            mid_z.start()

        z = jnp.where(gz > 0, j, 3 - j)
        for r in range(5):
            x_face(0, 0, adj, z, r, 6)
        for r in range(5):
            at, rows = slice(7 + 8 * r, 15 + 8 * r), slice(8 * r, 8 * r + 8)
            here = [state[0, v, z + 1, at] for v in range(5)]
            held = [adj[0, v, z + 1, at] for v in range(5)]
            below, above = face(
                [here[v] + ahead(here[v], state[1, v, z + 1, at]) for v in range(5)],
                [ahead(held[v], adj[1, v, z + 1, at]) - held[v] for v in range(5)],
                1,
            )
            for v in range(5):
                mid[0, v, z + 1, at] = (
                    held[v]
                    + below[v]
                    + jnp.where(lane == 0, beside[v, z, at], pltpu.roll(above[v], 1, 1))
                    + gx_terms[0, 0, v, 8 * r + 1 : 8 * r + 9]
                    + gx_terms[1, 0, v, rows]
                    + gz_terms[0, 0, v, z + 1, rows]
                    + gz_terms[1, 0, v, z, rows]
                )
        return carry

    lax.fori_loop(0, 4, first_plane, 0)
    levels_copy.wait()
    state_second.wait()
    up_part = jnp.where(gz > 0, 0.0, 1.0).astype(f32)
    down_part = 1.0 - up_part

    def next_plane(kind, v):
        tile = levels[kind, 0, v]
        from_other = levels_z[kind, v]
        return (
            jnp.where(sublane8 >= 6, up_part * pltpu.roll(from_other, 6, 0), pltpu.roll(tile, 6, 0)),
            jnp.where(sublane8 < 2, down_part * pltpu.roll(from_other, 2, 0), pltpu.roll(tile, 2, 0)),
        )

    rim_adj, rim_state = level(0, 0), level(1, 0)
    next_adj = [next_plane(0, v) for v in range(5)]
    next_state = [next_plane(1, v) for v in range(5)]
    lower, _ = face(
        [rim_state[v] + next_state[v][0] for v in range(5)],
        [next_adj[v][0] - rim_adj[v] for v in range(5)],
        2,
    )
    _, upper_share = face(
        [rim_state[v] + next_state[v][1] for v in range(5)],
        [rim_adj[v] - next_adj[v][1] for v in range(5)],
        2,
        jnp.where(sublane8 < 2, keep_bottom, 1.0),
    )
    for v in range(5):
        packed[8 * v : 8 * v + 8] = levels[0, 1, v] + lower[v] + upper_share[v]
    back = packed[...].T
    for i in range(20):
        v, z = i // 4, i % 4
        mid_rim[v, z, :] = pltpu.roll(back[8:40], (127 - 8 * v - 2 * z) % 128, 1)
    for k in range(4):
        z_face(0, 5, mid, gz + k, 4, 8)

    def second_plane(j, carry):
        z = jnp.where(gz > 0, 3 - j, j)

        @pl.when(j == 3)
        def _():
            mid_z.wait()
            z_face(0, 5, mid, 4 - 4 * gz, 4, 8)

        for r in range(5):
            x_face(0, 5, mid, z, r, 7)
        for r in range(4):
            at, rows = slice(8 + 8 * r, 16 + 8 * r), slice(8 * r, 8 * r + 8)
            here = [state[0, 5 + v, z + 1, at] for v in range(5)]
            edge = [state[1, 5 + v, z + 1, at] for v in range(5)]
            held = [mid[0, v, z + 1, at] for v in range(5)]
            held_edge = [mid_rim[v, z, rows] for v in range(5)]
            adj_up = [ahead(held[v], held_edge[v]) for v in range(5)]
            adj_down = [behind(held[v], held_edge[v]) for v in range(5)]
            below, _ = face(
                [here[v] + ahead(here[v], edge[v]) for v in range(5)],
                [adj_up[v] - held[v] for v in range(5)],
                1,
            )
            _, above = face(
                [here[v] + behind(here[v], edge[v]) for v in range(5)],
                [held[v] - adj_down[v] for v in range(5)],
                1,
            )
            for v in range(5):
                result[v, z, rows] = 0.5 * (
                    adj[0, v, z + 1, at]
                    + held[v]
                    + below[v]
                    + above[v]
                    + gx_terms[0, 0, v, 8 * r + 1 : 8 * r + 9]
                    + gx_terms[1, 0, v, rows]
                    + gz_terms[0, 0, v, z + 1, rows]
                    + gz_terms[1, 0, v, z, rows]
                )
        return carry

    lax.fori_loop(0, 4, second_plane, 0)


def shards(coarse, detail_x1, detail_y1, detail_x2, detail_y2, significance, adjoint):
    operands = [
        pltpu.with_memory_space_constraint(value, pltpu.HBM)
        for value in (
            coarse.reshape(320, 32),
            detail_x1.reshape(320, 32),
            detail_y1.reshape(640, 32),
            detail_x2.reshape(640, 64),
            detail_y2.reshape(1280, 64),
            significance,
            adjoint,
            jnp.asarray(y_matrices()),
            jnp.asarray(small_matrices()),
        )
    ]
    anywhere = pl.BlockSpec(memory_space=pl.ANY)
    return pl.pallas_call(
        kernel,
        out_shape=jax.ShapeDtypeStruct(adjoint.shape, f32),
        in_specs=[anywhere] * 9,
        out_specs=pl.BlockSpec(memory_space=pltpu.VMEM),
        scratch_shapes=[
            pltpu.VMEM((640, 32), bf16),
            pltpu.VMEM((640, 32), bf16),
            pltpu.VMEM((640, 64), bf16),
            pltpu.VMEM((1280, 64), bf16),
            pltpu.VMEM((2, 4, 4, 4), jnp.int32),
            pltpu.VMEM((5, 4, 32, 128), f32),
            pltpu.VMEM((352, 256), bf16),
            pltpu.VMEM((192, 128), bf16),
            pltpu.SemaphoreType.DMA((9,)),
            pltpu.VMEM((2, 4, 8, 64), f32),
            pltpu.VMEM((2, 4, 16, 64), f32),
            pltpu.VMEM((2, 4, 32, 64), f32),
            pltpu.VMEM((3200, 128), f32),
            pltpu.VMEM((96, 128), f32),
            pltpu.VMEM((16, 640), bf16),
            pltpu.VMEM((16, 640), bf16),
            pltpu.VMEM((8, 640), bf16),
            pltpu.VMEM((8, 640), bf16),
            pltpu.VMEM((160, 128), bf16),
            pltpu.VMEM((160, 128), bf16),
            pltpu.VMEM((208, 128), bf16),
            pltpu.VMEM((208, 128), bf16),
            pltpu.VMEM((8, 384), bf16),
            pltpu.VMEM((2, 8, 384), bf16),
            pltpu.VMEM((8, 512), bf16),
            pltpu.VMEM((2, 8, 512), bf16),
            pltpu.VMEM((2, 48, 128), f32),
            pltpu.VMEM((2, 48, 128), bf16),
            pltpu.VMEM((2, 48, 128), bf16),
            pltpu.VMEM((32, 128), bf16),
            pltpu.VMEM((2, 32, 128), bf16),
            pltpu.VMEM((48, 128), f32),
            pltpu.VMEM((40, 48, 256), f32),
            pltpu.VMEM((40, 32, 256), f32),
            pltpu.VMEM((40, 16, 256), f32),
            pltpu.VMEM((40, 80, 256), bf16),
            pltpu.VMEM((40, 32, 128), f32),
            pltpu.VMEM((40, 8, 256), f32),
            pltpu.VMEM((2, 10, 6, 48, 128), f32),
            pltpu.VMEM((2, 5, 6, 48, 128), f32),
            pltpu.VMEM((2, 5, 6, 48, 128), f32),
            pltpu.VMEM((2, 1, 5, 48, 128), f32),
            pltpu.VMEM((2, 1, 5, 5, 40, 128), f32),
            pltpu.VMEM((48, 128), f32),
            pltpu.VMEM((5, 128, 128), f32),
            pltpu.VMEM((128, 128), f32),
            pltpu.VMEM((128, 128), f32),
            pltpu.VMEM((2, 3, 5, 8, 128), f32),
            pltpu.VMEM((2, 5, 8, 128), f32),
            pltpu.VMEM((128, 128), f32),
            pltpu.VMEM((5, 4, 48, 128), f32),
            pltpu.VMEM((5, 4, 32, 128), f32),
            pltpu.SemaphoreType.DMA((17,)),
            pltpu.SemaphoreType.DMA((17,)),
        ],
        compiler_params=pltpu.CompilerParams(collective_id=0, has_side_effects=True, vmem_limit_bytes=40*2**20),
    )(
        *operands,
    )


def solution(mesh):
    return jax.shard_map(
        shards,
        mesh=mesh,
        in_specs=(
            P(None, None, "gz", "gx", "gy"),
            P(None, None, "gz", "gx", "gy"),
            P(None, None, "gz", "gx", "gy"),
            P(None, None, "gz", "gx", "gy"),
            P(None, None, "gz", "gx", "gy"),
            P(None, "gz", "gx", "gy"),
            P(None, "gz", "gx", "gy"),
        ),
        out_specs=P(None, "gz", "gx", "gy"),
        check_vma=False,
    )
```
